256 devices in a mesh: row: 8 (over y, core), col: 32 (over x, z).
Axes of the slice: x: 4, y: 4, z: 8, core: 2. Of those that a mesh axis runs over, the one named last changes fastest.
Arguments:
- sources: float32 [65536, 256], P(('row', 'col')), may hold values from -6 to 6
- targets: float32 [65536, 256], P(('col', 'row')), may hold values from -6 to 6
- g_pot: float32 [65536], P(('col', 'row')), may hold values from -1 to 12
- log_a: float32 [65536], P(('row', 'col')), may hold values from -14 to -8
- log_b: float32 [65536], P(('col', 'row')), may hold values from -14 to -8
- src_block: int32 [16384], P(('row', 'col')), may hold values from 0 to 31, as said below
- tgt_block: int32 [16384], P(('row', 'col')), may hold values from 0 to 7, as said below
- pair_count: int32 [256], P(('row', 'col')), may hold values from 16 to 64, as said below
Outputs:
- f_new: float32 [65536], P(('row', 'col'))
- g_new: float32 [65536], P(('col', 'row'))
The draws below stay inside these ranges and needn't reach their ends.
Inputs may be any that keep to these rules, and one draw needn't show every extreme that they name: `src_block`: within each row index, slot 0 of the 32 devices names together every source block of that row index once; slot k and slot k + 32 of a device name the same source block. `tgt_block`: within each col index, slot 0 of the 8 devices names together every target block of that col index once. `pair_count`: some device has all 64 slots live.
All inputs are finite; a program needn't handle non-finite values.
Results may differ from the reference program's by a relative error of at most 0.0003.
Values sent between devices are 32-bit elements; how exact they have to be, the bound alone decides.
A program may use at most 128 MiB of HBM per device.

```python
import jax
import jax.numpy as jnp
from jax import lax

D = 256
BLK = 256
SRC_BLK_DEV = 1
TGT_BLK_DEV = 1
P_DEV = 64
NS = 65536
NT = 65536
N_ROW = 8
N_COL = 32
DEVICES = 256


def draw_g_pot(key, part):
    return jnp.clip(0.3 * jax.random.normal(key, (NT,), jnp.float32), -1.0, 1.0)


def draw_src_block(key, part):
    subkeys = jax.random.split(key, N_ROW)
    orders = jax.vmap(lambda single: jax.random.permutation(single, SRC_BLK_DEV * N_COL))(subkeys)
    row_ids = jnp.arange(N_ROW)[:, None, None]
    col_ids = jnp.arange(N_COL)[None, :, None]
    slot_ids = jnp.arange(P_DEV)[None, None, :]
    within = (col_ids * SRC_BLK_DEV + slot_ids) % (SRC_BLK_DEV * N_COL)
    picked = orders[row_ids, within]
    return picked.reshape(-1).astype(jnp.int32)


def draw_tgt_block(key, part):
    subkeys = jax.random.split(key, N_COL)
    orders = jax.vmap(lambda single: jax.random.permutation(single, TGT_BLK_DEV * N_ROW))(subkeys)
    row_ids = jnp.arange(N_ROW)[:, None, None]
    col_ids = jnp.arange(N_COL)[None, :, None]
    slot_ids = jnp.arange(P_DEV)[None, None, :]
    within = (row_ids * TGT_BLK_DEV + slot_ids) % (TGT_BLK_DEV * N_ROW)
    fixed_ids = orders[col_ids, within]
    drawn = jax.random.randint(jax.random.fold_in(key, 7), (N_ROW, N_COL, P_DEV), 0, TGT_BLK_DEV * N_ROW)
    picked = jnp.where(slot_ids < TGT_BLK_DEV, fixed_ids, drawn)
    return picked.reshape(-1).astype(jnp.int32)


def draw_pair_count(key, part):
    base = jax.random.randint(key, (DEVICES,), P_DEV // 4, P_DEV + 1)
    full_device = jax.random.randint(jax.random.fold_in(key, 3), (), 0, DEVICES)
    return jnp.where(jnp.arange(DEVICES) == full_device, P_DEV, base).astype(jnp.int32)


def shard_levels(own_key, shape, cuts, smallest, top_value):
    def one(axis_at, blocks):
        heights = jax.random.uniform(jax.random.fold_in(jax.random.fold_in(own_key, 6), axis_at), (blocks,), jnp.float32, smallest / len(cuts), top_value / len(cuts))
        return jnp.repeat(jnp.exp(heights), shape[axis_at] // blocks).reshape((-1,) + (1,) * (len(shape) - axis_at - 1))

    loudness = one(*cuts[0])
    for cut in cuts[1:]:
        loudness = loudness * one(*cut)
    return loudness


def scatter_about(stream_key, shape, deviation, most, cuts=(), kind=jnp.bfloat16):
    loudness = shard_levels(stream_key, shape, cuts, -0.22, 0.18) if cuts else 1.0
    values = jax.random.normal(stream_key, shape, jnp.float32) * deviation * loudness
    return jnp.minimum(jnp.maximum(values, -most), most).astype(kind)


def setup_inputs(seed: int = 0) -> dict:
    arg_keys = jax.random.split(jax.random.key(seed), 9)
    return {
        "sources": scatter_about(arg_keys[0], (NS, D), 1.0, 6.0, ((0, 256),), jnp.float32),
        "targets": scatter_about(arg_keys[1], (NT, D), 1.0, 6.0, ((0, 256),), jnp.float32),
        "g_pot": draw_g_pot(jax.random.fold_in(arg_keys[8], 71), 0),
        "log_a": jnp.clip(-14.0 + 6.0 * jax.random.uniform(arg_keys[3], (NS,), jnp.float32) ** shard_levels(arg_keys[3], (NS,), ((0, 256),), -0.2, 0.2), -14.0, -8.0),
        "log_b": jnp.clip(-14.0 + 6.0 * jax.random.uniform(arg_keys[4], (NT,), jnp.float32) ** shard_levels(arg_keys[4], (NT,), ((0, 256),), -0.2, 0.2), -14.0, -8.0),
        "src_block": draw_src_block(jax.random.fold_in(arg_keys[8], 71), 0),
        "tgt_block": draw_tgt_block(jax.random.fold_in(arg_keys[8], 71), 0),
        "pair_count": draw_pair_count(jax.random.fold_in(arg_keys[8], 71), 0),
    }


entropy = 0.05
lowest = -1.0e30


def cost_block(src_rows, tgt_rows):
    src_sq = jnp.sum(src_rows * src_rows, axis=1)
    tgt_sq = jnp.sum(tgt_rows * tgt_rows, axis=1)
    inner = jnp.dot(src_rows, tgt_rows.T, precision=lax.Precision.HIGHEST)
    return (src_sq[:, None] + tgt_sq[None, :] - 2.0 * inner) / src_rows.shape[1]


def absorb(top, total, scores, axis):
    block_top = jnp.max(scores, axis=axis)
    new_top = jnp.maximum(top, block_top)
    spread = jnp.expand_dims(new_top, axis)
    new_total = total * jnp.exp(top - new_top) + jnp.sum(jnp.exp(scores - spread), axis=axis)
    return new_top, new_total


def reference(sources, targets, g_pot, log_a, log_b, src_block, tgt_block, pair_count):
    device_ids = jnp.arange(N_ROW * N_COL, dtype=jnp.int32)
    row_of = device_ids // N_COL
    col_of = device_ids % N_COL
    src_glob = (row_of[:, None] * (SRC_BLK_DEV * N_COL) + src_block.reshape(-1, P_DEV)).reshape(-1)
    tgt_glob = (col_of[:, None] * (TGT_BLK_DEV * N_ROW) + tgt_block.reshape(-1, P_DEV)).reshape(-1)
    alive_all = (jnp.arange(P_DEV, dtype=jnp.int32)[None, :] < pair_count[:, None]).reshape(-1)

    def source_step(carry, item):
        top, total = carry
        sblk, tblk, alive = item
        src_start = (sblk * BLK).astype(jnp.int32)
        tgt_start = (tblk * BLK).astype(jnp.int32)
        src_rows = lax.dynamic_slice_in_dim(sources, src_start, BLK, 0)
        tgt_rows = lax.dynamic_slice_in_dim(targets, tgt_start, BLK, 0)
        pot_rows = lax.dynamic_slice_in_dim(g_pot, tgt_start, BLK, 0)
        scores = (pot_rows[None, :] - cost_block(src_rows, tgt_rows)) / entropy
        old_top = lax.dynamic_slice_in_dim(top, src_start, BLK, 0)
        old_total = lax.dynamic_slice_in_dim(total, src_start, BLK, 0)
        new_top, new_total = absorb(old_top, old_total, scores, 1)
        new_top = jnp.where(alive, new_top, old_top)
        new_total = jnp.where(alive, new_total, old_total)
        top = lax.dynamic_update_slice_in_dim(top, new_top, src_start, 0)
        total = lax.dynamic_update_slice_in_dim(total, new_total, src_start, 0)
        return (top, total), None

    start_src = (jnp.full((NS,), lowest, jnp.float32), jnp.zeros((NS,), jnp.float32))
    (src_top, src_total), _ = lax.scan(source_step, start_src, (src_glob, tgt_glob, alive_all))
    f_new = entropy * log_a - entropy * (src_top + jnp.log(src_total))

    def target_step(carry, item):
        top, total = carry
        sblk, tblk, alive = item
        src_start = (sblk * BLK).astype(jnp.int32)
        tgt_start = (tblk * BLK).astype(jnp.int32)
        src_rows = lax.dynamic_slice_in_dim(sources, src_start, BLK, 0)
        tgt_rows = lax.dynamic_slice_in_dim(targets, tgt_start, BLK, 0)
        pot_rows = lax.dynamic_slice_in_dim(f_new, src_start, BLK, 0)
        scores = (pot_rows[:, None] - cost_block(src_rows, tgt_rows)) / entropy
        old_top = lax.dynamic_slice_in_dim(top, tgt_start, BLK, 0)
        old_total = lax.dynamic_slice_in_dim(total, tgt_start, BLK, 0)
        new_top, new_total = absorb(old_top, old_total, scores, 0)
        new_top = jnp.where(alive, new_top, old_top)
        new_total = jnp.where(alive, new_total, old_total)
        top = lax.dynamic_update_slice_in_dim(top, new_top, tgt_start, 0)
        total = lax.dynamic_update_slice_in_dim(total, new_total, tgt_start, 0)
        return (top, total), None

    start_tgt = (jnp.full((NT,), lowest, jnp.float32), jnp.zeros((NT,), jnp.float32))
    (tgt_top, tgt_total), _ = lax.scan(target_step, start_tgt, (src_glob, tgt_glob, alive_all))
    g_new = entropy * log_b - entropy * (tgt_top + jnp.log(tgt_total))
    return f_new, g_new
```

```python
import functools
import math

import jax
import jax.numpy as jnp
from jax import lax
from jax.experimental import pallas as pl
from jax.experimental.pallas import tpu as pltpu
from jax.sharding import PartitionSpec as P

MESH = pl.DeviceIdType.MESH
BLK = 256
D = 256
ROWS = 264
NX, NY, NZ = 4, 4, 8
N_ROW, N_COL = 8, 32
ENTROPY = 0.05
LOG2E = 1.0 / math.log(2.0)
LN2 = math.log(2.0)
KAPPA = LOG2E / ENTROPY
LOWEST = -1.0e30
CHUNKS = ((0, 128), (128, 136))
VMEM_LIMIT = 60 * 1024 * 1024


def place():
    r, c = lax.axis_index("row"), lax.axis_index("col")
    return r // 2, lax.rem(r, 2), c // NZ, lax.rem(c, NZ)


def device(y, core, x, z):
    return {"row": y * 2 + core, "col": x * NZ + z}


def signal(sem, where):
    pl.semaphore_signal(sem, inc=1, device_id=where, device_id_type=MESH)


FIRST = ((1, 0), (3, 0), (0, 1), (0, 3))
SECOND = ((2, 0), (1, 1), (1, 3), (3, 1), (3, 3), (0, 2))
THIRD = ((2, 1), (2, 3), (1, 2), (3, 2))
FOURTH = ((2, 2),)


def sends_of(da, db):
    out = []
    if db == 0:
        if da == 0:
            out += [("A+", (1, 0)), ("A-", (3, 0))]
        if da == 1:
            out += [("A+", (2, 0))]
        out += [("B+", (da, 1)), ("B-", (da, 3))]
    elif db == 1 and da in (0, 1):
        out += [("B+", (da, 2))]
    elif db == 3 and da in (2, 3):
        out += [("B-", (da, 2))]
    return out


def gather_kernel(src_ref, tgt_ref, pot_ref, mass_ref, list_ref, x_out, y_out, lists_out,
                  load_sem, send_sem, recv_sem, mate_send, mate_recv, z_send, z_recv, l_send, l_recv):
    y, k, x, z = place()
    row = y * 2 + k

    def wrap4(v):
        return lax.rem(v + 8, 4)

    sigma = 1 - 2 * k

    def step_a(n):
        return wrap4(y + n * sigma * k), wrap4(x + n * sigma * (1 - k))

    def step_b(n):
        return wrap4(y + n * (1 - k)), wrap4(x + n * k)

    def dev_of(name):
        n = 1 if name[1] == "+" else -1
        ny, nx = step_a(n) if name[0] == "A" else step_b(n)
        return device(ny, k, nx, z)

    mate = device(y, 1 - k, x, z)
    z_long = device(y, k, x, lax.rem(z + sigma + NZ, NZ))
    z_short = device(y, k, x, lax.rem(z - sigma + NZ, NZ))

    def slot(da, db, core=None):
        if core is None:
            core = k
        oy = wrap4(y - db * (1 - core) + da * core)
        ox = wrap4(x - da * (1 - core) - db * core)
        return ox, oy * 2 + core

    loads = [
        pltpu.make_async_copy(tgt_ref, y_out.at[x, row, pl.ds(0, BLK)], load_sem.at[0]),
        pltpu.make_async_copy(pot_ref, y_out.at[x, row, pl.ds(BLK, 1)], load_sem.at[1]),
        pltpu.make_async_copy(src_ref, x_out.at[z, pl.ds(0, BLK)], load_sem.at[2]),
        pltpu.make_async_copy(mass_ref, x_out.at[z, pl.ds(BLK, 1)], load_sem.at[3]),
        pltpu.make_async_copy(list_ref, lists_out.at[x], load_sem.at[4]),
    ]
    for copy in loads:
        copy.start()
    barrier = pltpu.get_barrier_semaphore()
    peers = [device(y, k, wrap4(x + 1), z), device(y, k, wrap4(x + 3), z), device(y, k, wrap4(x + 2), z),
             device(wrap4(y + 1), k, x, z), device(wrap4(y + 3), k, x, z), mate, z_long, z_short]
    for peer in peers:
        signal(barrier, peer)
    pl.semaphore_wait(barrier, len(peers))
    for copy in loads:
        copy.wait()

    pending = []

    def at(pos):
        return pos[0] * 4 + pos[1]

    def part(ref, ch):
        return ref.at[pl.ds(*CHUNKS[ch])]

    def y_copy(pos, ch, where, target, n):
        ox, orow = slot(*pos)
        return pltpu.make_async_remote_copy(
            src_ref=part(y_out.at[ox, orow], ch), dst_ref=part(y_out.at[ox, orow], ch),
            send_sem=send_sem.at[at(pos), ch, n], recv_sem=recv_sem.at[at(target), ch],
            device_id=where, device_id_type=MESH)

    def mate_copy(pos, ch):
        ox, orow = slot(*pos)
        return pltpu.make_async_remote_copy(
            src_ref=part(y_out.at[ox, orow], ch), dst_ref=part(y_out.at[ox, orow], ch),
            send_sem=mate_send.at[at(pos), ch], recv_sem=mate_recv.at[at(pos), ch],
            device_id=mate, device_id_type=MESH)

    def send_y(pos, ch):
        for n, (name, target) in enumerate(sends_of(*pos)):
            copy = y_copy(pos, ch, dev_of(name), target, n)
            copy.start()
            pending.append(copy)
        copy = mate_copy(pos, ch)
        copy.start()
        pending.append(copy)

    def recv_y(pos, ch):
        ox, orow = slot(*pos)
        ref = part(y_out.at[ox, orow], ch)
        pltpu.make_async_remote_copy(src_ref=ref, dst_ref=ref, send_sem=send_sem.at[0, 0, 0],
                                     recv_sem=recv_sem.at[at(pos), ch], device_id=mate,
                                     device_id_type=MESH).wait_recv()

    def recv_mate(pos, ch):
        ox, orow = slot(*pos, core=1 - k)
        ref = part(y_out.at[ox, orow], ch)
        pltpu.make_async_remote_copy(src_ref=ref, dst_ref=ref, send_sem=send_sem.at[0, 0, 0],
                                     recv_sem=mate_recv.at[at(pos), ch], device_id=mate,
                                     device_id_type=MESH).wait_recv()

    def z_slot(n):
        return lax.rem(z - n * sigma + NZ * 4, NZ)

    def send_z(n, ch, long):
        target = n + 1 if long else n - 1
        ref = part(x_out.at[z_slot(n)], ch)
        copy = pltpu.make_async_remote_copy(
            src_ref=ref, dst_ref=ref, send_sem=z_send.at[n + 4, ch, 0 if long else 1],
            recv_sem=z_recv.at[target + 4, ch],
            device_id=z_long if long else z_short, device_id_type=MESH)
        copy.start()
        pending.append(copy)

    def recv_z(n, ch):
        ref = part(x_out.at[z_slot(n)], ch)
        pltpu.make_async_remote_copy(src_ref=ref, dst_ref=ref, send_sem=send_sem.at[0, 0, 0],
                                     recv_sem=z_recv.at[n + 4, ch], device_id=mate,
                                     device_id_type=MESH).wait_recv()

    for n in (1, 2, 3):
        copy = pltpu.make_async_remote_copy(
            src_ref=lists_out.at[x], dst_ref=lists_out.at[x], send_sem=l_send.at[n - 1], recv_sem=l_recv.at[n - 1],
            device_id=device(y, k, wrap4(x + n), z), device_id_type=MESH)
        copy.start()
        pending.append(copy)
    for ch in (0, 1):
        send_y((0, 0), ch)
        send_z(0, ch, True)
        send_z(0, ch, False)
    levels = (FIRST, SECOND, THIRD, FOURTH)
    for level in range(4):
        for ch in (0, 1):
            for pos in levels[level]:
                recv_y(pos, ch)
                send_y(pos, ch)
            n = level + 1
            recv_z(n, ch)
            if n < 4:
                send_z(n, ch, True)
                recv_z(-n, ch)
                if n < 3:
                    send_z(-n, ch, False)
    for n in (1, 2, 3):
        ref = lists_out.at[wrap4(x - n)]
        pltpu.make_async_remote_copy(src_ref=ref, dst_ref=ref, send_sem=l_send.at[0], recv_sem=l_recv.at[n - 1],
                                     device_id=mate, device_id_type=MESH).wait_recv()
    for ch in (0, 1):
        for da in range(4):
            for db in range(4):
                recv_mate((da, db), ch)
    for copy in pending:
        copy.wait_send()


def split3(v):
    hi = v.astype(jnp.bfloat16)
    lo = (v - hi.astype(jnp.float32)).astype(jnp.bfloat16)
    return hi, lo


def prep_kernel_body(x_raw, y_raw, x3, y3, bias):
    def one_x(i, carry):
        hi, lo = split3(x_raw[i, pl.ds(0, BLK), :])
        x3[i, :, pl.ds(0, D)] = hi
        x3[i, :, pl.ds(D, D)] = lo
        x3[i, :, pl.ds(2 * D, D)] = hi
        return carry

    lax.fori_loop(0, NZ, one_x, 0)

    def one_y(i, carry):
        block = y_raw[i, pl.ds(0, BLK), :].T
        pot = y_raw[i, pl.ds(BLK, 1), :]
        square = jnp.sum(block * block, axis=0, keepdims=True)
        row = KAPPA * (pot - square * (1.0 / D))
        bias[i] = jnp.broadcast_to(row, (8, BLK))
        hi, lo = split3(block * (2.0 * KAPPA / D))
        y3[i, pl.ds(0, D), :] = hi
        y3[i, pl.ds(D, D), :] = hi
        y3[i, pl.ds(2 * D, D), :] = lo
        return carry

    lax.fori_loop(0, NX * N_ROW, one_y, 0)


def pairs_of(lists, quarter, body):
    for other in range(NX):
        def one(i, carry, other=other):
            src = lists[other, 0, i]

            @pl.when(src // NZ == quarter)
            def _():
                body(lax.rem(src, NZ), other * N_ROW + lists[other, 0, 64 + i])
            return carry

        lax.fori_loop(0, lists[other, 1, 0], one, 0)


def first_kernel(lists, quarter, x_raw, y_raw, x3, y3, part_out, bias, top, total):
    prep_kernel_body(x_raw, y_raw, x3, y3, bias)
    top[...] = jnp.full(top.shape, LOWEST, jnp.float32)
    total[...] = jnp.zeros(total.shape, jnp.float32)

    def pair(b, t):
        g = jnp.dot(x3[b], y3[t], preferred_element_type=jnp.float32)
        row = bias[t]
        s1 = g[:, :128] + row[0:1, :128]
        s2 = g[:, 128:] + row[0:1, 128:]
        old = top[b]
        new = jnp.maximum(old, jnp.maximum(s1, s2))
        total[b] = total[b] * jnp.exp2(old - new) + jnp.exp2(s1 - new) + jnp.exp2(s2 - new)
        top[b] = new

    pairs_of(lists, quarter[0], pair)

    def close(b, carry):
        high = jnp.max(top[b], axis=1, keepdims=True)
        whole = jnp.sum(total[b] * jnp.exp2(top[b] - high), axis=1, keepdims=True)
        logs = jnp.where(whole > 0.0, high + jnp.log2(whole), LOWEST)
        part_out[b] = jnp.broadcast_to(logs, (BLK, 128)).T[0:8, :]
        return carry

    lax.fori_loop(0, NZ, close, 0)


def row_exchange_kernel(part_ref, x_raw, f_out, c_out, got, send_sem, recv_sem):
    y, k, x, z = place()
    barrier = pltpu.get_barrier_semaphore()
    for n in range(1, NZ):
        signal(barrier, device(y, k, x, lax.rem(z + n, NZ)))
    pl.semaphore_wait(barrier, NZ - 1)
    copies = []
    for n in range(1, NZ):
        copy = pltpu.make_async_remote_copy(
            src_ref=part_ref, dst_ref=got.at[n - 1], send_sem=send_sem.at[n - 1], recv_sem=recv_sem.at[n - 1],
            device_id=device(y, k, x, lax.rem(z + n, NZ)), device_id_type=MESH)
        copy.start()
        copies.append(copy)
    for copy in copies:
        copy.wait()
    own = part_ref[...]
    others = [got[n] for n in range(NZ - 1)]
    top = own
    for v in others:
        top = jnp.maximum(top, v)
    total = jnp.exp2(own - top)
    for v in others:
        total = total + jnp.exp2(v - top)
    logs = top + jnp.log2(total)
    c_out[...] = LOG2E * x_raw[:, pl.ds(BLK, 1), :] - logs
    square = x_raw[z, pl.ds(0, BLK), :].T
    square = jnp.sum(square * square, axis=0, keepdims=True)
    mass = x_raw[z, pl.ds(BLK, 1), :]
    c_here = c_out[z]
    f_out[...] = ENTROPY * mass - (ENTROPY * LN2) * (LOG2E * mass - c_here[0:1, :]) + square * (1.0 / D)


def second_kernel(lists, quarter, x3, y3, c_ref, part_out, cols, top, total):
    top[...] = jnp.full(top.shape, LOWEST, jnp.float32)
    total[...] = jnp.zeros(total.shape, jnp.float32)

    def widen(b, carry):
        cols[b] = jnp.broadcast_to(c_ref[b, pl.ds(0, 1), :], (128, BLK)).T
        return carry

    lax.fori_loop(0, NZ, widen, 0)

    def pair(b, t):
        g = jnp.dot(x3[b], y3[t], preferred_element_type=jnp.float32)
        col = cols[b]
        u = g + jnp.concatenate([col, col], axis=1)
        u = u.reshape(BLK // 8, 8, BLK)
        old = top[t]
        new = jnp.maximum(old, jnp.max(u, axis=0))
        total[t] = total[t] * jnp.exp2(old - new) + jnp.sum(jnp.exp2(u - new[None]), axis=0)
        top[t] = new

    pairs_of(lists, quarter[0], pair)

    def close(t, carry):
        high = jnp.max(top[t], axis=0, keepdims=True)
        whole = jnp.sum(total[t] * jnp.exp2(top[t] - high), axis=0, keepdims=True)
        part_out[t] = jnp.where(whole > 0.0, high + jnp.log2(whole), LOWEST)
        return carry

    lax.fori_loop(0, NX * N_ROW, close, 0)


def col_exchange_kernel(part_ref, tgt_ref, mass_ref, g_out, got, send_sem, recv_sem):
    y, k, x, z = place()
    me = x * N_ROW + y * 2 + k
    many = NX * N_ROW
    barrier = pltpu.get_barrier_semaphore()

    def peer(n):
        other = lax.rem(me + n, many)
        return other, {"row": lax.rem(other, N_ROW), "col": (other // N_ROW) * NZ + z}

    for n in range(1, many):
        signal(barrier, peer(n)[1])
    pl.semaphore_wait(barrier, many - 1)
    copies = []
    for n in range(1, many):
        other, where = peer(n)
        copy = pltpu.make_async_remote_copy(
            src_ref=part_ref.at[other], dst_ref=got.at[n], send_sem=send_sem.at[n], recv_sem=recv_sem.at[n],
            device_id=where, device_id_type=MESH)
        copy.start()
        copies.append(copy)
    block = tgt_ref[...].T
    square = jnp.sum(block * block, axis=0, keepdims=True)
    for copy in copies:
        copy.wait()
    got[0] = part_ref[me]
    every = got[...]
    top = jnp.max(every, axis=0)
    total = jnp.sum(jnp.exp2(every - top[None]), axis=0)
    logs = top + jnp.log2(total)
    g_out[...] = ENTROPY * mass_ref[...] - (ENTROPY * LN2) * logs + square * (1.0 / D)


def shape(*dims, kind=jnp.float32):
    return jax.ShapeDtypeStruct(dims, kind)


def local(sources, targets, g_pot, log_a, log_b, src_block, tgt_block, pair_count):
    whole = pl.BlockSpec(memory_space=pltpu.VMEM)
    anywhere = pl.BlockSpec(memory_space=pl.ANY)
    scalars = pl.BlockSpec(memory_space=pltpu.SMEM)
    dma = pltpu.SemaphoreType.DMA
    packed = jnp.zeros((8, 128), jnp.int32)
    packed = packed.at[0, :64].set(src_block).at[0, 64:].set(tgt_block).at[1, 0].set(pair_count[0])
    x_raw, y_raw, lists = pl.pallas_call(
        gather_kernel,
        out_shape=(shape(NZ, ROWS, D), shape(NX, N_ROW, ROWS, D), shape(NX, 8, 128, kind=jnp.int32)),
        in_specs=[anywhere] * 5,
        out_specs=(whole, whole, whole),
        scratch_shapes=[dma((5,)), dma((16, 2, 4)), dma((16, 2)), dma((16, 2)), dma((16, 2)),
                        dma((9, 2, 2)), dma((9, 2)), dma((3,)), dma((3,))],
        compiler_params=pltpu.CompilerParams(collective_id=0, has_side_effects=True, vmem_limit_bytes=VMEM_LIMIT),
    )(sources, targets, g_pot[None], log_a[None], packed)
    y_raw = y_raw.reshape(NX * N_ROW, ROWS, D)
    quarter = (lax.axis_index("col") // NZ).astype(jnp.int32).reshape(1)
    x3, y3, part = pl.pallas_call(
        first_kernel,
        out_shape=(shape(NZ, BLK, 3 * D, kind=jnp.bfloat16), shape(NX * N_ROW, 3 * D, BLK, kind=jnp.bfloat16),
                   shape(NZ, 8, BLK)),
        in_specs=[scalars, scalars, whole, whole],
        out_specs=(whole, whole, whole),
        scratch_shapes=[pltpu.VMEM((NX * N_ROW, 8, BLK), jnp.float32), pltpu.VMEM((NZ, BLK, 128), jnp.float32),
                        pltpu.VMEM((NZ, BLK, 128), jnp.float32)],
        compiler_params=pltpu.CompilerParams(vmem_limit_bytes=VMEM_LIMIT),
    )(lists, quarter, x_raw, y_raw)
    f_own, c_all = pl.pallas_call(
        row_exchange_kernel,
        out_shape=(shape(1, BLK), shape(NZ, 8, BLK)),
        in_specs=[whole, whole],
        out_specs=(whole, whole),
        scratch_shapes=[pltpu.VMEM((NZ - 1, NZ, 8, BLK), jnp.float32), dma((NZ - 1,)), dma((NZ - 1,))],
        compiler_params=pltpu.CompilerParams(collective_id=1, has_side_effects=True, vmem_limit_bytes=VMEM_LIMIT),
    )(part, x_raw)
    sums = pl.pallas_call(
        second_kernel,
        out_shape=shape(NX * N_ROW, 1, BLK),
        in_specs=[scalars, scalars, whole, whole, whole],
        out_specs=whole,
        scratch_shapes=[pltpu.VMEM((NZ, BLK, 128), jnp.float32), pltpu.VMEM((NX * N_ROW, 8, BLK), jnp.float32),
                        pltpu.VMEM((NX * N_ROW, 8, BLK), jnp.float32)],
        compiler_params=pltpu.CompilerParams(vmem_limit_bytes=VMEM_LIMIT),
    )(lists, quarter, x3, y3, c_all)
    g_own = pl.pallas_call(
        col_exchange_kernel,
        out_shape=shape(1, BLK),
        in_specs=[whole, whole, whole],
        out_specs=whole,
        scratch_shapes=[pltpu.VMEM((NX * N_ROW, 1, BLK), jnp.float32), dma((NX * N_ROW,)), dma((NX * N_ROW,))],
        compiler_params=pltpu.CompilerParams(collective_id=2, has_side_effects=True),
    )(sums, targets, log_b[None])
    return f_own.reshape(BLK), g_own.reshape(BLK)


def solution(mesh):
    placed = (
        P(("row", "col"), None),
        P(("col", "row"), None),
        P(("col", "row")),
        P(("row", "col")),
        P(("col", "row")),
        P(("row", "col")),
        P(("row", "col")),
        P(("row", "col")),
    )
    return jax.shard_map(
        local,
        mesh=mesh,
        in_specs=placed,
        out_specs=(P(("row", "col")), P(("col", "row"))),
        check_vma=False,
    )
```

```python
import functools
import math

import jax
import jax.numpy as jnp
from jax import lax
from jax.experimental import pallas as pl
from jax.experimental.pallas import tpu as pltpu
from jax.sharding import PartitionSpec as P

MESH = pl.DeviceIdType.MESH
BLK = 256
D = 256
ROWS = 264
NX, NY, NZ = 4, 4, 8
N_ROW, N_COL = 8, 32
ENTROPY = 0.05
LOG2E = 1.0 / math.log(2.0)
LN2 = math.log(2.0)
KAPPA = LOG2E / ENTROPY
LOWEST = -1.0e30
CHUNKS = ((0, 128), (128, 136))
VMEM_LIMIT = 60 * 1024 * 1024


def place():
    r, c = lax.axis_index("row"), lax.axis_index("col")
    return r // 2, lax.rem(r, 2), c // NZ, lax.rem(c, NZ)


def device(y, core, x, z):
    return {"row": y * 2 + core, "col": x * NZ + z}


def signal(sem, where):
    pl.semaphore_signal(sem, inc=1, device_id=where, device_id_type=MESH)


FIRST = ((1, 0), (3, 0), (0, 1), (0, 3))
SECOND = ((2, 0), (1, 1), (1, 3), (3, 1), (3, 3), (0, 2))
THIRD = ((2, 1), (2, 3), (1, 2), (3, 2))
FOURTH = ((2, 2),)


def sends_of(da, db):
    out = []
    if db == 0:
        if da == 0:
            out += [("A+", (1, 0)), ("A-", (3, 0))]
        if da == 1:
            out += [("A+", (2, 0))]
        out += [("B+", (da, 1)), ("B-", (da, 3))]
    elif db == 1 and da in (0, 1):
        out += [("B+", (da, 2))]
    elif db == 3 and da in (2, 3):
        out += [("B-", (da, 2))]
    return out


def gather_kernel(src_ref, tgt_ref, pot_ref, mass_ref, list_ref, x_out, y_out, lists_out,
                  load_sem, send_sem, recv_sem, mate_send, mate_recv, z_send, z_recv, l_send, l_recv):
    y, k, x, z = place()
    row = y * 2 + k

    def wrap4(v):
        return lax.rem(v + 8, 4)

    sigma = 1 - 2 * k

    def step_a(n):
        return wrap4(y + n * sigma * k), wrap4(x + n * sigma * (1 - k))

    def step_b(n):
        return wrap4(y + n * (1 - k)), wrap4(x + n * k)

    def dev_of(name):
        n = 1 if name[1] == "+" else -1
        ny, nx = step_a(n) if name[0] == "A" else step_b(n)
        return device(ny, k, nx, z)

    mate = device(y, 1 - k, x, z)
    z_long = device(y, k, x, lax.rem(z + sigma + NZ, NZ))
    z_short = device(y, k, x, lax.rem(z - sigma + NZ, NZ))

    def slot(da, db, core=None):
        if core is None:
            core = k
        oy = wrap4(y - db * (1 - core) + da * core)
        ox = wrap4(x - da * (1 - core) - db * core)
        return ox, oy * 2 + core

    loads = [
        pltpu.make_async_copy(tgt_ref, y_out.at[x, row, pl.ds(0, BLK)], load_sem.at[0]),
        pltpu.make_async_copy(pot_ref, y_out.at[x, row, pl.ds(BLK, 1)], load_sem.at[1]),
        pltpu.make_async_copy(src_ref, x_out.at[z, pl.ds(0, BLK)], load_sem.at[2]),
        pltpu.make_async_copy(mass_ref, x_out.at[z, pl.ds(BLK, 1)], load_sem.at[3]),
        pltpu.make_async_copy(list_ref, lists_out.at[x], load_sem.at[4]),
    ]
    for copy in loads:
        copy.start()
    barrier = pltpu.get_barrier_semaphore()
    peers = [device(y, k, wrap4(x + 1), z), device(y, k, wrap4(x + 3), z), device(y, k, wrap4(x + 2), z),
             device(wrap4(y + 1), k, x, z), device(wrap4(y + 3), k, x, z), mate, z_long, z_short]
    for peer in peers:
        signal(barrier, peer)
    pl.semaphore_wait(barrier, len(peers))
    for copy in loads:
        copy.wait()

    pending = []

    def at(pos):
        return pos[0] * 4 + pos[1]

    def part(ref, ch):
        return ref.at[pl.ds(*CHUNKS[ch])]

    def y_copy(pos, ch, where, target, n):
        ox, orow = slot(*pos)
        return pltpu.make_async_remote_copy(
            src_ref=part(y_out.at[ox, orow], ch), dst_ref=part(y_out.at[ox, orow], ch),
            send_sem=send_sem.at[at(pos), ch, n], recv_sem=recv_sem.at[at(target), ch],
            device_id=where, device_id_type=MESH)

    def mate_copy(pos, ch):
        ox, orow = slot(*pos)
        return pltpu.make_async_remote_copy(
            src_ref=part(y_out.at[ox, orow], ch), dst_ref=part(y_out.at[ox, orow], ch),
            send_sem=mate_send.at[at(pos), ch], recv_sem=mate_recv.at[at(pos), ch],
            device_id=mate, device_id_type=MESH)

    def send_y(pos, ch):
        for n, (name, target) in enumerate(sends_of(*pos)):
            copy = y_copy(pos, ch, dev_of(name), target, n)
            copy.start()
            pending.append(copy)
        copy = mate_copy(pos, ch)
        copy.start()
        pending.append(copy)

    def recv_y(pos, ch):
        ox, orow = slot(*pos)
        ref = part(y_out.at[ox, orow], ch)
        pltpu.make_async_remote_copy(src_ref=ref, dst_ref=ref, send_sem=send_sem.at[0, 0, 0],
                                     recv_sem=recv_sem.at[at(pos), ch], device_id=mate,
                                     device_id_type=MESH).wait_recv()

    def recv_mate(pos, ch):
        ox, orow = slot(*pos, core=1 - k)
        ref = part(y_out.at[ox, orow], ch)
        pltpu.make_async_remote_copy(src_ref=ref, dst_ref=ref, send_sem=send_sem.at[0, 0, 0],
                                     recv_sem=mate_recv.at[at(pos), ch], device_id=mate,
                                     device_id_type=MESH).wait_recv()

    def z_slot(n):
        return lax.rem(z - n * sigma + NZ * 4, NZ)

    def send_z(n, ch, long):
        target = n + 1 if long else n - 1
        ref = part(x_out.at[z_slot(n)], ch)
        copy = pltpu.make_async_remote_copy(
            src_ref=ref, dst_ref=ref, send_sem=z_send.at[n + 4, ch, 0 if long else 1],
            recv_sem=z_recv.at[target + 4, ch],
            device_id=z_long if long else z_short, device_id_type=MESH)
        copy.start()
        pending.append(copy)

    def recv_z(n, ch):
        ref = part(x_out.at[z_slot(n)], ch)
        pltpu.make_async_remote_copy(src_ref=ref, dst_ref=ref, send_sem=send_sem.at[0, 0, 0],
                                     recv_sem=z_recv.at[n + 4, ch], device_id=mate,
                                     device_id_type=MESH).wait_recv()

    for n in (1, 2, 3):
        copy = pltpu.make_async_remote_copy(
            src_ref=lists_out.at[x], dst_ref=lists_out.at[x], send_sem=l_send.at[n - 1], recv_sem=l_recv.at[n - 1],
            device_id=device(y, k, wrap4(x + n), z), device_id_type=MESH)
        copy.start()
        pending.append(copy)
    for ch in (0, 1):
        send_y((0, 0), ch)
        send_z(0, ch, True)
        send_z(0, ch, False)
    levels = (FIRST, SECOND, THIRD, FOURTH)
    for level in range(4):
        for ch in (0, 1):
            for pos in levels[level]:
                recv_y(pos, ch)
                send_y(pos, ch)
            n = level + 1
            recv_z(n, ch)
            if n < 4:
                send_z(n, ch, True)
                recv_z(-n, ch)
                if n < 3:
                    send_z(-n, ch, False)
    for n in (1, 2, 3):
        ref = lists_out.at[wrap4(x - n)]
        pltpu.make_async_remote_copy(src_ref=ref, dst_ref=ref, send_sem=l_send.at[0], recv_sem=l_recv.at[n - 1],
                                     device_id=mate, device_id_type=MESH).wait_recv()
    for ch in (0, 1):
        for da in range(4):
            for db in range(4):
                recv_mate((da, db), ch)
    for copy in pending:
        copy.wait_send()


def split3(v):
    hi = v.astype(jnp.bfloat16)
    lo = (v - hi.astype(jnp.float32)).astype(jnp.bfloat16)
    return hi, lo


def prep_kernel_body(x_raw, y_raw, x3, y3, bias):
    def one_x(i, carry):
        hi, lo = split3(x_raw[i, pl.ds(0, BLK), :])
        x3[i, :, pl.ds(0, D)] = hi
        x3[i, :, pl.ds(D, D)] = lo
        x3[i, :, pl.ds(2 * D, D)] = hi
        return carry

    lax.fori_loop(0, NZ, one_x, 0)

    def one_y(i, carry):
        block = y_raw[i, pl.ds(0, BLK), :].T
        pot = y_raw[i, pl.ds(BLK, 1), :]
        square = jnp.sum(block * block, axis=0, keepdims=True)
        row = KAPPA * (pot - square * (1.0 / D))
        bias[i] = jnp.broadcast_to(row, (8, BLK))
        hi, lo = split3(block * (2.0 * KAPPA / D))
        y3[i, pl.ds(0, D), :] = hi
        y3[i, pl.ds(D, D), :] = hi
        y3[i, pl.ds(2 * D, D), :] = lo
        return carry

    lax.fori_loop(0, NX * N_ROW, one_y, 0)


def pairs_of(lists, quarter, body):
    for other in range(NX):
        def one(i, carry, other=other):
            src = lists[other, 0, i]

            @pl.when(src // NZ == quarter)
            def _():
                body(lax.rem(src, NZ), other * N_ROW + lists[other, 0, 64 + i])
            return carry

        lax.fori_loop(0, lists[other, 1, 0], one, 0)


def first_kernel(lists, quarter, x_raw, y_raw, x3, y3, part_out, bias, top, total):
    prep_kernel_body(x_raw, y_raw, x3, y3, bias)
    top[...] = jnp.full(top.shape, LOWEST, jnp.float32)
    total[...] = jnp.zeros(total.shape, jnp.float32)

    def pair(b, t):
        g = jnp.dot(x3[b], y3[t], preferred_element_type=jnp.float32)
        row = bias[t]
        s1 = g[:, :128] + row[0:1, :128]
        s2 = g[:, 128:] + row[0:1, 128:]
        old = top[b]
        new = jnp.maximum(old, jnp.maximum(s1, s2))
        total[b] = total[b] * jnp.exp2(old - new) + jnp.exp2(s1 - new) + jnp.exp2(s2 - new)
        top[b] = new

    pairs_of(lists, quarter[0], pair)

    def close(b, carry):
        high = jnp.max(top[b], axis=1, keepdims=True)
        whole = jnp.sum(total[b] * jnp.exp2(top[b] - high), axis=1, keepdims=True)
        logs = jnp.where(whole > 0.0, high + jnp.log2(whole), LOWEST)
        part_out[b] = jnp.broadcast_to(logs, (BLK, 128)).T[0:8, :]
        return carry

    lax.fori_loop(0, NZ, close, 0)


def row_exchange_kernel(part_ref, x_raw, f_out, c_out, got, send_sem, recv_sem):
    y, k, x, z = place()
    barrier = pltpu.get_barrier_semaphore()
    for n in range(1, NZ):
        signal(barrier, device(y, k, x, lax.rem(z + n, NZ)))
    pl.semaphore_wait(barrier, NZ - 1)
    copies = []
    for n in range(1, NZ):
        copy = pltpu.make_async_remote_copy(
            src_ref=part_ref, dst_ref=got.at[n - 1], send_sem=send_sem.at[n - 1], recv_sem=recv_sem.at[n - 1],
            device_id=device(y, k, x, lax.rem(z + n, NZ)), device_id_type=MESH)
        copy.start()
        copies.append(copy)
    for copy in copies:
        copy.wait()
    own = part_ref[...]
    others = [got[n] for n in range(NZ - 1)]
    top = own
    for v in others:
        top = jnp.maximum(top, v)
    total = jnp.exp2(own - top)
    for v in others:
        total = total + jnp.exp2(v - top)
    logs = top + jnp.log2(total)
    c_out[...] = LOG2E * x_raw[:, pl.ds(BLK, 1), :] - logs
    square = x_raw[z, pl.ds(0, BLK), :].T
    square = jnp.sum(square * square, axis=0, keepdims=True)
    mass = x_raw[z, pl.ds(BLK, 1), :]
    c_here = c_out[z]
    f_out[...] = ENTROPY * mass - (ENTROPY * LN2) * (LOG2E * mass - c_here[0:1, :]) + square * (1.0 / D)


def second_kernel(lists, quarter, x3, y3, c_ref, part_out, cols, top, total):
    top[...] = jnp.full(top.shape, LOWEST, jnp.float32)
    total[...] = jnp.zeros(total.shape, jnp.float32)

    def widen(b, carry):
        cols[b] = jnp.broadcast_to(c_ref[b, pl.ds(0, 1), :], (128, BLK)).T
        return carry

    lax.fori_loop(0, NZ, widen, 0)

    def pair(b, t):
        g = jnp.dot(x3[b], y3[t], preferred_element_type=jnp.float32)
        col = cols[b]
        u = g + jnp.concatenate([col, col], axis=1)
        u = u.reshape(BLK // 8, 8, BLK)
        old = top[t]
        new = jnp.maximum(old, jnp.max(u, axis=0))
        total[t] = total[t] * jnp.exp2(old - new) + jnp.sum(jnp.exp2(u - new[None]), axis=0)
        top[t] = new

    pairs_of(lists, quarter[0], pair)

    def close(t, carry):
        high = jnp.max(top[t], axis=0, keepdims=True)
        whole = jnp.sum(total[t] * jnp.exp2(top[t] - high), axis=0, keepdims=True)
        part_out[t] = jnp.where(whole > 0.0, high + jnp.log2(whole), LOWEST)
        return carry

    lax.fori_loop(0, NX * N_ROW, close, 0)


def col_exchange_kernel(part_ref, tgt_ref, mass_ref, g_out, got, send_sem, recv_sem):
    y, k, x, z = place()
    me = x * N_ROW + y * 2 + k
    many = NX * N_ROW
    barrier = pltpu.get_barrier_semaphore()

    def peer(n):
        other = lax.rem(me + n, many)
        return other, {"row": lax.rem(other, N_ROW), "col": (other // N_ROW) * NZ + z}

    for n in range(1, many):
        signal(barrier, peer(n)[1])
    pl.semaphore_wait(barrier, many - 1)
    copies = []
    for n in range(1, many):
        other, where = peer(n)
        copy = pltpu.make_async_remote_copy(
            src_ref=part_ref.at[other], dst_ref=got.at[n], send_sem=send_sem.at[n], recv_sem=recv_sem.at[n],
            device_id=where, device_id_type=MESH)
        copy.start()
        copies.append(copy)
    block = tgt_ref[...].T
    square = jnp.sum(block * block, axis=0, keepdims=True)
    for copy in copies:
        copy.wait()
    got[0] = part_ref[me]
    every = got[...]
    top = jnp.max(every, axis=0)
    total = jnp.sum(jnp.exp2(every - top[None]), axis=0)
    logs = top + jnp.log2(total)
    g_out[...] = ENTROPY * mass_ref[...] - (ENTROPY * LN2) * logs + square * (1.0 / D)

def nt_dot(a, b):
    return lax.dot_general(a, b, (((1,), (1,)), ((), ())), preferred_element_type=jnp.float32)


def merged_kernel(src_list, tgt_list, count_ref, src_ref, tgt_ref, pot_ref, mass_ref, mass_b_ref,
                  f_out, g_out, bad_out,
                  y_raw, x_raw, y3, x3, bias, top, total, scores, col_top, col_sum, tabs, tab_s, mine, row_out, row_logs, row_got,
                  col_out, col_got,
                  load_sem, send_sem, recv_sem, mate_send, mate_recv, z_send, z_recv, l_send, l_recv,
                  row_send, row_recv, col_send, col_recv):
    y, k, x, z = place()
    row = y * 2 + k
    sigma = 1 - 2 * k

    def wrap4(v):
        return lax.rem(v + 8, 4)

    def step_a(n):
        return wrap4(y + n * sigma * k), wrap4(x + n * sigma * (1 - k))

    def step_b(n):
        return wrap4(y + n * (1 - k)), wrap4(x + n * k)

    def dev_of(name):
        n = 1 if name[1] == "+" else -1
        ny, nx = step_a(n) if name[0] == "A" else step_b(n)
        return device(ny, k, nx, z)

    mate = device(y, 1 - k, x, z)
    z_long = device(y, k, x, lax.rem(z + sigma + NZ, NZ))
    z_short = device(y, k, x, lax.rem(z - sigma + NZ, NZ))

    def slot(da, db, core):
        oy = wrap4(y - db * (1 - core) + da * core)
        ox = wrap4(x - da * (1 - core) - db * core)
        return ox, oy * 2 + core

    loads = [
        pltpu.make_async_copy(tgt_ref, y_raw.at[x, row, pl.ds(0, BLK)], load_sem.at[0]),
        pltpu.make_async_copy(pot_ref, y_raw.at[x, row, pl.ds(BLK, 1)], load_sem.at[1]),
        pltpu.make_async_copy(src_ref, x_raw.at[z, pl.ds(0, BLK)], load_sem.at[2]),
        pltpu.make_async_copy(mass_ref, x_raw.at[z, pl.ds(BLK, 1)], load_sem.at[3]),
    ]
    for copy in loads:
        copy.start()
    barrier = pltpu.get_barrier_semaphore()
    peers = [device(y, k, wrap4(x + 1), z), device(y, k, wrap4(x + 3), z), device(y, k, wrap4(x + 2), z),
             device(wrap4(y + 1), k, x, z), device(wrap4(y + 3), k, x, z), mate, z_long, z_short]
    for peer in peers:
        signal(barrier, peer)

    ids = lax.broadcasted_iota(jnp.int32, (N_COL, 128), 0)
    left = lax.broadcasted_iota(jnp.int32, (N_COL, 128), 1) < 64
    live = count_ref[0]

    def enter(i, carry):
        table, named = carry
        one = jnp.where(i < live, tgt_list[i] + 1, 0)
        two = jnp.where(i + 32 < live, tgt_list[i + 32] + 1, 0)
        here = ids == src_list[i]
        table = table + jnp.where(here, jnp.where(left, one, two), 0)
        named = named + jnp.where(here, jnp.where(i < live, 1, 0), 0)
        return table, named

    nothing = jnp.zeros((N_COL, 128), jnp.int32)
    table, named = lax.fori_loop(0, 32, enter, (nothing, nothing))
    mine[...] = jnp.minimum(table, N_ROW)
    bad = jnp.max(jnp.where(named > 1, 1.0, 0.0), axis=0, keepdims=True)
    top[...] = jnp.full(top.shape, LOWEST, jnp.float32)
    total[...] = jnp.zeros(total.shape, jnp.float32)

    pl.semaphore_wait(barrier, len(peers))
    for copy in loads:
        copy.wait()

    pending = []

    def at(pos):
        return pos[0] * 4 + pos[1]

    def part(ref, ch):
        return ref.at[pl.ds(*CHUNKS[ch])]

    def remote(src, dst, send, recv, where):
        return pltpu.make_async_remote_copy(src_ref=src, dst_ref=dst, send_sem=send, recv_sem=recv,
                                            device_id=where, device_id_type=MESH)

    def start(copy):
        copy.start()
        pending.append(copy)

    def arrived(ref, sem):
        remote(ref, ref, send_sem.at[0, 0, 0], sem, mate).wait_recv()

    def send_y(pos, ch):
        ref = part(y_raw.at[slot(*pos, k)], ch)
        for n, (name, target) in enumerate(sends_of(*pos)):
            start(remote(ref, ref, send_sem.at[at(pos), ch, n], recv_sem.at[at(target), ch], dev_of(name)))

    def send_mate(pos, ch):
        ref = part(y_raw.at[slot(*pos, k)], ch)
        start(remote(ref, ref, mate_send.at[at(pos), ch], mate_recv.at[at(pos), ch], mate))

    def recv_y(pos, ch):
        arrived(part(y_raw.at[slot(*pos, k)], ch), recv_sem.at[at(pos), ch])

    def z_slot(n):
        return lax.rem(z - n * sigma + NZ * 4, NZ)

    def send_z(n, ch, long):
        target = n + 1 if long else n - 1
        ref = part(x_raw.at[z_slot(n)], ch)
        start(remote(ref, ref, z_send.at[n + 4, ch, 0 if long else 1], z_recv.at[target + 4, ch],
                     z_long if long else z_short))

    def recv_z(n, ch):
        arrived(part(x_raw.at[z_slot(n)], ch), z_recv.at[n + 4, ch])

    def prep_x(zb):
        hi, lo = split3(x_raw[zb, pl.ds(0, BLK), :])
        x3[zb, :, pl.ds(0, D)] = hi
        x3[zb, :, pl.ds(D, D)] = lo
        x3[zb, :, pl.ds(2 * D, D)] = hi

    def prep_y(da, db, core):
        xq, t = slot(da, db, core)
        block = y_raw[xq, t, pl.ds(0, BLK), :]
        square = jnp.sum(block * block, axis=1, keepdims=True)
        square = jnp.broadcast_to(square, (BLK, 128)).T[0:8]
        bias[xq, t] = KAPPA * (y_raw[xq, t, pl.ds(BLK, 1), :] - square * (1.0 / D))
        hi, lo = split3(block * (2.0 * KAPPA / D))
        y3[xq, t, :, pl.ds(0, D)] = hi
        y3[xq, t, :, pl.ds(D, D)] = hi
        y3[xq, t, :, pl.ds(2 * D, D)] = lo

    def prep_mate(da, db):
        for ch in (0, 1):
            arrived(part(y_raw.at[slot(da, db, 1 - k)], ch), mate_recv.at[da * 4 + db, ch])
        prep_y(da, db, 1 - k)

    def prep_loop(many, pos):
        def one(i, carry):
            da, db = pos(i)
            prep_y(da, db, k)
            prep_mate(da, db)
            return carry

        lax.fori_loop(0, many, one, 0)

    def pair(xq, zb):
        parts = []
        for n in (0, 1):
            t = tab_s[xq, zb, 64 * n]
            alive = t > 0
            t = lax.max(t - 1, 0)
            g = nt_dot(x3[zb], y3[xq, t])
            scores[xq, n, zb] = g
            shift = jnp.where(alive, bias[xq, t], LOWEST)[0:1]
            parts += [g[:, :128] + shift[:, :128], g[:, 128:] + shift[:, 128:]]
        old = top[zb]
        new = jnp.maximum(old, jnp.maximum(jnp.maximum(parts[0], parts[1]), jnp.maximum(parts[2], parts[3])))
        e = [jnp.exp2(v - new) for v in parts]
        total[zb] = total[zb] * jnp.exp2(old - new) + ((e[0] + e[1]) + (e[2] + e[3]))
        top[zb] = new

    def pair_loop(many, which):
        def one(i, carry):
            pair(*which(i))
            return carry

        lax.fori_loop(0, many, one, 0)

    for ch in (0, 1):
        send_y((0, 0), ch)
        send_z(0, ch, True)
        send_z(0, ch, False)
        send_mate((0, 0), ch)
    keep = pltpu.make_async_copy(mine.at[pl.ds(x * NZ, NZ)], tabs.at[x], load_sem.at[0])
    keep.start()
    for n in (1, 2, 3):
        to = wrap4(x + n)
        start(remote(mine.at[pl.ds(to * NZ, NZ)], tabs.at[x], l_send.at[n - 1], l_recv.at[n - 1], device(y, k, to, z)))
    keep.wait()
    prep_x(z)
    prep_y(0, 0, k)

    levels = (FIRST, SECOND, THIRD, FOURTH)

    def events(level):
        n = level + 1
        for ch in (0, 1):
            for pos in levels[level]:
                recv_y(pos, ch)
                send_y(pos, ch)
                send_mate(pos, ch)
            recv_z(n, ch)
            if n < 4:
                send_z(n, ch, True)
                recv_z(-n, ch)
                if n < 3:
                    send_z(-n, ch, False)

    def prep_xs(n):
        def one(i, carry):
            prep_x(z_slot(n * (1 - 2 * i)))
            return carry

        lax.fori_loop(0, 2 if n < 4 else 1, one, 0)

    def odd(i):
        return 1 + 2 * (i // 2)

    events(0)
    prep_xs(1)
    prep_mate(0, 0)
    prep_loop(4, lambda i: (odd(i) * lax.rem(i, 2), odd(i) * (1 - lax.rem(i, 2))))
    for n in (1, 2, 3):
        ref = tabs.at[wrap4(x - n)]
        arrived(ref, l_recv.at[n - 1])
    tab_copy = pltpu.make_async_copy(tabs, tab_s, load_sem.at[1])
    tab_copy.start()
    tab_copy.wait()
    events(1)
    prep_xs(2)
    prep_loop(2, lambda i: (2 * i, 2 - 2 * i))
    pair_loop(5, lambda i: (x, z_slot(i - 2)))
    prep_loop(4, lambda i: (odd(i), 1 + 2 * lax.rem(i, 2)))
    events(2)
    prep_xs(3)
    prep_loop(4, lambda i: (odd(i) * lax.rem(i, 2) + 2 * (1 - lax.rem(i, 2)),
                            odd(i) * (1 - lax.rem(i, 2)) + 2 * lax.rem(i, 2)))
    pair_loop(2, lambda i: (x, z_slot(6 * i - 3)))
    pair_loop(7, lambda i: (wrap4(x - 1), z_slot(i - 3)))
    events(3)
    prep_xs(4)
    pair_loop(7, lambda i: (wrap4(x + 1), z_slot(i - 3)))
    pair_loop(3, lambda i: (wrap4(x - i - i // 2), z_slot(4)))
    prep_loop(1, lambda i: (2 + i, 2 + i))
    pair_loop(8, lambda i: (wrap4(x + 2), z_slot(i - 3)))

    def close(b, logs):
        high = jnp.max(top[b], axis=1, keepdims=True)
        whole = jnp.sum(total[b] * jnp.exp2(top[b] - high), axis=1, keepdims=True)
        mine_b = jnp.where(whole > 0.0, high + jnp.log2(whole), LOWEST)
        lane = lax.broadcasted_iota(jnp.int32, (BLK, 128), 1)
        return jnp.where(lane == b, mine_b, logs)

    logs = lax.fori_loop(0, NZ, close, jnp.zeros((BLK, 128), jnp.float32)).T[0:NZ]
    row_out[:, pl.ds(0, BLK)] = logs
    row_out[:, pl.ds(BLK, 128)] = jnp.broadcast_to(bad, (NZ, 128))
    for n in range(1, NZ):
        start(remote(row_out, row_got.at[n - 1], row_send.at[n - 1], row_recv.at[n - 1],
                     device(y, k, x, lax.rem(z + n, NZ))))
    own_x = x_raw[z, pl.ds(0, BLK), :]
    own_x = jnp.broadcast_to(jnp.sum(own_x * own_x, axis=1, keepdims=True), (BLK, 128)).T[0:1]
    own_y = y_raw[x, row, pl.ds(0, BLK), :]
    own_y = jnp.broadcast_to(jnp.sum(own_y * own_y, axis=1, keepdims=True), (BLK, 128)).T[0:1]
    masses = x_raw[:, pl.ds(BLK, 1), :].reshape(NZ, BLK)
    for n in range(1, NZ):
        arrived(row_got.at[n - 1], row_recv.at[n - 1])
    others = [row_got[n, :, pl.ds(0, BLK)] for n in range(NZ - 1)]
    for n in range(NZ - 1):
        bad = jnp.maximum(bad, row_got[n, pl.ds(0, 1), pl.ds(BLK, 128)])
    high = logs
    for v in others:
        high = jnp.maximum(high, v)
    whole = jnp.exp2(logs - high)
    for v in others:
        whole = whole + jnp.exp2(v - high)
    logs = high + jnp.log2(whole)
    shift = LOG2E * masses - logs
    row_logs[...] = logs
    f_out[...] = (ENTROPY * x_raw[z, pl.ds(BLK, 1), :] - (ENTROPY * LN2) * row_logs[pl.ds(z, 1), :]
                  + own_x * (1.0 / D))
    for b in range(NZ):
        top[b] = jnp.broadcast_to(shift[b:b + 1], (128, BLK)).T

    def second(i, carry):
        xq, zb = i // NZ, lax.rem(i, NZ)
        for n in (0, 1):
            for h in (0, 128):
                u = (scores[xq, n, zb, :, pl.ds(h, 128)] + top[zb]).reshape(BLK // 8, 8, 128)
                m = jnp.max(u, axis=0)
                col_top[xq, n, zb, :, pl.ds(h, 128)] = m
                col_sum[xq, n, zb, :, pl.ds(h, 128)] = jnp.sum(jnp.exp2(u - m[None]), axis=0)
        return carry

    lax.fori_loop(0, NX * NZ, second, 0)

    def columns(xq, carry):
        m = col_top[xq].reshape(2 * NZ, 8, BLK)
        high = jnp.max(m, axis=1)
        whole = jnp.sum(col_sum[xq].reshape(2 * NZ, 8, BLK) * jnp.exp2(m - high[:, None, :]), axis=1)
        slots = high + jnp.log2(whole)
        named = tabs[xq]
        named = jnp.concatenate([jnp.broadcast_to(named[:, 0:1], (NZ, BLK)),
                                 jnp.broadcast_to(named[:, 64:65], (NZ, BLK))], axis=0)
        for t in range(N_ROW):
            v = jnp.where(named == t + 1, slots, LOWEST)
            high = jnp.max(v, axis=0, keepdims=True)
            whole = jnp.sum(jnp.exp2(v - high), axis=0, keepdims=True)
            col_out[xq, t, :, pl.ds(0, BLK)] = high + jnp.log2(whole)
            col_out[xq, t, :, pl.ds(BLK, 128)] = bad
        return carry

    lax.fori_loop(0, NX, columns, 0)
    many = NX * N_ROW
    me = x * N_ROW + row

    def peer(n):
        other = lax.rem(me + n, many)
        return other // N_ROW, lax.rem(other, N_ROW)

    for n in range(1, many):
        ox, orow = peer(n)
        start(remote(col_out.at[ox, orow], col_got.at[n], col_send.at[n], col_recv.at[n],
                     {"row": orow, "col": ox * NZ + z}))
    col_got[0] = col_out[x, row]
    for n in range(1, many):
        arrived(col_got.at[n], col_recv.at[n])
    every = col_got[:, :, pl.ds(0, BLK)]
    high = jnp.max(every, axis=0)
    whole = jnp.sum(jnp.exp2(every - high[None]), axis=0)
    g_out[...] = (ENTROPY * mass_b_ref[...] - (ENTROPY * LN2) * (high + jnp.log2(whole)) + own_y * (1.0 / D))
    bad_out[...] = jnp.max(col_got[:, :, pl.ds(BLK, 128)], axis=0)
    for copy in pending:
        copy.wait_send()


def shape(*dims, kind=jnp.float32):
    return jax.ShapeDtypeStruct(dims, kind)


def general(sources, targets, g_pot, log_a, log_b, src_block, tgt_block, pair_count):
    whole = pl.BlockSpec(memory_space=pltpu.VMEM)
    anywhere = pl.BlockSpec(memory_space=pl.ANY)
    scalars = pl.BlockSpec(memory_space=pltpu.SMEM)
    dma = pltpu.SemaphoreType.DMA
    packed = jnp.zeros((8, 128), jnp.int32)
    packed = packed.at[0, :64].set(src_block).at[0, 64:].set(tgt_block).at[1, 0].set(pair_count[0])
    x_raw, y_raw, lists = pl.pallas_call(
        gather_kernel,
        out_shape=(shape(NZ, ROWS, D), shape(NX, N_ROW, ROWS, D), shape(NX, 8, 128, kind=jnp.int32)),
        in_specs=[anywhere] * 5,
        out_specs=(whole, whole, whole),
        scratch_shapes=[dma((5,)), dma((16, 2, 4)), dma((16, 2)), dma((16, 2)), dma((16, 2)),
                        dma((9, 2, 2)), dma((9, 2)), dma((3,)), dma((3,))],
        compiler_params=pltpu.CompilerParams(collective_id=3, has_side_effects=True, vmem_limit_bytes=VMEM_LIMIT),
    )(sources, targets, g_pot[None], log_a[None], packed)
    y_raw = y_raw.reshape(NX * N_ROW, ROWS, D)
    quarter = (lax.axis_index("col") // NZ).astype(jnp.int32).reshape(1)
    x3, y3, part = pl.pallas_call(
        first_kernel,
        out_shape=(shape(NZ, BLK, 3 * D, kind=jnp.bfloat16), shape(NX * N_ROW, 3 * D, BLK, kind=jnp.bfloat16),
                   shape(NZ, 8, BLK)),
        in_specs=[scalars, scalars, whole, whole],
        out_specs=(whole, whole, whole),
        scratch_shapes=[pltpu.VMEM((NX * N_ROW, 8, BLK), jnp.float32), pltpu.VMEM((NZ, BLK, 128), jnp.float32),
                        pltpu.VMEM((NZ, BLK, 128), jnp.float32)],
        compiler_params=pltpu.CompilerParams(vmem_limit_bytes=VMEM_LIMIT),
    )(lists, quarter, x_raw, y_raw)
    f_own, c_all = pl.pallas_call(
        row_exchange_kernel,
        out_shape=(shape(1, BLK), shape(NZ, 8, BLK)),
        in_specs=[whole, whole],
        out_specs=(whole, whole),
        scratch_shapes=[pltpu.VMEM((NZ - 1, NZ, 8, BLK), jnp.float32), dma((NZ - 1,)), dma((NZ - 1,))],
        compiler_params=pltpu.CompilerParams(collective_id=1, has_side_effects=True, vmem_limit_bytes=VMEM_LIMIT),
    )(part, x_raw)
    sums = pl.pallas_call(
        second_kernel,
        out_shape=shape(NX * N_ROW, 1, BLK),
        in_specs=[scalars, scalars, whole, whole, whole],
        out_specs=whole,
        scratch_shapes=[pltpu.VMEM((NZ, BLK, 128), jnp.float32), pltpu.VMEM((NX * N_ROW, 8, BLK), jnp.float32),
                        pltpu.VMEM((NX * N_ROW, 8, BLK), jnp.float32)],
        compiler_params=pltpu.CompilerParams(vmem_limit_bytes=VMEM_LIMIT),
    )(lists, quarter, x3, y3, c_all)
    g_own = pl.pallas_call(
        col_exchange_kernel,
        out_shape=shape(1, BLK),
        in_specs=[whole, whole, whole],
        out_specs=whole,
        scratch_shapes=[pltpu.VMEM((NX * N_ROW, 1, BLK), jnp.float32), dma((NX * N_ROW,)), dma((NX * N_ROW,))],
        compiler_params=pltpu.CompilerParams(collective_id=2, has_side_effects=True),
    )(sums, targets, log_b[None])
    return f_own.reshape(BLK), g_own.reshape(BLK)


def local(sources, targets, g_pot, log_a, log_b, src_block, tgt_block, pair_count):
    whole = pl.BlockSpec(memory_space=pltpu.VMEM)
    anywhere = pl.BlockSpec(memory_space=pl.ANY)
    scalars = pl.BlockSpec(memory_space=pltpu.SMEM)
    dma = pltpu.SemaphoreType.DMA
    vmem = pltpu.VMEM
    f32 = jnp.float32
    f_own, g_own, bad = pl.pallas_call(
        merged_kernel,
        out_shape=(shape(1, BLK), shape(1, BLK), shape(1, 128)),
        in_specs=[scalars] * 3 + [anywhere] * 4 + [whole],
        out_specs=(whole, whole, whole),
        scratch_shapes=[
            vmem((NX, N_ROW, ROWS, D), f32), vmem((NZ, ROWS, D), f32),
            vmem((NX, N_ROW, BLK, 3 * D), jnp.bfloat16), vmem((NZ, BLK, 3 * D), jnp.bfloat16),
            vmem((NX, N_ROW, 8, BLK), f32), vmem((NZ, BLK, 128), f32), vmem((NZ, BLK, 128), f32),
            vmem((NX, 2, NZ, BLK, BLK), f32), vmem((NX, 2, NZ, 8, BLK), f32), vmem((NX, 2, NZ, 8, BLK), f32),
            vmem((NX, NZ, 128), jnp.int32), pltpu.SMEM((NX, NZ, 128), jnp.int32), vmem((N_COL, 128), jnp.int32),
            vmem((NZ, BLK + 128), f32), vmem((NZ, BLK), f32), vmem((NZ - 1, NZ, BLK + 128), f32),
            vmem((NX, N_ROW, 1, BLK + 128), f32), vmem((NX * N_ROW, 1, BLK + 128), f32),
            dma((4,)), dma((16, 2, 4)), dma((16, 2)), dma((16, 2)), dma((16, 2)),
            dma((9, 2, 2)), dma((9, 2)), dma((3,)), dma((3,)),
            dma((NZ - 1,)), dma((NZ - 1,)), dma((NX * N_ROW,)), dma((NX * N_ROW,))],
        compiler_params=pltpu.CompilerParams(collective_id=0, has_side_effects=True, vmem_limit_bytes=VMEM_LIMIT),
    )(src_block, tgt_block, pair_count, sources, targets, g_pot[None], log_a[None], log_b[None])
    args = (sources, targets, g_pot, log_a, log_b, src_block, tgt_block, pair_count)
    return lax.cond(bad[0, 0] > 0.5, lambda: general(*args), lambda: (f_own.reshape(BLK), g_own.reshape(BLK)))


def solution(mesh):
    placed = (
        P(("row", "col"), None),
        P(("col", "row"), None),
        P(("col", "row")),
        P(("row", "col")),
        P(("col", "row")),
        P(("row", "col")),
        P(("row", "col")),
        P(("row", "col")),
    )
    return jax.shard_map(
        local,
        mesh=mesh,
        in_specs=placed,
        out_specs=(P(("row", "col")), P(("col", "row"))),
        check_vma=False,
    )
```

```python
import functools
import math

import jax
import jax.numpy as jnp
from jax import lax
from jax.experimental import pallas as pl
from jax.experimental.pallas import tpu as pltpu
from jax.sharding import PartitionSpec as P

MESH = pl.DeviceIdType.MESH
BLK = 256
D = 256
ROWS = 264
NX, NY, NZ = 4, 4, 8
N_ROW, N_COL = 8, 32
ENTROPY = 0.05
LOG2E = 1.0 / math.log(2.0)
LN2 = math.log(2.0)
KAPPA = LOG2E / ENTROPY
LOWEST = -1.0e30
CHUNKS = ((0, 128), (128, 136))
VMEM_LIMIT = 60 * 1024 * 1024


def place():
    r, c = lax.axis_index("row"), lax.axis_index("col")
    return r // 2, lax.rem(r, 2), c // NZ, lax.rem(c, NZ)


def device(y, core, x, z):
    return {"row": y * 2 + core, "col": x * NZ + z}


def signal(sem, where):
    pl.semaphore_signal(sem, inc=1, device_id=where, device_id_type=MESH)


FIRST = ((1, 0), (3, 0), (0, 1), (0, 3))
SECOND = ((2, 0), (1, 1), (1, 3), (3, 1), (3, 3), (0, 2))
THIRD = ((2, 1), (2, 3), (1, 2), (3, 2))
FOURTH = ((2, 2),)


def sends_of(da, db):
    out = []
    if db == 0:
        if da == 0:
            out += [("A+", (1, 0)), ("A-", (3, 0))]
        if da == 1:
            out += [("A+", (2, 0))]
        out += [("B+", (da, 1)), ("B-", (da, 3))]
    elif db == 1 and da in (0, 1):
        out += [("B+", (da, 2))]
    elif db == 3 and da in (2, 3):
        out += [("B-", (da, 2))]
    return out


REACHED = FIRST + SECOND + THIRD + FOURTH
OTHER_WAY = {"A+": "A-", "A-": "A+", "B+": "B+", "B-": "B-"}


def mirror(pos):
    return (4 - pos[0]) % 4, pos[1]


def chunk_sends(pos, ch):
    if ch == 0:
        return sends_of(*pos)
    return [(OTHER_WAY[name], mirror(target)) for name, target in sends_of(*mirror(pos))]


PARTS = ((0, 128), (128, 136))
STEPS = (
    ("X", 0), ("Y", 0, 0), ("M", 0, 0), ("y", 0, 3, 0), ("z", -1, 0), ("y", 3, 0, 0), ("y", 1, 0, 0), ("z", 1, 0),
    ("y", 0, 1, 0), ("y", 1, 0, 1), ("y", 0, 1, 1), ("z", 1, 1), ("y", 0, 3, 1), ("z", -1, 1), ("y", 3, 0, 1),
    ("X", 1), ("X", -1), ("Y", 1, 0), ("Y", 3, 0), ("Y", 0, 1), ("Y", 0, 3), ("M", 1, 0), ("M", 0, 1), ("M", 0, 3),
    ("z", -2, 0), ("z", 2, 0), ("y", 3, 1, 0), ("y", 3, 3, 0), ("y", 2, 0, 0), ("M", 3, 0), ("y", 2, 0, 1),
    ("Y", 2, 0), ("y", 1, 3, 0), ("y", 1, 1, 0), ("M", 2, 0), ("y", 0, 2, 0), ("z", -2, 1), ("z", 2, 1), ("X", 2),
    ("y", 1, 3, 1), ("X", -2), ("Y", 1, 3), ("y", 1, 1, 1), ("Y", 1, 1), ("y", 3, 3, 1), ("Y", 3, 3), ("M", 1, 3),
    ("z", -3, 0), ("z", 3, 0), ("M", 1, 1), ("y", 0, 2, 1), ("y", 3, 2, 0), ("Y", 0, 2), ("M", 3, 3), ("y", 2, 3, 0),
    ("M", 0, 2), ("y", 3, 1, 1), ("Y", 3, 1), ("D", 0, 1), ("y", 2, 1, 0), ("z", -3, 1), ("y", 2, 3, 1), ("z", 3, 1),
    ("X", 3), ("X", -3), ("Y", 2, 3), ("M", 3, 1), ("D", -1, 2), ("z", 4, 0), ("y", 1, 2, 1), ("y", 2, 1, 1),
    ("Y", 2, 1), ("D", -2, 3), ("M", 2, 3), ("z", 4, 1), ("y", 1, 2, 0), ("y", 2, 2, 0), ("X", 4), ("Y", 1, 2),
    ("D", -3, 4), ("M", 2, 1), ("M", 1, 2), ("y", 3, 2, 1), ("y", 2, 2, 1), ("Y", 3, 2), ("Y", 2, 2), ("M", 3, 2),
    ("M", 2, 2),
)


def gather_kernel(src_ref, tgt_ref, pot_ref, mass_ref, list_ref, x_out, y_out, lists_out,
                  load_sem, send_sem, recv_sem, mate_send, mate_recv, z_send, z_recv, l_send, l_recv):
    y, k, x, z = place()
    row = y * 2 + k

    def wrap4(v):
        return lax.rem(v + 8, 4)

    sigma = 1 - 2 * k

    def step_a(n):
        return wrap4(y + n * sigma * k), wrap4(x + n * sigma * (1 - k))

    def step_b(n):
        return wrap4(y + n * (1 - k)), wrap4(x + n * k)

    def dev_of(name):
        n = 1 if name[1] == "+" else -1
        ny, nx = step_a(n) if name[0] == "A" else step_b(n)
        return device(ny, k, nx, z)

    mate = device(y, 1 - k, x, z)
    z_long = device(y, k, x, lax.rem(z + sigma + NZ, NZ))
    z_short = device(y, k, x, lax.rem(z - sigma + NZ, NZ))

    def slot(da, db, core=None):
        if core is None:
            core = k
        oy = wrap4(y - db * (1 - core) + da * core)
        ox = wrap4(x - da * (1 - core) - db * core)
        return ox, oy * 2 + core

    loads = [
        pltpu.make_async_copy(tgt_ref, y_out.at[x, row, pl.ds(0, BLK)], load_sem.at[0]),
        pltpu.make_async_copy(pot_ref, y_out.at[x, row, pl.ds(BLK, 1)], load_sem.at[1]),
        pltpu.make_async_copy(src_ref, x_out.at[z, pl.ds(0, BLK)], load_sem.at[2]),
        pltpu.make_async_copy(mass_ref, x_out.at[z, pl.ds(BLK, 1)], load_sem.at[3]),
        pltpu.make_async_copy(list_ref, lists_out.at[x], load_sem.at[4]),
    ]
    for copy in loads:
        copy.start()
    barrier = pltpu.get_barrier_semaphore()
    peers = [device(y, k, wrap4(x + 1), z), device(y, k, wrap4(x + 3), z), device(y, k, wrap4(x + 2), z),
             device(wrap4(y + 1), k, x, z), device(wrap4(y + 3), k, x, z), mate, z_long, z_short]
    for peer in peers:
        signal(barrier, peer)
    pl.semaphore_wait(barrier, len(peers))
    for copy in loads:
        copy.wait()

    pending = []

    def at(pos):
        return pos[0] * 4 + pos[1]

    def part(ref, ch):
        return ref.at[pl.ds(*CHUNKS[ch])]

    def y_copy(pos, ch, where, target, n):
        ox, orow = slot(*pos)
        return pltpu.make_async_remote_copy(
            src_ref=part(y_out.at[ox, orow], ch), dst_ref=part(y_out.at[ox, orow], ch),
            send_sem=send_sem.at[at(pos), ch, n], recv_sem=recv_sem.at[at(target), ch],
            device_id=where, device_id_type=MESH)

    def mate_copy(pos, ch):
        ox, orow = slot(*pos)
        return pltpu.make_async_remote_copy(
            src_ref=part(y_out.at[ox, orow], ch), dst_ref=part(y_out.at[ox, orow], ch),
            send_sem=mate_send.at[at(pos), ch], recv_sem=mate_recv.at[at(pos), ch],
            device_id=mate, device_id_type=MESH)

    def send_y(pos, ch):
        for n, (name, target) in enumerate(sends_of(*pos)):
            copy = y_copy(pos, ch, dev_of(name), target, n)
            copy.start()
            pending.append(copy)
        copy = mate_copy(pos, ch)
        copy.start()
        pending.append(copy)

    def recv_y(pos, ch):
        ox, orow = slot(*pos)
        ref = part(y_out.at[ox, orow], ch)
        pltpu.make_async_remote_copy(src_ref=ref, dst_ref=ref, send_sem=send_sem.at[0, 0, 0],
                                     recv_sem=recv_sem.at[at(pos), ch], device_id=mate,
                                     device_id_type=MESH).wait_recv()

    def recv_mate(pos, ch):
        ox, orow = slot(*pos, core=1 - k)
        ref = part(y_out.at[ox, orow], ch)
        pltpu.make_async_remote_copy(src_ref=ref, dst_ref=ref, send_sem=send_sem.at[0, 0, 0],
                                     recv_sem=mate_recv.at[at(pos), ch], device_id=mate,
                                     device_id_type=MESH).wait_recv()

    def z_slot(n):
        return lax.rem(z - n * sigma + NZ * 4, NZ)

    def send_z(n, ch, long):
        target = n + 1 if long else n - 1
        ref = part(x_out.at[z_slot(n)], ch)
        copy = pltpu.make_async_remote_copy(
            src_ref=ref, dst_ref=ref, send_sem=z_send.at[n + 4, ch, 0 if long else 1],
            recv_sem=z_recv.at[target + 4, ch],
            device_id=z_long if long else z_short, device_id_type=MESH)
        copy.start()
        pending.append(copy)

    def recv_z(n, ch):
        ref = part(x_out.at[z_slot(n)], ch)
        pltpu.make_async_remote_copy(src_ref=ref, dst_ref=ref, send_sem=send_sem.at[0, 0, 0],
                                     recv_sem=z_recv.at[n + 4, ch], device_id=mate,
                                     device_id_type=MESH).wait_recv()

    for n in (1, 2, 3):
        copy = pltpu.make_async_remote_copy(
            src_ref=lists_out.at[x], dst_ref=lists_out.at[x], send_sem=l_send.at[n - 1], recv_sem=l_recv.at[n - 1],
            device_id=device(y, k, wrap4(x + n), z), device_id_type=MESH)
        copy.start()
        pending.append(copy)
    for ch in (0, 1):
        send_y((0, 0), ch)
        send_z(0, ch, True)
        send_z(0, ch, False)
    levels = (FIRST, SECOND, THIRD, FOURTH)
    for level in range(4):
        for ch in (0, 1):
            for pos in levels[level]:
                recv_y(pos, ch)
                send_y(pos, ch)
            n = level + 1
            recv_z(n, ch)
            if n < 4:
                send_z(n, ch, True)
                recv_z(-n, ch)
                if n < 3:
                    send_z(-n, ch, False)
    for n in (1, 2, 3):
        ref = lists_out.at[wrap4(x - n)]
        pltpu.make_async_remote_copy(src_ref=ref, dst_ref=ref, send_sem=l_send.at[0], recv_sem=l_recv.at[n - 1],
                                     device_id=mate, device_id_type=MESH).wait_recv()
    for ch in (0, 1):
        for da in range(4):
            for db in range(4):
                recv_mate((da, db), ch)
    for copy in pending:
        copy.wait_send()


def split3(v):
    hi = v.astype(jnp.bfloat16)
    lo = (v - hi.astype(jnp.float32)).astype(jnp.bfloat16)
    return hi, lo


def prep_kernel_body(x_raw, y_raw, x3, y3, bias):
    def one_x(i, carry):
        hi, lo = split3(x_raw[i, pl.ds(0, BLK), :])
        x3[i, :, pl.ds(0, D)] = hi
        x3[i, :, pl.ds(D, D)] = lo
        x3[i, :, pl.ds(2 * D, D)] = hi
        return carry

    lax.fori_loop(0, NZ, one_x, 0)

    def one_y(i, carry):
        block = y_raw[i, pl.ds(0, BLK), :].T
        pot = y_raw[i, pl.ds(BLK, 1), :]
        square = jnp.sum(block * block, axis=0, keepdims=True)
        row = KAPPA * (pot - square * (1.0 / D))
        bias[i] = jnp.broadcast_to(row, (8, BLK))
        hi, lo = split3(block * (2.0 * KAPPA / D))
        y3[i, pl.ds(0, D), :] = hi
        y3[i, pl.ds(D, D), :] = hi
        y3[i, pl.ds(2 * D, D), :] = lo
        return carry

    lax.fori_loop(0, NX * N_ROW, one_y, 0)


def pairs_of(lists, quarter, body):
    for other in range(NX):
        def one(i, carry, other=other):
            src = lists[other, 0, i]

            @pl.when(src // NZ == quarter)
            def _():
                body(lax.rem(src, NZ), other * N_ROW + lists[other, 0, 64 + i])
            return carry

        lax.fori_loop(0, lists[other, 1, 0], one, 0)


def first_kernel(lists, quarter, x_raw, y_raw, x3, y3, part_out, bias, top, total):
    prep_kernel_body(x_raw, y_raw, x3, y3, bias)
    top[...] = jnp.full(top.shape, LOWEST, jnp.float32)
    total[...] = jnp.zeros(total.shape, jnp.float32)

    def pair(b, t):
        g = jnp.dot(x3[b], y3[t], preferred_element_type=jnp.float32)
        row = bias[t]
        s1 = g[:, :128] + row[0:1, :128]
        s2 = g[:, 128:] + row[0:1, 128:]
        old = top[b]
        new = jnp.maximum(old, jnp.maximum(s1, s2))
        total[b] = total[b] * jnp.exp2(old - new) + jnp.exp2(s1 - new) + jnp.exp2(s2 - new)
        top[b] = new

    pairs_of(lists, quarter[0], pair)

    def close(b, carry):
        high = jnp.max(top[b], axis=1, keepdims=True)
        whole = jnp.sum(total[b] * jnp.exp2(top[b] - high), axis=1, keepdims=True)
        logs = jnp.where(whole > 0.0, high + jnp.log2(whole), LOWEST)
        part_out[b] = jnp.broadcast_to(logs, (BLK, 128)).T[0:8, :]
        return carry

    lax.fori_loop(0, NZ, close, 0)


def row_exchange_kernel(part_ref, x_raw, f_out, c_out, got, send_sem, recv_sem):
    y, k, x, z = place()
    barrier = pltpu.get_barrier_semaphore()
    for n in range(1, NZ):
        signal(barrier, device(y, k, x, lax.rem(z + n, NZ)))
    pl.semaphore_wait(barrier, NZ - 1)
    copies = []
    for n in range(1, NZ):
        copy = pltpu.make_async_remote_copy(
            src_ref=part_ref, dst_ref=got.at[n - 1], send_sem=send_sem.at[n - 1], recv_sem=recv_sem.at[n - 1],
            device_id=device(y, k, x, lax.rem(z + n, NZ)), device_id_type=MESH)
        copy.start()
        copies.append(copy)
    for copy in copies:
        copy.wait()
    own = part_ref[...]
    others = [got[n] for n in range(NZ - 1)]
    top = own
    for v in others:
        top = jnp.maximum(top, v)
    total = jnp.exp2(own - top)
    for v in others:
        total = total + jnp.exp2(v - top)
    logs = top + jnp.log2(total)
    c_out[...] = LOG2E * x_raw[:, pl.ds(BLK, 1), :] - logs
    square = x_raw[z, pl.ds(0, BLK), :].T
    square = jnp.sum(square * square, axis=0, keepdims=True)
    mass = x_raw[z, pl.ds(BLK, 1), :]
    c_here = c_out[z]
    f_out[...] = ENTROPY * mass - (ENTROPY * LN2) * (LOG2E * mass - c_here[0:1, :]) + square * (1.0 / D)


def second_kernel(lists, quarter, x3, y3, c_ref, part_out, cols, top, total):
    top[...] = jnp.full(top.shape, LOWEST, jnp.float32)
    total[...] = jnp.zeros(total.shape, jnp.float32)

    def widen(b, carry):
        cols[b] = jnp.broadcast_to(c_ref[b, pl.ds(0, 1), :], (128, BLK)).T
        return carry

    lax.fori_loop(0, NZ, widen, 0)

    def pair(b, t):
        g = jnp.dot(x3[b], y3[t], preferred_element_type=jnp.float32)
        col = cols[b]
        u = g + jnp.concatenate([col, col], axis=1)
        u = u.reshape(BLK // 8, 8, BLK)
        old = top[t]
        new = jnp.maximum(old, jnp.max(u, axis=0))
        total[t] = total[t] * jnp.exp2(old - new) + jnp.sum(jnp.exp2(u - new[None]), axis=0)
        top[t] = new

    pairs_of(lists, quarter[0], pair)

    def close(t, carry):
        high = jnp.max(top[t], axis=0, keepdims=True)
        whole = jnp.sum(total[t] * jnp.exp2(top[t] - high), axis=0, keepdims=True)
        part_out[t] = jnp.where(whole > 0.0, high + jnp.log2(whole), LOWEST)
        return carry

    lax.fori_loop(0, NX * N_ROW, close, 0)


def col_exchange_kernel(part_ref, tgt_ref, mass_ref, g_out, got, send_sem, recv_sem):
    y, k, x, z = place()
    me = x * N_ROW + y * 2 + k
    many = NX * N_ROW
    barrier = pltpu.get_barrier_semaphore()

    def peer(n):
        other = lax.rem(me + n, many)
        return other, {"row": lax.rem(other, N_ROW), "col": (other // N_ROW) * NZ + z}

    for n in range(1, many):
        signal(barrier, peer(n)[1])
    pl.semaphore_wait(barrier, many - 1)
    copies = []
    for n in range(1, many):
        other, where = peer(n)
        copy = pltpu.make_async_remote_copy(
            src_ref=part_ref.at[other], dst_ref=got.at[n], send_sem=send_sem.at[n], recv_sem=recv_sem.at[n],
            device_id=where, device_id_type=MESH)
        copy.start()
        copies.append(copy)
    block = tgt_ref[...].T
    square = jnp.sum(block * block, axis=0, keepdims=True)
    for copy in copies:
        copy.wait()
    got[0] = part_ref[me]
    every = got[...]
    top = jnp.max(every, axis=0)
    total = jnp.sum(jnp.exp2(every - top[None]), axis=0)
    logs = top + jnp.log2(total)
    g_out[...] = ENTROPY * mass_ref[...] - (ENTROPY * LN2) * logs + square * (1.0 / D)

def nt_dot(a, b):
    return lax.dot_general(a, b, (((1,), (1,)), ((), ())), preferred_element_type=jnp.float32)


def merged_kernel(src_list, tgt_list, count_ref, src_ref, tgt_ref, pot_ref, mass_ref, mass_b_ref,
                  f_out, g_out, bad_out,
                  y_raw, x_raw, y3, x3, bias, top, total, scores, col_top, col_sum, tabs, tab_s, mine, row_out, row_logs, row_got,
                  col_out, col_got,
                  load_sem, send_sem, recv_sem, mate_send, mate_recv, z_send, z_recv, l_send, l_recv,
                  row_send, row_recv, col_send, col_recv):
    y, k, x, z = place()
    row = y * 2 + k
    sigma = 1 - 2 * k

    def wrap4(v):
        return lax.rem(v + 8, 4)

    def step_a(n):
        return wrap4(y + n * sigma * k), wrap4(x + n * sigma * (1 - k))

    def step_b(n):
        return wrap4(y + n * (1 - k)), wrap4(x + n * k)

    def dev_of(name):
        n = 1 if name[1] == "+" else -1
        ny, nx = step_a(n) if name[0] == "A" else step_b(n)
        return device(ny, k, nx, z)

    mate = device(y, 1 - k, x, z)
    z_long = device(y, k, x, lax.rem(z + sigma + NZ, NZ))
    z_short = device(y, k, x, lax.rem(z - sigma + NZ, NZ))

    def slot(da, db, core):
        oy = wrap4(y - db * (1 - core) + da * core)
        ox = wrap4(x - da * (1 - core) - db * core)
        return ox, oy * 2 + core

    loads = [
        pltpu.make_async_copy(tgt_ref, y_raw.at[x, row, pl.ds(0, BLK)], load_sem.at[0]),
        pltpu.make_async_copy(pot_ref, y_raw.at[x, row, pl.ds(BLK, 1)], load_sem.at[1]),
        pltpu.make_async_copy(src_ref, x_raw.at[z, pl.ds(0, BLK)], load_sem.at[2]),
        pltpu.make_async_copy(mass_ref, x_raw.at[z, pl.ds(BLK, 1)], load_sem.at[3]),
    ]
    for copy in loads:
        copy.start()
    barrier = pltpu.get_barrier_semaphore()
    peers = [device(y, k, wrap4(x + 1), z), device(y, k, wrap4(x + 3), z), device(y, k, wrap4(x + 2), z),
             device(wrap4(y + 1), k, x, z), device(wrap4(y + 3), k, x, z), mate, z_long, z_short]
    for peer in peers:
        signal(barrier, peer)

    pl.semaphore_wait(barrier, len(peers))
    for copy in loads:
        copy.wait()

    pending = []

    def at(pos):
        return pos[0] * 4 + pos[1]

    def part(ref, ch):
        return ref.at[pl.ds(*PARTS[ch])]

    def remote(src, dst, send, recv, where):
        return pltpu.make_async_remote_copy(src_ref=src, dst_ref=dst, send_sem=send, recv_sem=recv,
                                            device_id=where, device_id_type=MESH)

    def start(copy):
        copy.start()
        pending.append(copy)

    def arrived(ref, sem):
        remote(ref, ref, send_sem.at[0, 0, 0], sem, mate).wait_recv()

    def send_y(pos, ch):
        ref = part(y_raw.at[slot(*pos, k)], ch)
        for n, (name, target) in enumerate(chunk_sends(pos, ch)):
            start(remote(ref, ref, send_sem.at[at(pos), ch, n], recv_sem.at[at(target), ch], dev_of(name)))

    def send_mate(pos, ch):
        ref = part(y_raw.at[slot(*pos, k)], ch)
        start(remote(ref, ref, mate_send.at[at(pos), ch], mate_recv.at[at(pos), ch], mate))

    def recv_y(pos, ch):
        arrived(part(y_raw.at[slot(*pos, k)], ch), recv_sem.at[at(pos), ch])

    def z_slot(n):
        return lax.rem(z - n * sigma + NZ * 4, NZ)

    def send_z(n, ch, long):
        target = n + 1 if long else n - 1
        ref = part(x_raw.at[z_slot(n)], ch)
        start(remote(ref, ref, z_send.at[n + 4, ch, 0 if long else 1], z_recv.at[target + 4, ch],
                     z_long if long else z_short))

    def recv_z(n, ch):
        arrived(part(x_raw.at[z_slot(n)], ch), z_recv.at[n + 4, ch])

    def prep_x(zb):
        hi, lo = split3(x_raw[zb, pl.ds(0, BLK), :])
        x3[zb, :, pl.ds(0, D)] = hi
        x3[zb, :, pl.ds(D, D)] = lo
        x3[zb, :, pl.ds(2 * D, D)] = hi

    def prep_y(da, db, core):
        xq, t = slot(da, db, core)
        block = y_raw[xq, t, pl.ds(0, BLK), :]
        square = jnp.sum(block * block, axis=1, keepdims=True)
        square = jnp.broadcast_to(square, (BLK, 128)).T[0:8]
        bias[xq, t] = KAPPA * (y_raw[xq, t, pl.ds(BLK, 1), :] - square * (1.0 / D))
        hi, lo = split3(block * (2.0 * KAPPA / D))
        y3[xq, t, :, pl.ds(0, D)] = hi
        y3[xq, t, :, pl.ds(D, D)] = hi
        y3[xq, t, :, pl.ds(2 * D, D)] = lo

    def prep_mate(da, db):
        for ch in (0, 1):
            arrived(part(y_raw.at[slot(da, db, 1 - k)], ch), mate_recv.at[da * 4 + db, ch])
        prep_y(da, db, 1 - k)

    def pair(xq, zb):
        parts = []
        for n in (0, 1):
            t = tab_s[xq, zb, 64 * n]
            alive = t > 0
            t = lax.max(t - 1, 0)
            g = nt_dot(x3[zb], y3[xq, t])
            scores[xq, n, zb] = g
            shift = jnp.where(alive, bias[xq, t], LOWEST)[0:1]
            parts += [g[:, :128] + shift[:, :128], g[:, 128:] + shift[:, 128:]]
        old = top[zb]
        new = jnp.maximum(old, jnp.maximum(jnp.maximum(parts[0], parts[1]), jnp.maximum(parts[2], parts[3])))
        e = [jnp.exp2(v - new) for v in parts]
        total[zb] = total[zb] * jnp.exp2(old - new) + ((e[0] + e[1]) + (e[2] + e[3]))
        top[zb] = new

    for ch in (0, 1):
        send_y((0, 0), ch)
        send_z(0, ch, True)
        send_z(0, ch, False)
        send_mate((0, 0), ch)
    ids = lax.broadcasted_iota(jnp.int32, (N_COL, 128), 0)
    left = lax.broadcasted_iota(jnp.int32, (N_COL, 128), 1) < 64
    live = count_ref[0]

    def enter(i, carry):
        table, named = carry
        one = jnp.where(i < live, tgt_list[i] + 1, 0)
        two = jnp.where(i + 32 < live, tgt_list[i + 32] + 1, 0)
        here = ids == src_list[i]
        table = table + jnp.where(here, jnp.where(left, one, two), 0)
        named = named + jnp.where(here, jnp.where(i < live, 1, 0), 0)
        return table, named

    nothing = jnp.zeros((N_COL, 128), jnp.int32)
    table, named = lax.fori_loop(0, 32, enter, (nothing, nothing))
    mine[...] = jnp.minimum(table, N_ROW)
    bad = jnp.max(jnp.where(named > 1, 1.0, 0.0), axis=0, keepdims=True)
    top[...] = jnp.full(top.shape, LOWEST, jnp.float32)
    total[...] = jnp.zeros(total.shape, jnp.float32)

    keep = pltpu.make_async_copy(mine.at[pl.ds(x * NZ, NZ)], tabs.at[x], load_sem.at[0])
    keep.start()
    for n in (1, 2, 3):
        to = wrap4(x + n)
        start(remote(mine.at[pl.ds(to * NZ, NZ)], tabs.at[x], l_send.at[n - 1], l_recv.at[n - 1], device(y, k, to, z)))
    keep.wait()
    tab_copy = pltpu.make_async_copy(tabs, tab_s, load_sem.at[1])
    paired = 0
    for step in STEPS:
        kind = step[0]
        if kind == "y":
            pos, ch = step[1:3], step[3]
            recv_y(pos, ch)
            send_y(pos, ch)
            send_mate(pos, ch)
        elif kind == "z":
            n, ch = step[1:]
            recv_z(n, ch)
            if 0 < n < 4:
                send_z(n, ch, True)
            if -3 < n < 0:
                send_z(n, ch, False)
        elif kind == "X":
            prep_x(z_slot(step[1]))
            if step[1] == -1:
                for n in (1, 2, 3):
                    arrived(tabs.at[wrap4(x - n)], l_recv.at[n - 1])
                tab_copy.start()
        elif kind == "Y":
            prep_y(step[1], step[2], k)
        elif kind == "M":
            prep_mate(step[1], step[2])
        else:
            if not paired:
                tab_copy.wait()
            paired += 1
            pair(x, z_slot(step[1]))
            pair(x, z_slot(step[2]))

    def sides(i, carry):
        xq = wrap4(x + 1 + 2 * (i // 4))
        zb = 2 * lax.rem(i, 4)
        pair(xq, zb)
        pair(xq, zb + 1)
        return carry

    lax.fori_loop(0, 8, sides, 0)

    def row_copy(b, n):
        return remote(row_out.at[b], row_got.at[b, n - 1], row_send.at[b, n - 1], row_recv.at[b, n - 1],
                      device(y, k, x, lax.rem(z + n, NZ)))

    def close(b):
        high = jnp.max(top[b], axis=1, keepdims=True)
        whole = jnp.sum(total[b] * jnp.exp2(top[b] - high), axis=1, keepdims=True)
        logs = jnp.where(whole > 0.0, high + jnp.log2(whole), LOWEST)
        row_out[b, :, pl.ds(0, BLK)] = jnp.broadcast_to(logs, (BLK, 128)).T[0:1]
        row_out[b, :, pl.ds(BLK, 128)] = bad

    def far(i, carry):
        for b in (2 * i, 2 * i + 1):
            pair(wrap4(x + 2), b)
        for b in (2 * i, 2 * i + 1):
            close(b)
        for b in (2 * i, 2 * i + 1):
            for n in range(1, NZ):
                row_copy(b, n).start()
        return carry

    lax.fori_loop(0, NZ // 2, far, 0)

    def rows_of(b, bad):
        for n in range(1, NZ):
            arrived(row_got.at[b, n - 1], row_recv.at[b, n - 1])
        own = row_out[b, :, pl.ds(0, BLK)]
        others = [row_got[b, n, :, pl.ds(0, BLK)] for n in range(NZ - 1)]
        for n in range(NZ - 1):
            bad = jnp.maximum(bad, row_got[b, n, :, pl.ds(BLK, 128)])
        high = own
        for v in others:
            high = jnp.maximum(high, v)
        whole = jnp.exp2(own - high)
        for v in others:
            whole = whole + jnp.exp2(v - high)
        logs = high + jnp.log2(whole)
        row_logs[pl.ds(b, 1), :] = logs
        shift = LOG2E * x_raw[b, pl.ds(BLK, 1), :] - logs
        top[b] = jnp.broadcast_to(shift, (128, BLK)).T
        return bad

    def second(xq, zb):
        for n in (0, 1):
            for h in (0, 128):
                u = (scores[xq, n, zb, :, pl.ds(h, 128)] + top[zb]).reshape(BLK // 8, 8, 128)
                m = jnp.max(u, axis=0)
                col_top[xq, n, zb, :, pl.ds(h, 128)] = m
                col_sum[xq, n, zb, :, pl.ds(h, 128)] = jnp.sum(jnp.exp2(u - m[None]), axis=0)

    def early(b, bad):
        bad = rows_of(b, bad)

        def one(i, carry):
            second(2 * i, b)
            second(2 * i + 1, b)
            return carry

        lax.fori_loop(0, NX // 2, one, 0)
        return bad

    bad = lax.fori_loop(0, NZ - 2, early, bad)
    bad = rows_of(NZ - 1, rows_of(NZ - 2, bad))

    def columns(xq):
        m = col_top[xq].reshape(2 * NZ, 8, BLK)
        high = jnp.max(m, axis=1)
        whole = jnp.sum(col_sum[xq].reshape(2 * NZ, 8, BLK) * jnp.exp2(m - high[:, None, :]), axis=1)
        slots = high + jnp.log2(whole)
        named = tabs[xq]
        named = jnp.concatenate([jnp.broadcast_to(named[:, 0:1], (NZ, BLK)),
                                 jnp.broadcast_to(named[:, 64:65], (NZ, BLK))], axis=0)
        for t in range(N_ROW):
            v = jnp.where(named == t + 1, slots, LOWEST)
            high = jnp.max(v, axis=0, keepdims=True)
            whole = jnp.sum(jnp.exp2(v - high), axis=0, keepdims=True)
            col_out[xq, t, :, pl.ds(0, BLK)] = high + jnp.log2(whole)
            col_out[xq, t, :, pl.ds(BLK, 128)] = bad

    def col_copy(xq, t):
        return remote(col_out.at[xq, t], col_got.at[x, row], col_send.at[xq, t], col_recv.at[x, row],
                      {"row": t, "col": xq * NZ + z})

    for away in (2, 1, 3, 0):
        xq = wrap4(x + away)
        second(xq, NZ - 2)
        second(xq, NZ - 1)
        columns(xq)
        for n in range(N_ROW):
            if away or n:
                start(col_copy(xq, lax.rem(row + n, N_ROW)))
    f_square = x_raw[z, pl.ds(0, BLK), :]
    f_square = jnp.broadcast_to(jnp.sum(f_square * f_square, axis=1, keepdims=True), (BLK, 128)).T[0:1]
    g_square = y_raw[x, row, pl.ds(0, BLK), :]
    g_square = jnp.broadcast_to(jnp.sum(g_square * g_square, axis=1, keepdims=True), (BLK, 128)).T[0:1]
    f_out[...] = (ENTROPY * x_raw[z, pl.ds(BLK, 1), :] - (ENTROPY * LN2) * row_logs[pl.ds(z, 1), :]
                  + f_square * (1.0 / D))
    col_got[x, row] = col_out[x, row]
    for away in (2, 1, 3, 0):
        for n in range(N_ROW):
            if away or n:
                ox, orow = wrap4(x + away), lax.rem(row + n, N_ROW)
                arrived(col_got.at[ox, orow], col_recv.at[ox, orow])
    every = col_got[...].reshape(NX * N_ROW, 1, BLK + 128)
    high = jnp.max(every[:, :, :BLK], axis=0)
    whole = jnp.sum(jnp.exp2(every[:, :, :BLK] - high[None]), axis=0)
    g_out[...] = (ENTROPY * mass_b_ref[...] - (ENTROPY * LN2) * (high + jnp.log2(whole)) + g_square * (1.0 / D))
    bad_out[...] = jnp.max(every[:, :, BLK:], axis=0)

    def sent(b, carry):
        for n in range(1, NZ):
            row_copy(b, n).wait_send()
        return carry

    lax.fori_loop(0, NZ, sent, 0)
    for copy in pending:
        copy.wait_send()


def shape(*dims, kind=jnp.float32):
    return jax.ShapeDtypeStruct(dims, kind)


def general(sources, targets, g_pot, log_a, log_b, src_block, tgt_block, pair_count):
    whole = pl.BlockSpec(memory_space=pltpu.VMEM)
    anywhere = pl.BlockSpec(memory_space=pl.ANY)
    scalars = pl.BlockSpec(memory_space=pltpu.SMEM)
    dma = pltpu.SemaphoreType.DMA
    packed = jnp.zeros((8, 128), jnp.int32)
    packed = packed.at[0, :64].set(src_block).at[0, 64:].set(tgt_block).at[1, 0].set(pair_count[0])
    x_raw, y_raw, lists = pl.pallas_call(
        gather_kernel,
        out_shape=(shape(NZ, ROWS, D), shape(NX, N_ROW, ROWS, D), shape(NX, 8, 128, kind=jnp.int32)),
        in_specs=[anywhere] * 5,
        out_specs=(whole, whole, whole),
        scratch_shapes=[dma((5,)), dma((16, 2, 4)), dma((16, 2)), dma((16, 2)), dma((16, 2)),
                        dma((9, 2, 2)), dma((9, 2)), dma((3,)), dma((3,))],
        compiler_params=pltpu.CompilerParams(collective_id=3, has_side_effects=True, vmem_limit_bytes=VMEM_LIMIT),
    )(sources, targets, g_pot[None], log_a[None], packed)
    y_raw = y_raw.reshape(NX * N_ROW, ROWS, D)
    quarter = (lax.axis_index("col") // NZ).astype(jnp.int32).reshape(1)
    x3, y3, part = pl.pallas_call(
        first_kernel,
        out_shape=(shape(NZ, BLK, 3 * D, kind=jnp.bfloat16), shape(NX * N_ROW, 3 * D, BLK, kind=jnp.bfloat16),
                   shape(NZ, 8, BLK)),
        in_specs=[scalars, scalars, whole, whole],
        out_specs=(whole, whole, whole),
        scratch_shapes=[pltpu.VMEM((NX * N_ROW, 8, BLK), jnp.float32), pltpu.VMEM((NZ, BLK, 128), jnp.float32),
                        pltpu.VMEM((NZ, BLK, 128), jnp.float32)],
        compiler_params=pltpu.CompilerParams(vmem_limit_bytes=VMEM_LIMIT),
    )(lists, quarter, x_raw, y_raw)
    f_own, c_all = pl.pallas_call(
        row_exchange_kernel,
        out_shape=(shape(1, BLK), shape(NZ, 8, BLK)),
        in_specs=[whole, whole],
        out_specs=(whole, whole),
        scratch_shapes=[pltpu.VMEM((NZ - 1, NZ, 8, BLK), jnp.float32), dma((NZ - 1,)), dma((NZ - 1,))],
        compiler_params=pltpu.CompilerParams(collective_id=1, has_side_effects=True, vmem_limit_bytes=VMEM_LIMIT),
    )(part, x_raw)
    sums = pl.pallas_call(
        second_kernel,
        out_shape=shape(NX * N_ROW, 1, BLK),
        in_specs=[scalars, scalars, whole, whole, whole],
        out_specs=whole,
        scratch_shapes=[pltpu.VMEM((NZ, BLK, 128), jnp.float32), pltpu.VMEM((NX * N_ROW, 8, BLK), jnp.float32),
                        pltpu.VMEM((NX * N_ROW, 8, BLK), jnp.float32)],
        compiler_params=pltpu.CompilerParams(vmem_limit_bytes=VMEM_LIMIT),
    )(lists, quarter, x3, y3, c_all)
    g_own = pl.pallas_call(
        col_exchange_kernel,
        out_shape=shape(1, BLK),
        in_specs=[whole, whole, whole],
        out_specs=whole,
        scratch_shapes=[pltpu.VMEM((NX * N_ROW, 1, BLK), jnp.float32), dma((NX * N_ROW,)), dma((NX * N_ROW,))],
        compiler_params=pltpu.CompilerParams(collective_id=2, has_side_effects=True),
    )(sums, targets, log_b[None])
    return f_own.reshape(BLK), g_own.reshape(BLK)


def local(sources, targets, g_pot, log_a, log_b, src_block, tgt_block, pair_count):
    whole = pl.BlockSpec(memory_space=pltpu.VMEM)
    anywhere = pl.BlockSpec(memory_space=pl.ANY)
    scalars = pl.BlockSpec(memory_space=pltpu.SMEM)
    dma = pltpu.SemaphoreType.DMA
    vmem = pltpu.VMEM
    f32 = jnp.float32
    f_own, g_own, bad = pl.pallas_call(
        merged_kernel,
        out_shape=(shape(1, BLK), shape(1, BLK), shape(1, 128)),
        in_specs=[scalars] * 3 + [anywhere] * 4 + [whole],
        out_specs=(whole, whole, whole),
        scratch_shapes=[
            vmem((NX, N_ROW, ROWS, D), f32), vmem((NZ, ROWS, D), f32),
            vmem((NX, N_ROW, BLK, 3 * D), jnp.bfloat16), vmem((NZ, BLK, 3 * D), jnp.bfloat16),
            vmem((NX, N_ROW, 8, BLK), f32), vmem((NZ, BLK, 128), f32), vmem((NZ, BLK, 128), f32),
            vmem((NX, 2, NZ, BLK, BLK), f32), vmem((NX, 2, NZ, 8, BLK), f32), vmem((NX, 2, NZ, 8, BLK), f32),
            vmem((NX, NZ, 128), jnp.int32), pltpu.SMEM((NX, NZ, 128), jnp.int32), vmem((N_COL, 128), jnp.int32),
            vmem((NZ, 1, BLK + 128), f32), vmem((NZ, BLK), f32), vmem((NZ, NZ - 1, 1, BLK + 128), f32),
            vmem((NX, N_ROW, 1, BLK + 128), f32), vmem((NX, N_ROW, 1, BLK + 128), f32),
            dma((4,)), dma((16, 2, 4)), dma((16, 2)), dma((16, 2)), dma((16, 2)),
            dma((9, 2, 2)), dma((9, 2)), dma((3,)), dma((3,)),
            dma((NZ, NZ - 1)), dma((NZ, NZ - 1)), dma((NX, N_ROW)), dma((NX, N_ROW))],
        compiler_params=pltpu.CompilerParams(collective_id=0, has_side_effects=True, vmem_limit_bytes=VMEM_LIMIT),
    )(src_block, tgt_block, pair_count, sources, targets, g_pot[None], log_a[None], log_b[None])
    args = (sources, targets, g_pot, log_a, log_b, src_block, tgt_block, pair_count)
    return lax.cond(bad[0, 0] > 0.5, lambda: general(*args), lambda: (f_own.reshape(BLK), g_own.reshape(BLK)))


def solution(mesh):
    placed = (
        P(("row", "col"), None),
        P(("col", "row"), None),
        P(("col", "row")),
        P(("row", "col")),
        P(("col", "row")),
        P(("row", "col")),
        P(("row", "col")),
        P(("row", "col")),
    )
    return jax.shard_map(
        local,
        mesh=mesh,
        in_specs=placed,
        out_specs=(P(("row", "col")), P(("col", "row"))),
        check_vma=False,
    )
```

```python
import functools
import math

import jax
import jax.numpy as jnp
from jax import lax
from jax.experimental import pallas as pl
from jax.experimental.pallas import tpu as pltpu
from jax.sharding import PartitionSpec as P

MESH = pl.DeviceIdType.MESH
BLK = 256
D = 256
ROWS = 264
NX, NY, NZ = 4, 4, 8
N_ROW, N_COL = 8, 32
ENTROPY = 0.05
LOG2E = 1.0 / math.log(2.0)
LN2 = math.log(2.0)
KAPPA = LOG2E / ENTROPY
LOWEST = -1.0e30
CHUNKS = ((0, 128), (128, 136))
VMEM_LIMIT = 60 * 1024 * 1024


def place():
    r, c = lax.axis_index("row"), lax.axis_index("col")
    return r // 2, lax.rem(r, 2), c // NZ, lax.rem(c, NZ)


def device(y, core, x, z):
    return {"row": y * 2 + core, "col": x * NZ + z}


def signal(sem, where):
    pl.semaphore_signal(sem, inc=1, device_id=where, device_id_type=MESH)


FIRST = ((1, 0), (3, 0), (0, 1), (0, 3))
SECOND = ((2, 0), (1, 1), (1, 3), (3, 1), (3, 3), (0, 2))
THIRD = ((2, 1), (2, 3), (1, 2), (3, 2))
FOURTH = ((2, 2),)


def sends_of(da, db):
    out = []
    if db == 0:
        if da == 0:
            out += [("A+", (1, 0)), ("A-", (3, 0))]
        if da == 1:
            out += [("A+", (2, 0))]
        out += [("B+", (da, 1)), ("B-", (da, 3))]
    elif db == 1 and da in (0, 1):
        out += [("B+", (da, 2))]
    elif db == 3 and da in (2, 3):
        out += [("B-", (da, 2))]
    return out


REACHED = FIRST + SECOND + THIRD + FOURTH
OTHER_WAY = {"A+": "A-", "A-": "A+", "B+": "B+", "B-": "B-"}


def mirror(pos):
    return (4 - pos[0]) % 4, pos[1]


def chunk_sends(pos, ch):
    if ch == 0:
        return sends_of(*pos)
    return [(OTHER_WAY[name], mirror(target)) for name, target in sends_of(*mirror(pos))]


PARTS = ((0, 128), (128, 136))
STEPS = (
    ("X", 0), ("Y", 0, 0), ("M", 0, 0), ("y", 1, 0, 0), ("y", 0, 1, 0), ("z", 1, 0), ("y", 0, 3, 0), ("y", 3, 0, 0),
    ("z", -1, 0), ("y", 1, 0, 1), ("y", 0, 1, 1), ("z", 1, 1), ("y", 0, 3, 1), ("y", 3, 0, 1), ("z", -1, 1), ("X", 1),
    ("X", -1), ("Y", 1, 0), ("Y", 3, 0), ("Y", 0, 1), ("Y", 0, 3), ("M", 1, 0), ("M", 0, 1), ("M", 0, 3), ("z", 2, 0),
    ("y", 2, 0, 0), ("y", 1, 3, 0), ("y", 1, 1, 0), ("z", -2, 0), ("M", 3, 0), ("y", 2, 0, 1), ("Y", 2, 0),
    ("y", 3, 3, 0), ("y", 0, 2, 0), ("M", 2, 0), ("y", 3, 1, 0), ("z", -2, 1), ("z", 2, 1), ("X", 2), ("y", 1, 3, 1),
    ("X", -2), ("Y", 1, 3), ("y", 1, 1, 1), ("Y", 1, 1), ("y", 3, 3, 1), ("Y", 3, 3), ("M", 1, 3), ("z", -3, 0),
    ("z", 3, 0), ("M", 1, 1), ("y", 0, 2, 1), ("y", 2, 3, 0), ("Y", 0, 2), ("M", 3, 3), ("M", 0, 2), ("y", 2, 3, 1),
    ("y", 3, 1, 1), ("Y", 3, 1), ("Y", 2, 3), ("D", 0, 1), ("z", -3, 1), ("z", 3, 1), ("y", 3, 2, 0), ("y", 2, 1, 0),
    ("X", 3), ("X", -3), ("M", 2, 3), ("M", 3, 1), ("D", -1, 2), ("z", 4, 0), ("y", 1, 2, 0), ("y", 1, 2, 1),
    ("Y", 1, 2), ("D", -2, 3), ("y", 2, 2, 0), ("y", 2, 1, 1), ("Y", 2, 1), ("z", 4, 1), ("X", 4), ("D", -3, 4),
    ("M", 1, 2), ("y", 3, 2, 1), ("y", 2, 2, 1), ("Y", 3, 2), ("Y", 2, 2), ("M", 2, 1), ("M", 3, 2), ("M", 2, 2),
)


def gather_kernel(src_ref, tgt_ref, pot_ref, mass_ref, list_ref, x_out, y_out, lists_out,
                  load_sem, send_sem, recv_sem, mate_send, mate_recv, z_send, z_recv, l_send, l_recv):
    y, k, x, z = place()
    row = y * 2 + k

    def wrap4(v):
        return lax.rem(v + 8, 4)

    sigma = 1 - 2 * k

    def step_a(n):
        return wrap4(y + n * sigma * k), wrap4(x + n * sigma * (1 - k))

    def step_b(n):
        return wrap4(y + n * (1 - k)), wrap4(x + n * k)

    def dev_of(name):
        n = 1 if name[1] == "+" else -1
        ny, nx = step_a(n) if name[0] == "A" else step_b(n)
        return device(ny, k, nx, z)

    mate = device(y, 1 - k, x, z)
    z_long = device(y, k, x, lax.rem(z + sigma + NZ, NZ))
    z_short = device(y, k, x, lax.rem(z - sigma + NZ, NZ))

    def slot(da, db, core=None):
        if core is None:
            core = k
        oy = wrap4(y - db * (1 - core) + da * core)
        ox = wrap4(x - da * (1 - core) - db * core)
        return ox, oy * 2 + core

    loads = [
        pltpu.make_async_copy(tgt_ref, y_out.at[x, row, pl.ds(0, BLK)], load_sem.at[0]),
        pltpu.make_async_copy(pot_ref, y_out.at[x, row, pl.ds(BLK, 1)], load_sem.at[1]),
        pltpu.make_async_copy(src_ref, x_out.at[z, pl.ds(0, BLK)], load_sem.at[2]),
        pltpu.make_async_copy(mass_ref, x_out.at[z, pl.ds(BLK, 1)], load_sem.at[3]),
        pltpu.make_async_copy(list_ref, lists_out.at[x], load_sem.at[4]),
    ]
    for copy in loads:
        copy.start()
    barrier = pltpu.get_barrier_semaphore()
    peers = [device(y, k, wrap4(x + 1), z), device(y, k, wrap4(x + 3), z), device(y, k, wrap4(x + 2), z),
             device(wrap4(y + 1), k, x, z), device(wrap4(y + 3), k, x, z), mate, z_long, z_short]
    for peer in peers:
        signal(barrier, peer)
    pl.semaphore_wait(barrier, len(peers))
    for copy in loads:
        copy.wait()

    pending = []

    def at(pos):
        return pos[0] * 4 + pos[1]

    def part(ref, ch):
        return ref.at[pl.ds(*CHUNKS[ch])]

    def y_copy(pos, ch, where, target, n):
        ox, orow = slot(*pos)
        return pltpu.make_async_remote_copy(
            src_ref=part(y_out.at[ox, orow], ch), dst_ref=part(y_out.at[ox, orow], ch),
            send_sem=send_sem.at[at(pos), ch, n], recv_sem=recv_sem.at[at(target), ch],
            device_id=where, device_id_type=MESH)

    def mate_copy(pos, ch):
        ox, orow = slot(*pos)
        return pltpu.make_async_remote_copy(
            src_ref=part(y_out.at[ox, orow], ch), dst_ref=part(y_out.at[ox, orow], ch),
            send_sem=mate_send.at[at(pos), ch], recv_sem=mate_recv.at[at(pos), ch],
            device_id=mate, device_id_type=MESH)

    def send_y(pos, ch):
        for n, (name, target) in enumerate(sends_of(*pos)):
            copy = y_copy(pos, ch, dev_of(name), target, n)
            copy.start()
            pending.append(copy)
        copy = mate_copy(pos, ch)
        copy.start()
        pending.append(copy)

    def recv_y(pos, ch):
        ox, orow = slot(*pos)
        ref = part(y_out.at[ox, orow], ch)
        pltpu.make_async_remote_copy(src_ref=ref, dst_ref=ref, send_sem=send_sem.at[0, 0, 0],
                                     recv_sem=recv_sem.at[at(pos), ch], device_id=mate,
                                     device_id_type=MESH).wait_recv()

    def recv_mate(pos, ch):
        ox, orow = slot(*pos, core=1 - k)
        ref = part(y_out.at[ox, orow], ch)
        pltpu.make_async_remote_copy(src_ref=ref, dst_ref=ref, send_sem=send_sem.at[0, 0, 0],
                                     recv_sem=mate_recv.at[at(pos), ch], device_id=mate,
                                     device_id_type=MESH).wait_recv()

    def z_slot(n):
        return lax.rem(z - n * sigma + NZ * 4, NZ)

    def send_z(n, ch, long):
        target = n + 1 if long else n - 1
        ref = part(x_out.at[z_slot(n)], ch)
        copy = pltpu.make_async_remote_copy(
            src_ref=ref, dst_ref=ref, send_sem=z_send.at[n + 4, ch, 0 if long else 1],
            recv_sem=z_recv.at[target + 4, ch],
            device_id=z_long if long else z_short, device_id_type=MESH)
        copy.start()
        pending.append(copy)

    def recv_z(n, ch):
        ref = part(x_out.at[z_slot(n)], ch)
        pltpu.make_async_remote_copy(src_ref=ref, dst_ref=ref, send_sem=send_sem.at[0, 0, 0],
                                     recv_sem=z_recv.at[n + 4, ch], device_id=mate,
                                     device_id_type=MESH).wait_recv()

    for n in (1, 2, 3):
        copy = pltpu.make_async_remote_copy(
            src_ref=lists_out.at[x], dst_ref=lists_out.at[x], send_sem=l_send.at[n - 1], recv_sem=l_recv.at[n - 1],
            device_id=device(y, k, wrap4(x + n), z), device_id_type=MESH)
        copy.start()
        pending.append(copy)
    for ch in (0, 1):
        send_y((0, 0), ch)
        send_z(0, ch, True)
        send_z(0, ch, False)
    levels = (FIRST, SECOND, THIRD, FOURTH)
    for level in range(4):
        for ch in (0, 1):
            for pos in levels[level]:
                recv_y(pos, ch)
                send_y(pos, ch)
            n = level + 1
            recv_z(n, ch)
            if n < 4:
                send_z(n, ch, True)
                recv_z(-n, ch)
                if n < 3:
                    send_z(-n, ch, False)
    for n in (1, 2, 3):
        ref = lists_out.at[wrap4(x - n)]
        pltpu.make_async_remote_copy(src_ref=ref, dst_ref=ref, send_sem=l_send.at[0], recv_sem=l_recv.at[n - 1],
                                     device_id=mate, device_id_type=MESH).wait_recv()
    for ch in (0, 1):
        for da in range(4):
            for db in range(4):
                recv_mate((da, db), ch)
    for copy in pending:
        copy.wait_send()


def split3(v):
    hi = v.astype(jnp.bfloat16)
    lo = (v - hi.astype(jnp.float32)).astype(jnp.bfloat16)
    return hi, lo


def prep_kernel_body(x_raw, y_raw, x3, y3, bias):
    def one_x(i, carry):
        hi, lo = split3(x_raw[i, pl.ds(0, BLK), :])
        x3[i, :, pl.ds(0, D)] = hi
        x3[i, :, pl.ds(D, D)] = lo
        x3[i, :, pl.ds(2 * D, D)] = hi
        return carry

    lax.fori_loop(0, NZ, one_x, 0)

    def one_y(i, carry):
        block = y_raw[i, pl.ds(0, BLK), :].T
        pot = y_raw[i, pl.ds(BLK, 1), :]
        square = jnp.sum(block * block, axis=0, keepdims=True)
        row = KAPPA * (pot - square * (1.0 / D))
        bias[i] = jnp.broadcast_to(row, (8, BLK))
        hi, lo = split3(block * (2.0 * KAPPA / D))
        y3[i, pl.ds(0, D), :] = hi
        y3[i, pl.ds(D, D), :] = hi
        y3[i, pl.ds(2 * D, D), :] = lo
        return carry

    lax.fori_loop(0, NX * N_ROW, one_y, 0)


def pairs_of(lists, quarter, body):
    for other in range(NX):
        def one(i, carry, other=other):
            src = lists[other, 0, i]

            @pl.when(src // NZ == quarter)
            def _():
                body(lax.rem(src, NZ), other * N_ROW + lists[other, 0, 64 + i])
            return carry

        lax.fori_loop(0, lists[other, 1, 0], one, 0)


def first_kernel(lists, quarter, x_raw, y_raw, x3, y3, part_out, bias, top, total):
    prep_kernel_body(x_raw, y_raw, x3, y3, bias)
    top[...] = jnp.full(top.shape, LOWEST, jnp.float32)
    total[...] = jnp.zeros(total.shape, jnp.float32)

    def pair(b, t):
        g = jnp.dot(x3[b], y3[t], preferred_element_type=jnp.float32)
        row = bias[t]
        s1 = g[:, :128] + row[0:1, :128]
        s2 = g[:, 128:] + row[0:1, 128:]
        old = top[b]
        new = jnp.maximum(old, jnp.maximum(s1, s2))
        total[b] = total[b] * jnp.exp2(old - new) + jnp.exp2(s1 - new) + jnp.exp2(s2 - new)
        top[b] = new

    pairs_of(lists, quarter[0], pair)

    def close(b, carry):
        high = jnp.max(top[b], axis=1, keepdims=True)
        whole = jnp.sum(total[b] * jnp.exp2(top[b] - high), axis=1, keepdims=True)
        logs = jnp.where(whole > 0.0, high + jnp.log2(whole), LOWEST)
        part_out[b] = jnp.broadcast_to(logs, (BLK, 128)).T[0:8, :]
        return carry

    lax.fori_loop(0, NZ, close, 0)


def row_exchange_kernel(part_ref, x_raw, f_out, c_out, got, send_sem, recv_sem):
    y, k, x, z = place()
    barrier = pltpu.get_barrier_semaphore()
    for n in range(1, NZ):
        signal(barrier, device(y, k, x, lax.rem(z + n, NZ)))
    pl.semaphore_wait(barrier, NZ - 1)
    copies = []
    for n in range(1, NZ):
        copy = pltpu.make_async_remote_copy(
            src_ref=part_ref, dst_ref=got.at[n - 1], send_sem=send_sem.at[n - 1], recv_sem=recv_sem.at[n - 1],
            device_id=device(y, k, x, lax.rem(z + n, NZ)), device_id_type=MESH)
        copy.start()
        copies.append(copy)
    for copy in copies:
        copy.wait()
    own = part_ref[...]
    others = [got[n] for n in range(NZ - 1)]
    top = own
    for v in others:
        top = jnp.maximum(top, v)
    total = jnp.exp2(own - top)
    for v in others:
        total = total + jnp.exp2(v - top)
    logs = top + jnp.log2(total)
    c_out[...] = LOG2E * x_raw[:, pl.ds(BLK, 1), :] - logs
    square = x_raw[z, pl.ds(0, BLK), :].T
    square = jnp.sum(square * square, axis=0, keepdims=True)
    mass = x_raw[z, pl.ds(BLK, 1), :]
    c_here = c_out[z]
    f_out[...] = ENTROPY * mass - (ENTROPY * LN2) * (LOG2E * mass - c_here[0:1, :]) + square * (1.0 / D)


def second_kernel(lists, quarter, x3, y3, c_ref, part_out, cols, top, total):
    top[...] = jnp.full(top.shape, LOWEST, jnp.float32)
    total[...] = jnp.zeros(total.shape, jnp.float32)

    def widen(b, carry):
        cols[b] = jnp.broadcast_to(c_ref[b, pl.ds(0, 1), :], (128, BLK)).T
        return carry

    lax.fori_loop(0, NZ, widen, 0)

    def pair(b, t):
        g = jnp.dot(x3[b], y3[t], preferred_element_type=jnp.float32)
        col = cols[b]
        u = g + jnp.concatenate([col, col], axis=1)
        u = u.reshape(BLK // 8, 8, BLK)
        old = top[t]
        new = jnp.maximum(old, jnp.max(u, axis=0))
        total[t] = total[t] * jnp.exp2(old - new) + jnp.sum(jnp.exp2(u - new[None]), axis=0)
        top[t] = new

    pairs_of(lists, quarter[0], pair)

    def close(t, carry):
        high = jnp.max(top[t], axis=0, keepdims=True)
        whole = jnp.sum(total[t] * jnp.exp2(top[t] - high), axis=0, keepdims=True)
        part_out[t] = jnp.where(whole > 0.0, high + jnp.log2(whole), LOWEST)
        return carry

    lax.fori_loop(0, NX * N_ROW, close, 0)


def col_exchange_kernel(part_ref, tgt_ref, mass_ref, g_out, got, send_sem, recv_sem):
    y, k, x, z = place()
    me = x * N_ROW + y * 2 + k
    many = NX * N_ROW
    barrier = pltpu.get_barrier_semaphore()

    def peer(n):
        other = lax.rem(me + n, many)
        return other, {"row": lax.rem(other, N_ROW), "col": (other // N_ROW) * NZ + z}

    for n in range(1, many):
        signal(barrier, peer(n)[1])
    pl.semaphore_wait(barrier, many - 1)
    copies = []
    for n in range(1, many):
        other, where = peer(n)
        copy = pltpu.make_async_remote_copy(
            src_ref=part_ref.at[other], dst_ref=got.at[n], send_sem=send_sem.at[n], recv_sem=recv_sem.at[n],
            device_id=where, device_id_type=MESH)
        copy.start()
        copies.append(copy)
    block = tgt_ref[...].T
    square = jnp.sum(block * block, axis=0, keepdims=True)
    for copy in copies:
        copy.wait()
    got[0] = part_ref[me]
    every = got[...]
    top = jnp.max(every, axis=0)
    total = jnp.sum(jnp.exp2(every - top[None]), axis=0)
    logs = top + jnp.log2(total)
    g_out[...] = ENTROPY * mass_ref[...] - (ENTROPY * LN2) * logs + square * (1.0 / D)

def nt_dot(a, b):
    return lax.dot_general(a, b, (((1,), (1,)), ((), ())), preferred_element_type=jnp.float32)


def merged_kernel(src_in, tgt_in, count_in, src_ref, tgt_ref, pot_ref, mass_ref, mass_b_in,
                  f_out, g_out, bad_out,
                  y_raw, x_raw, y3, x3, bias, top, total, scores, col_top, col_sum, tabs, tab_s, mine, src_list, tgt_list, count_ref, mass_b_ref, row_out, row_logs, row_got,
                  col_out, col_got,
                  load_sem, send_sem, recv_sem, mate_send, mate_recv, z_send, z_recv, l_send, l_recv,
                  row_send, row_recv, col_send, col_recv):
    y, k, x, z = place()
    row = y * 2 + k
    sigma = 1 - 2 * k

    def wrap4(v):
        return lax.rem(v + 8, 4)

    def step_a(n):
        return wrap4(y + n * sigma * k), wrap4(x + n * sigma * (1 - k))

    def step_b(n):
        return wrap4(y + n * (1 - k)), wrap4(x + n * k)

    def dev_of(name):
        n = 1 if name[1] == "+" else -1
        ny, nx = step_a(n) if name[0] == "A" else step_b(n)
        return device(ny, k, nx, z)

    mate = device(y, 1 - k, x, z)
    z_long = device(y, k, x, lax.rem(z + sigma + NZ, NZ))
    z_short = device(y, k, x, lax.rem(z - sigma + NZ, NZ))

    def slot(da, db, core):
        oy = wrap4(y - db * (1 - core) + da * core)
        ox = wrap4(x - da * (1 - core) - db * core)
        return ox, oy * 2 + core

    loads = [
        pltpu.make_async_copy(tgt_ref, y_raw.at[x, row, pl.ds(0, BLK)], load_sem.at[0]),
        pltpu.make_async_copy(pot_ref, y_raw.at[x, row, pl.ds(BLK, 1)], load_sem.at[1]),
        pltpu.make_async_copy(src_ref, x_raw.at[z, pl.ds(0, BLK)], load_sem.at[2]),
        pltpu.make_async_copy(mass_ref, x_raw.at[z, pl.ds(BLK, 1)], load_sem.at[3]),
    ]
    small = [
        pltpu.make_async_copy(src_in, src_list, load_sem.at[4]),
        pltpu.make_async_copy(tgt_in, tgt_list, load_sem.at[5]),
        pltpu.make_async_copy(count_in, count_ref, load_sem.at[6]),
        pltpu.make_async_copy(mass_b_in, mass_b_ref, load_sem.at[7]),
    ]
    for copy in loads + small:
        copy.start()
    barrier = pltpu.get_barrier_semaphore()
    peers = [device(y, k, wrap4(x + 1), z), device(y, k, wrap4(x + 3), z), device(y, k, wrap4(x + 2), z),
             device(wrap4(y + 1), k, x, z), device(wrap4(y + 3), k, x, z), mate, z_long, z_short]
    for peer in peers:
        signal(barrier, peer)

    pl.semaphore_wait(barrier, len(peers))
    for copy in loads:
        copy.wait()

    pending = []

    def at(pos):
        return pos[0] * 4 + pos[1]

    def part(ref, ch):
        return ref.at[pl.ds(*PARTS[ch])]

    def remote(src, dst, send, recv, where):
        return pltpu.make_async_remote_copy(src_ref=src, dst_ref=dst, send_sem=send, recv_sem=recv,
                                            device_id=where, device_id_type=MESH)

    def start(copy):
        copy.start()
        pending.append(copy)

    def arrived(ref, sem):
        remote(ref, ref, send_sem.at[0, 0, 0], sem, mate).wait_recv()

    def send_y(pos, ch):
        ref = part(y_raw.at[slot(*pos, k)], ch)
        for n, (name, target) in enumerate(chunk_sends(pos, ch)):
            start(remote(ref, ref, send_sem.at[at(pos), ch, n], recv_sem.at[at(target), ch], dev_of(name)))

    def send_mate(pos, ch):
        ref = part(y_raw.at[slot(*pos, k)], ch)
        start(remote(ref, ref, mate_send.at[at(pos), ch], mate_recv.at[at(pos), ch], mate))

    def recv_y(pos, ch):
        arrived(part(y_raw.at[slot(*pos, k)], ch), recv_sem.at[at(pos), ch])

    def z_slot(n):
        return lax.rem(z - n * sigma + NZ * 4, NZ)

    def send_z(n, ch, long):
        target = n + 1 if long else n - 1
        ref = part(x_raw.at[z_slot(n)], ch)
        start(remote(ref, ref, z_send.at[n + 4, ch, 0 if long else 1], z_recv.at[target + 4, ch],
                     z_long if long else z_short))

    def recv_z(n, ch):
        arrived(part(x_raw.at[z_slot(n)], ch), z_recv.at[n + 4, ch])

    def prep_x(zb):
        hi, lo = split3(x_raw[zb, pl.ds(0, BLK), :])
        x3[zb, :, pl.ds(0, D)] = hi
        x3[zb, :, pl.ds(D, D)] = lo
        x3[zb, :, pl.ds(2 * D, D)] = hi

    def prep_y(da, db, core):
        xq, t = slot(da, db, core)
        block = y_raw[xq, t, pl.ds(0, BLK), :]
        square = jnp.sum(block * block, axis=1, keepdims=True)
        square = jnp.broadcast_to(square, (BLK, 128)).T[0:8]
        bias[xq, t] = KAPPA * (y_raw[xq, t, pl.ds(BLK, 1), :] - square * (1.0 / D))
        hi, lo = split3(block * (2.0 * KAPPA / D))
        y3[xq, t, :, pl.ds(0, D)] = hi
        y3[xq, t, :, pl.ds(D, D)] = hi
        y3[xq, t, :, pl.ds(2 * D, D)] = lo

    def prep_mate(da, db):
        for ch in (0, 1):
            arrived(part(y_raw.at[slot(da, db, 1 - k)], ch), mate_recv.at[da * 4 + db, ch])
        prep_y(da, db, 1 - k)

    def pair(xq, zb):
        parts = []
        for n in (0, 1):
            t = tab_s[xq, zb, 64 * n]
            alive = t > 0
            t = lax.max(t - 1, 0)
            g = nt_dot(x3[zb], y3[xq, t])
            scores[xq, n, zb] = g
            shift = jnp.where(alive, bias[xq, t], LOWEST)[0:1]
            parts += [g[:, :128] + shift[:, :128], g[:, 128:] + shift[:, 128:]]
        old = top[zb]
        new = jnp.maximum(old, jnp.maximum(jnp.maximum(parts[0], parts[1]), jnp.maximum(parts[2], parts[3])))
        e = [jnp.exp2(v - new) for v in parts]
        total[zb] = total[zb] * jnp.exp2(old - new) + ((e[0] + e[1]) + (e[2] + e[3]))
        top[zb] = new

    for ch in (0, 1):
        send_y((0, 0), ch)
        send_z(0, ch, True)
        send_z(0, ch, False)
        send_mate((0, 0), ch)
    for copy in small:
        copy.wait()
    ids = lax.broadcasted_iota(jnp.int32, (N_COL, 128), 0)
    left = lax.broadcasted_iota(jnp.int32, (N_COL, 128), 1) < 64
    live = count_ref[0]

    def enter(i, carry):
        table, named = carry
        one = jnp.where(i < live, tgt_list[i] + 1, 0)
        two = jnp.where(i + 32 < live, tgt_list[i + 32] + 1, 0)
        here = ids == src_list[i]
        table = table + jnp.where(here, jnp.where(left, one, two), 0)
        named = named + jnp.where(here, jnp.where(i < live, 1, 0), 0)
        return table, named

    nothing = jnp.zeros((N_COL, 128), jnp.int32)
    table, named = lax.fori_loop(0, 32, enter, (nothing, nothing))
    mine[...] = jnp.minimum(table, N_ROW)
    bad = jnp.max(jnp.where(named > 1, 1.0, 0.0), axis=0, keepdims=True)
    top[...] = jnp.full(top.shape, LOWEST, jnp.float32)
    total[...] = jnp.zeros(total.shape, jnp.float32)

    keep = pltpu.make_async_copy(mine.at[pl.ds(x * NZ, NZ)], tabs.at[x], load_sem.at[0])
    keep.start()
    for n in (1, 2, 3):
        to = wrap4(x + n)
        start(remote(mine.at[pl.ds(to * NZ, NZ)], tabs.at[x], l_send.at[n - 1], l_recv.at[n - 1], device(y, k, to, z)))
    keep.wait()
    tab_copy = pltpu.make_async_copy(tabs, tab_s, load_sem.at[1])
    paired = 0
    for step in STEPS:
        kind = step[0]
        if kind == "y":
            pos, ch = step[1:3], step[3]
            recv_y(pos, ch)
            send_y(pos, ch)
            send_mate(pos, ch)
        elif kind == "z":
            n, ch = step[1:]
            recv_z(n, ch)
            if 0 < n < 4:
                send_z(n, ch, True)
            if -3 < n < 0:
                send_z(n, ch, False)
        elif kind == "X":
            prep_x(z_slot(step[1]))
            if step[1] == -1:
                for n in (1, 2, 3):
                    arrived(tabs.at[wrap4(x - n)], l_recv.at[n - 1])
                tab_copy.start()
        elif kind == "Y":
            prep_y(step[1], step[2], k)
        elif kind == "M":
            prep_mate(step[1], step[2])
        else:
            if not paired:
                tab_copy.wait()
            paired += 1
            pair(x, z_slot(step[1]))
            pair(x, z_slot(step[2]))

    def row_copy(b, n):
        return remote(row_out.at[b], row_got.at[b, n - 1], row_send.at[b, n - 1], row_recv.at[b, n - 1],
                      device(y, k, x, lax.rem(z + n, NZ)))

    def close(b):
        high = jnp.max(top[b], axis=1, keepdims=True)
        whole = jnp.sum(total[b] * jnp.exp2(top[b] - high), axis=1, keepdims=True)
        logs = jnp.where(whole > 0.0, high + jnp.log2(whole), LOWEST)
        row_out[b, :, pl.ds(0, BLK)] = jnp.broadcast_to(logs, (BLK, 128)).T[0:1]
        row_out[b, :, pl.ds(BLK, 128)] = bad

    def far(i, carry):
        for away in (1, 3, 2):
            for b in (2 * i, 2 * i + 1):
                pair(wrap4(x + away), b)
        for b in (2 * i, 2 * i + 1):
            close(b)
        for b in (2 * i, 2 * i + 1):
            for n in range(1, NZ):
                row_copy(b, n).start()
        return carry

    lax.fori_loop(0, NZ // 2, far, 0)

    def rows_of(b, bad):
        for n in range(1, NZ):
            arrived(row_got.at[b, n - 1], row_recv.at[b, n - 1])
        own = row_out[b, :, pl.ds(0, BLK)]
        others = [row_got[b, n, :, pl.ds(0, BLK)] for n in range(NZ - 1)]
        for n in range(NZ - 1):
            bad = jnp.maximum(bad, row_got[b, n, :, pl.ds(BLK, 128)])
        high = own
        for v in others:
            high = jnp.maximum(high, v)
        whole = jnp.exp2(own - high)
        for v in others:
            whole = whole + jnp.exp2(v - high)
        logs = high + jnp.log2(whole)
        row_logs[pl.ds(b, 1), :] = logs
        shift = LOG2E * x_raw[b, pl.ds(BLK, 1), :] - logs
        top[b] = jnp.broadcast_to(shift, (128, BLK)).T
        return bad

    def second(xq, zb):
        for n in (0, 1):
            for h in (0, 128):
                u = (scores[xq, n, zb, :, pl.ds(h, 128)] + top[zb]).reshape(BLK // 8, 8, 128)
                m = jnp.max(u, axis=0)
                col_top[xq, n, zb, :, pl.ds(h, 128)] = m
                col_sum[xq, n, zb, :, pl.ds(h, 128)] = jnp.sum(jnp.exp2(u - m[None]), axis=0)

    def early(b, bad):
        bad = rows_of(b, bad)

        def one(i, carry):
            second(2 * i, b)
            second(2 * i + 1, b)
            return carry

        lax.fori_loop(0, NX // 2, one, 0)
        return bad

    bad = lax.fori_loop(0, NZ - 2, early, bad)
    bad = rows_of(NZ - 1, rows_of(NZ - 2, bad))

    def columns(xq):
        m = col_top[xq].reshape(2 * NZ, 8, BLK)
        high = jnp.max(m, axis=1)
        whole = jnp.sum(col_sum[xq].reshape(2 * NZ, 8, BLK) * jnp.exp2(m - high[:, None, :]), axis=1)
        slots = high + jnp.log2(whole)
        named = tabs[xq]
        named = jnp.concatenate([jnp.broadcast_to(named[:, 0:1], (NZ, BLK)),
                                 jnp.broadcast_to(named[:, 64:65], (NZ, BLK))], axis=0)
        for t in range(N_ROW):
            v = jnp.where(named == t + 1, slots, LOWEST)
            high = jnp.max(v, axis=0, keepdims=True)
            whole = jnp.sum(jnp.exp2(v - high), axis=0, keepdims=True)
            col_out[xq, t, :, pl.ds(0, BLK)] = high + jnp.log2(whole)
            col_out[xq, t, :, pl.ds(BLK, 128)] = bad

    def col_copy(xq, t):
        return remote(col_out.at[xq, t], col_got.at[x, row], col_send.at[xq, t], col_recv.at[x, row],
                      {"row": t, "col": xq * NZ + z})

    for away in (2, 1, 3, 0):
        xq = wrap4(x + away)
        second(xq, NZ - 2)
        second(xq, NZ - 1)
        columns(xq)
        for n in range(N_ROW):
            if away or n:
                start(col_copy(xq, lax.rem(row + n, N_ROW)))
    f_square = x_raw[z, pl.ds(0, BLK), :]
    f_square = jnp.broadcast_to(jnp.sum(f_square * f_square, axis=1, keepdims=True), (BLK, 128)).T[0:1]
    g_square = y_raw[x, row, pl.ds(0, BLK), :]
    g_square = jnp.broadcast_to(jnp.sum(g_square * g_square, axis=1, keepdims=True), (BLK, 128)).T[0:1]
    f_out[...] = (ENTROPY * x_raw[z, pl.ds(BLK, 1), :] - (ENTROPY * LN2) * row_logs[pl.ds(z, 1), :]
                  + f_square * (1.0 / D))
    col_got[x, row] = col_out[x, row]
    for away in (2, 1, 3, 0):
        for n in range(N_ROW):
            if away or n:
                ox, orow = wrap4(x + away), lax.rem(row + n, N_ROW)
                arrived(col_got.at[ox, orow], col_recv.at[ox, orow])
    every = col_got[...].reshape(NX * N_ROW, 1, BLK + 128)
    high = jnp.max(every[:, :, :BLK], axis=0)
    whole = jnp.sum(jnp.exp2(every[:, :, :BLK] - high[None]), axis=0)
    g_out[...] = (ENTROPY * mass_b_ref[...] - (ENTROPY * LN2) * (high + jnp.log2(whole)) + g_square * (1.0 / D))
    bad_out[...] = jnp.max(every[:, :, BLK:], axis=0)

    def sent(b, carry):
        for n in range(1, NZ):
            row_copy(b, n).wait_send()
        return carry

    lax.fori_loop(0, NZ, sent, 0)
    for copy in pending:
        copy.wait_send()


def shape(*dims, kind=jnp.float32):
    return jax.ShapeDtypeStruct(dims, kind)


def general(sources, targets, g_pot, log_a, log_b, src_block, tgt_block, pair_count):
    whole = pl.BlockSpec(memory_space=pltpu.VMEM)
    anywhere = pl.BlockSpec(memory_space=pl.ANY)
    scalars = pl.BlockSpec(memory_space=pltpu.SMEM)
    dma = pltpu.SemaphoreType.DMA
    packed = jnp.zeros((8, 128), jnp.int32)
    packed = packed.at[0, :64].set(src_block).at[0, 64:].set(tgt_block).at[1, 0].set(pair_count[0])
    x_raw, y_raw, lists = pl.pallas_call(
        gather_kernel,
        out_shape=(shape(NZ, ROWS, D), shape(NX, N_ROW, ROWS, D), shape(NX, 8, 128, kind=jnp.int32)),
        in_specs=[anywhere] * 5,
        out_specs=(whole, whole, whole),
        scratch_shapes=[dma((5,)), dma((16, 2, 4)), dma((16, 2)), dma((16, 2)), dma((16, 2)),
                        dma((9, 2, 2)), dma((9, 2)), dma((3,)), dma((3,))],
        compiler_params=pltpu.CompilerParams(collective_id=3, has_side_effects=True, vmem_limit_bytes=VMEM_LIMIT),
    )(sources, targets, g_pot[None], log_a[None], packed)
    y_raw = y_raw.reshape(NX * N_ROW, ROWS, D)
    quarter = (lax.axis_index("col") // NZ).astype(jnp.int32).reshape(1)
    x3, y3, part = pl.pallas_call(
        first_kernel,
        out_shape=(shape(NZ, BLK, 3 * D, kind=jnp.bfloat16), shape(NX * N_ROW, 3 * D, BLK, kind=jnp.bfloat16),
                   shape(NZ, 8, BLK)),
        in_specs=[scalars, scalars, whole, whole],
        out_specs=(whole, whole, whole),
        scratch_shapes=[pltpu.VMEM((NX * N_ROW, 8, BLK), jnp.float32), pltpu.VMEM((NZ, BLK, 128), jnp.float32),
                        pltpu.VMEM((NZ, BLK, 128), jnp.float32)],
        compiler_params=pltpu.CompilerParams(vmem_limit_bytes=VMEM_LIMIT),
    )(lists, quarter, x_raw, y_raw)
    f_own, c_all = pl.pallas_call(
        row_exchange_kernel,
        out_shape=(shape(1, BLK), shape(NZ, 8, BLK)),
        in_specs=[whole, whole],
        out_specs=(whole, whole),
        scratch_shapes=[pltpu.VMEM((NZ - 1, NZ, 8, BLK), jnp.float32), dma((NZ - 1,)), dma((NZ - 1,))],
        compiler_params=pltpu.CompilerParams(collective_id=1, has_side_effects=True, vmem_limit_bytes=VMEM_LIMIT),
    )(part, x_raw)
    sums = pl.pallas_call(
        second_kernel,
        out_shape=shape(NX * N_ROW, 1, BLK),
        in_specs=[scalars, scalars, whole, whole, whole],
        out_specs=whole,
        scratch_shapes=[pltpu.VMEM((NZ, BLK, 128), jnp.float32), pltpu.VMEM((NX * N_ROW, 8, BLK), jnp.float32),
                        pltpu.VMEM((NX * N_ROW, 8, BLK), jnp.float32)],
        compiler_params=pltpu.CompilerParams(vmem_limit_bytes=VMEM_LIMIT),
    )(lists, quarter, x3, y3, c_all)
    g_own = pl.pallas_call(
        col_exchange_kernel,
        out_shape=shape(1, BLK),
        in_specs=[whole, whole, whole],
        out_specs=whole,
        scratch_shapes=[pltpu.VMEM((NX * N_ROW, 1, BLK), jnp.float32), dma((NX * N_ROW,)), dma((NX * N_ROW,))],
        compiler_params=pltpu.CompilerParams(collective_id=2, has_side_effects=True),
    )(sums, targets, log_b[None])
    return f_own.reshape(BLK), g_own.reshape(BLK)


def local(sources, targets, g_pot, log_a, log_b, src_block, tgt_block, pair_count):
    whole = pl.BlockSpec(memory_space=pltpu.VMEM)
    anywhere = pl.BlockSpec(memory_space=pl.ANY)
    dma = pltpu.SemaphoreType.DMA
    vmem = pltpu.VMEM
    f32 = jnp.float32
    f_own, g_own, bad = pl.pallas_call(
        merged_kernel,
        out_shape=(shape(1, BLK), shape(1, BLK), shape(1, 128)),
        in_specs=[anywhere] * 8,
        out_specs=(whole, whole, whole),
        scratch_shapes=[
            vmem((NX, N_ROW, ROWS, D), f32), vmem((NZ, ROWS, D), f32),
            vmem((NX, N_ROW, BLK, 3 * D), jnp.bfloat16), vmem((NZ, BLK, 3 * D), jnp.bfloat16),
            vmem((NX, N_ROW, 8, BLK), f32), vmem((NZ, BLK, 128), f32), vmem((NZ, BLK, 128), f32),
            vmem((NX, 2, NZ, BLK, BLK), f32), vmem((NX, 2, NZ, 8, BLK), f32), vmem((NX, 2, NZ, 8, BLK), f32),
            vmem((NX, NZ, 128), jnp.int32), pltpu.SMEM((NX, NZ, 128), jnp.int32), vmem((N_COL, 128), jnp.int32),
            pltpu.SMEM((64,), jnp.int32), pltpu.SMEM((64,), jnp.int32), pltpu.SMEM((1,), jnp.int32), vmem((1, BLK), f32),
            vmem((NZ, 1, BLK + 128), f32), vmem((NZ, BLK), f32), vmem((NZ, NZ - 1, 1, BLK + 128), f32),
            vmem((NX, N_ROW, 1, BLK + 128), f32), vmem((NX, N_ROW, 1, BLK + 128), f32),
            dma((8,)), dma((16, 2, 4)), dma((16, 2)), dma((16, 2)), dma((16, 2)),
            dma((9, 2, 2)), dma((9, 2)), dma((3,)), dma((3,)),
            dma((NZ, NZ - 1)), dma((NZ, NZ - 1)), dma((NX, N_ROW)), dma((NX, N_ROW))],
        compiler_params=pltpu.CompilerParams(collective_id=0, has_side_effects=True, vmem_limit_bytes=VMEM_LIMIT),
    )(src_block, tgt_block, pair_count, sources, targets, g_pot[None], log_a[None], log_b[None])
    args = (sources, targets, g_pot, log_a, log_b, src_block, tgt_block, pair_count)
    return lax.cond(bad[0, 0] > 0.5, lambda: general(*args), lambda: (f_own.reshape(BLK), g_own.reshape(BLK)))


def solution(mesh):
    placed = (
        P(("row", "col"), None),
        P(("col", "row"), None),
        P(("col", "row")),
        P(("row", "col")),
        P(("col", "row")),
        P(("row", "col")),
        P(("row", "col")),
        P(("row", "col")),
    )
    return jax.shard_map(
        local,
        mesh=mesh,
        in_specs=placed,
        out_specs=(P(("row", "col")), P(("col", "row"))),
        check_vma=False,
    )
```

```python
import functools
import math

import jax
import jax.numpy as jnp
from jax import lax
from jax.experimental import pallas as pl
from jax.experimental.pallas import tpu as pltpu
from jax.sharding import PartitionSpec as P

MESH = pl.DeviceIdType.MESH
BLK = 256
D = 256
ROWS = 264
NX, NY, NZ = 4, 4, 8
N_ROW, N_COL = 8, 32
ENTROPY = 0.05
LOG2E = 1.0 / math.log(2.0)
LN2 = math.log(2.0)
KAPPA = LOG2E / ENTROPY
LOWEST = -1.0e30
CHUNKS = ((0, 128), (128, 136))
VMEM_LIMIT = 60 * 1024 * 1024


def place():
    r, c = lax.axis_index("row"), lax.axis_index("col")
    return r // 2, lax.rem(r, 2), c // NZ, lax.rem(c, NZ)


def device(y, core, x, z):
    return {"row": y * 2 + core, "col": x * NZ + z}


def signal(sem, where):
    pl.semaphore_signal(sem, inc=1, device_id=where, device_id_type=MESH)


FIRST = ((1, 0), (3, 0), (0, 1), (0, 3))
SECOND = ((2, 0), (1, 1), (1, 3), (3, 1), (3, 3), (0, 2))
THIRD = ((2, 1), (2, 3), (1, 2), (3, 2))
FOURTH = ((2, 2),)


def sends_of(da, db):
    out = []
    if db == 0:
        if da == 0:
            out += [("A+", (1, 0)), ("A-", (3, 0))]
        if da == 1:
            out += [("A+", (2, 0))]
        out += [("B+", (da, 1)), ("B-", (da, 3))]
    elif db == 1 and da in (0, 1):
        out += [("B+", (da, 2))]
    elif db == 3 and da in (2, 3):
        out += [("B-", (da, 2))]
    return out


REACHED = FIRST + SECOND + THIRD + FOURTH
OTHER_WAY = {"A+": "A-", "A-": "A+", "B+": "B+", "B-": "B-"}


def mirror(pos):
    return (4 - pos[0]) % 4, pos[1]


def chunk_sends(pos, ch):
    if ch == 0:
        return sends_of(*pos)
    return [(OTHER_WAY[name], mirror(target)) for name, target in sends_of(*mirror(pos))]


PARTS = ((0, 160), (160, 104))
STEPS = (
    ("X", 0), ("Y", 0, 0), ("M", 0, 0), ("y", 1, 0, 0), ("y", 0, 1, 0), ("z", 1, 0), ("y", 0, 3, 0), ("y", 3, 0, 0),
    ("z", -1, 0), ("y", 1, 0, 1), ("y", 0, 1, 1), ("z", 1, 1), ("y", 0, 3, 1), ("y", 3, 0, 1), ("z", -1, 1), ("X", 1),
    ("X", -1), ("Y", 1, 0), ("Y", 3, 0), ("Y", 0, 1), ("Y", 0, 3), ("M", 1, 0), ("M", 0, 1), ("M", 0, 3), ("z", 2, 0),
    ("y", 2, 0, 0), ("y", 1, 3, 0), ("y", 1, 1, 0), ("z", -2, 0), ("M", 3, 0), ("y", 2, 0, 1), ("Y", 2, 0),
    ("y", 3, 3, 0), ("y", 0, 2, 0), ("M", 2, 0), ("y", 3, 1, 0), ("z", -2, 1), ("z", 2, 1), ("X", 2), ("y", 1, 3, 1),
    ("X", -2), ("Y", 1, 3), ("y", 1, 1, 1), ("Y", 1, 1), ("y", 3, 3, 1), ("Y", 3, 3), ("M", 1, 3), ("z", -3, 0),
    ("z", 3, 0), ("M", 1, 1), ("y", 0, 2, 1), ("y", 2, 3, 0), ("Y", 0, 2), ("M", 3, 3), ("M", 0, 2), ("y", 2, 3, 1),
    ("y", 3, 1, 1), ("Y", 3, 1), ("Y", 2, 3), ("D", 0, 1), ("z", -3, 1), ("z", 3, 1), ("y", 3, 2, 0), ("y", 2, 1, 0),
    ("X", 3), ("X", -3), ("M", 2, 3), ("M", 3, 1), ("D", -1, 2), ("z", 4, 0), ("y", 1, 2, 0), ("y", 1, 2, 1),
    ("Y", 1, 2), ("D", -2, 3), ("y", 2, 2, 0), ("y", 2, 1, 1), ("Y", 2, 1), ("z", 4, 1), ("X", 4), ("D", -3, 4),
    ("M", 1, 2), ("y", 3, 2, 1), ("y", 2, 2, 1), ("Y", 3, 2), ("Y", 2, 2), ("M", 2, 1), ("M", 3, 2), ("M", 2, 2),
)


def gather_kernel(src_ref, tgt_ref, pot_ref, mass_ref, list_ref, x_out, y_out, lists_out,
                  load_sem, send_sem, recv_sem, mate_send, mate_recv, z_send, z_recv, l_send, l_recv):
    y, k, x, z = place()
    row = y * 2 + k

    def wrap4(v):
        return lax.rem(v + 8, 4)

    sigma = 1 - 2 * k

    def step_a(n):
        return wrap4(y + n * sigma * k), wrap4(x + n * sigma * (1 - k))

    def step_b(n):
        return wrap4(y + n * (1 - k)), wrap4(x + n * k)

    def dev_of(name):
        n = 1 if name[1] == "+" else -1
        ny, nx = step_a(n) if name[0] == "A" else step_b(n)
        return device(ny, k, nx, z)

    mate = device(y, 1 - k, x, z)
    z_long = device(y, k, x, lax.rem(z + sigma + NZ, NZ))
    z_short = device(y, k, x, lax.rem(z - sigma + NZ, NZ))

    def slot(da, db, core=None):
        if core is None:
            core = k
        oy = wrap4(y - db * (1 - core) + da * core)
        ox = wrap4(x - da * (1 - core) - db * core)
        return ox, oy * 2 + core

    loads = [
        pltpu.make_async_copy(tgt_ref, y_out.at[x, row, pl.ds(0, BLK)], load_sem.at[0]),
        pltpu.make_async_copy(pot_ref, y_out.at[x, row, pl.ds(BLK, 1)], load_sem.at[1]),
        pltpu.make_async_copy(src_ref, x_out.at[z, pl.ds(0, BLK)], load_sem.at[2]),
        pltpu.make_async_copy(mass_ref, x_out.at[z, pl.ds(BLK, 1)], load_sem.at[3]),
        pltpu.make_async_copy(list_ref, lists_out.at[x], load_sem.at[4]),
    ]
    for copy in loads:
        copy.start()
    barrier = pltpu.get_barrier_semaphore()
    peers = [device(y, k, wrap4(x + 1), z), device(y, k, wrap4(x + 3), z), device(y, k, wrap4(x + 2), z),
             device(wrap4(y + 1), k, x, z), device(wrap4(y + 3), k, x, z), mate, z_long, z_short]
    for peer in peers:
        signal(barrier, peer)
    pl.semaphore_wait(barrier, len(peers))
    for copy in loads:
        copy.wait()

    pending = []

    def at(pos):
        return pos[0] * 4 + pos[1]

    def part(ref, ch):
        return ref.at[pl.ds(*CHUNKS[ch])]

    def y_copy(pos, ch, where, target, n):
        ox, orow = slot(*pos)
        return pltpu.make_async_remote_copy(
            src_ref=part(y_out.at[ox, orow], ch), dst_ref=part(y_out.at[ox, orow], ch),
            send_sem=send_sem.at[at(pos), ch, n], recv_sem=recv_sem.at[at(target), ch],
            device_id=where, device_id_type=MESH)

    def mate_copy(pos, ch):
        ox, orow = slot(*pos)
        return pltpu.make_async_remote_copy(
            src_ref=part(y_out.at[ox, orow], ch), dst_ref=part(y_out.at[ox, orow], ch),
            send_sem=mate_send.at[at(pos), ch], recv_sem=mate_recv.at[at(pos), ch],
            device_id=mate, device_id_type=MESH)

    def send_y(pos, ch):
        for n, (name, target) in enumerate(sends_of(*pos)):
            copy = y_copy(pos, ch, dev_of(name), target, n)
            copy.start()
            pending.append(copy)
        copy = mate_copy(pos, ch)
        copy.start()
        pending.append(copy)

    def recv_y(pos, ch):
        ox, orow = slot(*pos)
        ref = part(y_out.at[ox, orow], ch)
        pltpu.make_async_remote_copy(src_ref=ref, dst_ref=ref, send_sem=send_sem.at[0, 0, 0],
                                     recv_sem=recv_sem.at[at(pos), ch], device_id=mate,
                                     device_id_type=MESH).wait_recv()

    def recv_mate(pos, ch):
        ox, orow = slot(*pos, core=1 - k)
        ref = part(y_out.at[ox, orow], ch)
        pltpu.make_async_remote_copy(src_ref=ref, dst_ref=ref, send_sem=send_sem.at[0, 0, 0],
                                     recv_sem=mate_recv.at[at(pos), ch], device_id=mate,
                                     device_id_type=MESH).wait_recv()

    def z_slot(n):
        return lax.rem(z - n * sigma + NZ * 4, NZ)

    def send_z(n, ch, long):
        target = n + 1 if long else n - 1
        ref = part(x_out.at[z_slot(n)], ch)
        copy = pltpu.make_async_remote_copy(
            src_ref=ref, dst_ref=ref, send_sem=z_send.at[n + 4, ch, 0 if long else 1],
            recv_sem=z_recv.at[target + 4, ch],
            device_id=z_long if long else z_short, device_id_type=MESH)
        copy.start()
        pending.append(copy)

    def recv_z(n, ch):
        ref = part(x_out.at[z_slot(n)], ch)
        pltpu.make_async_remote_copy(src_ref=ref, dst_ref=ref, send_sem=send_sem.at[0, 0, 0],
                                     recv_sem=z_recv.at[n + 4, ch], device_id=mate,
                                     device_id_type=MESH).wait_recv()

    for n in (1, 2, 3):
        copy = pltpu.make_async_remote_copy(
            src_ref=lists_out.at[x], dst_ref=lists_out.at[x], send_sem=l_send.at[n - 1], recv_sem=l_recv.at[n - 1],
            device_id=device(y, k, wrap4(x + n), z), device_id_type=MESH)
        copy.start()
        pending.append(copy)
    for ch in (0, 1):
        send_y((0, 0), ch)
        send_z(0, ch, True)
        send_z(0, ch, False)
    levels = (FIRST, SECOND, THIRD, FOURTH)
    for level in range(4):
        for ch in (0, 1):
            for pos in levels[level]:
                recv_y(pos, ch)
                send_y(pos, ch)
            n = level + 1
            recv_z(n, ch)
            if n < 4:
                send_z(n, ch, True)
                recv_z(-n, ch)
                if n < 3:
                    send_z(-n, ch, False)
    for n in (1, 2, 3):
        ref = lists_out.at[wrap4(x - n)]
        pltpu.make_async_remote_copy(src_ref=ref, dst_ref=ref, send_sem=l_send.at[0], recv_sem=l_recv.at[n - 1],
                                     device_id=mate, device_id_type=MESH).wait_recv()
    for ch in (0, 1):
        for da in range(4):
            for db in range(4):
                recv_mate((da, db), ch)
    for copy in pending:
        copy.wait_send()


def split3(v):
    hi = v.astype(jnp.bfloat16)
    lo = (v - hi.astype(jnp.float32)).astype(jnp.bfloat16)
    return hi, lo


def prep_kernel_body(x_raw, y_raw, x3, y3, bias):
    def one_x(i, carry):
        hi, lo = split3(x_raw[i, pl.ds(0, BLK), :])
        x3[i, :, pl.ds(0, D)] = hi
        x3[i, :, pl.ds(D, D)] = lo
        x3[i, :, pl.ds(2 * D, D)] = hi
        return carry

    lax.fori_loop(0, NZ, one_x, 0)

    def one_y(i, carry):
        block = y_raw[i, pl.ds(0, BLK), :].T
        pot = y_raw[i, pl.ds(BLK, 1), :]
        square = jnp.sum(block * block, axis=0, keepdims=True)
        row = KAPPA * (pot - square * (1.0 / D))
        bias[i] = jnp.broadcast_to(row, (8, BLK))
        hi, lo = split3(block * (2.0 * KAPPA / D))
        y3[i, pl.ds(0, D), :] = hi
        y3[i, pl.ds(D, D), :] = hi
        y3[i, pl.ds(2 * D, D), :] = lo
        return carry

    lax.fori_loop(0, NX * N_ROW, one_y, 0)


def pairs_of(lists, quarter, body):
    for other in range(NX):
        def one(i, carry, other=other):
            src = lists[other, 0, i]

            @pl.when(src // NZ == quarter)
            def _():
                body(lax.rem(src, NZ), other * N_ROW + lists[other, 0, 64 + i])
            return carry

        lax.fori_loop(0, lists[other, 1, 0], one, 0)


def first_kernel(lists, quarter, x_raw, y_raw, x3, y3, part_out, bias, top, total):
    prep_kernel_body(x_raw, y_raw, x3, y3, bias)
    top[...] = jnp.full(top.shape, LOWEST, jnp.float32)
    total[...] = jnp.zeros(total.shape, jnp.float32)

    def pair(b, t):
        g = jnp.dot(x3[b], y3[t], preferred_element_type=jnp.float32)
        row = bias[t]
        s1 = g[:, :128] + row[0:1, :128]
        s2 = g[:, 128:] + row[0:1, 128:]
        old = top[b]
        new = jnp.maximum(old, jnp.maximum(s1, s2))
        total[b] = total[b] * jnp.exp2(old - new) + jnp.exp2(s1 - new) + jnp.exp2(s2 - new)
        top[b] = new

    pairs_of(lists, quarter[0], pair)

    def close(b, carry):
        high = jnp.max(top[b], axis=1, keepdims=True)
        whole = jnp.sum(total[b] * jnp.exp2(top[b] - high), axis=1, keepdims=True)
        logs = jnp.where(whole > 0.0, high + jnp.log2(whole), LOWEST)
        part_out[b] = jnp.broadcast_to(logs, (BLK, 128)).T[0:8, :]
        return carry

    lax.fori_loop(0, NZ, close, 0)


def row_exchange_kernel(part_ref, x_raw, f_out, c_out, got, send_sem, recv_sem):
    y, k, x, z = place()
    barrier = pltpu.get_barrier_semaphore()
    for n in range(1, NZ):
        signal(barrier, device(y, k, x, lax.rem(z + n, NZ)))
    pl.semaphore_wait(barrier, NZ - 1)
    copies = []
    for n in range(1, NZ):
        copy = pltpu.make_async_remote_copy(
            src_ref=part_ref, dst_ref=got.at[n - 1], send_sem=send_sem.at[n - 1], recv_sem=recv_sem.at[n - 1],
            device_id=device(y, k, x, lax.rem(z + n, NZ)), device_id_type=MESH)
        copy.start()
        copies.append(copy)
    for copy in copies:
        copy.wait()
    own = part_ref[...]
    others = [got[n] for n in range(NZ - 1)]
    top = own
    for v in others:
        top = jnp.maximum(top, v)
    total = jnp.exp2(own - top)
    for v in others:
        total = total + jnp.exp2(v - top)
    logs = top + jnp.log2(total)
    c_out[...] = LOG2E * x_raw[:, pl.ds(BLK, 1), :] - logs
    square = x_raw[z, pl.ds(0, BLK), :].T
    square = jnp.sum(square * square, axis=0, keepdims=True)
    mass = x_raw[z, pl.ds(BLK, 1), :]
    c_here = c_out[z]
    f_out[...] = ENTROPY * mass - (ENTROPY * LN2) * (LOG2E * mass - c_here[0:1, :]) + square * (1.0 / D)


def second_kernel(lists, quarter, x3, y3, c_ref, part_out, cols, top, total):
    top[...] = jnp.full(top.shape, LOWEST, jnp.float32)
    total[...] = jnp.zeros(total.shape, jnp.float32)

    def widen(b, carry):
        cols[b] = jnp.broadcast_to(c_ref[b, pl.ds(0, 1), :], (128, BLK)).T
        return carry

    lax.fori_loop(0, NZ, widen, 0)

    def pair(b, t):
        g = jnp.dot(x3[b], y3[t], preferred_element_type=jnp.float32)
        col = cols[b]
        u = g + jnp.concatenate([col, col], axis=1)
        u = u.reshape(BLK // 8, 8, BLK)
        old = top[t]
        new = jnp.maximum(old, jnp.max(u, axis=0))
        total[t] = total[t] * jnp.exp2(old - new) + jnp.sum(jnp.exp2(u - new[None]), axis=0)
        top[t] = new

    pairs_of(lists, quarter[0], pair)

    def close(t, carry):
        high = jnp.max(top[t], axis=0, keepdims=True)
        whole = jnp.sum(total[t] * jnp.exp2(top[t] - high), axis=0, keepdims=True)
        part_out[t] = jnp.where(whole > 0.0, high + jnp.log2(whole), LOWEST)
        return carry

    lax.fori_loop(0, NX * N_ROW, close, 0)


def col_exchange_kernel(part_ref, tgt_ref, mass_ref, g_out, got, send_sem, recv_sem):
    y, k, x, z = place()
    me = x * N_ROW + y * 2 + k
    many = NX * N_ROW
    barrier = pltpu.get_barrier_semaphore()

    def peer(n):
        other = lax.rem(me + n, many)
        return other, {"row": lax.rem(other, N_ROW), "col": (other // N_ROW) * NZ + z}

    for n in range(1, many):
        signal(barrier, peer(n)[1])
    pl.semaphore_wait(barrier, many - 1)
    copies = []
    for n in range(1, many):
        other, where = peer(n)
        copy = pltpu.make_async_remote_copy(
            src_ref=part_ref.at[other], dst_ref=got.at[n], send_sem=send_sem.at[n], recv_sem=recv_sem.at[n],
            device_id=where, device_id_type=MESH)
        copy.start()
        copies.append(copy)
    block = tgt_ref[...].T
    square = jnp.sum(block * block, axis=0, keepdims=True)
    for copy in copies:
        copy.wait()
    got[0] = part_ref[me]
    every = got[...]
    top = jnp.max(every, axis=0)
    total = jnp.sum(jnp.exp2(every - top[None]), axis=0)
    logs = top + jnp.log2(total)
    g_out[...] = ENTROPY * mass_ref[...] - (ENTROPY * LN2) * logs + square * (1.0 / D)

def nt_dot(a, b):
    return lax.dot_general(a, b, (((1,), (1,)), ((), ())), preferred_element_type=jnp.float32)


def merged_kernel(src_in, tgt_in, count_in, src_ref, tgt_ref, pot_ref, mass_ref, mass_b_in,
                  both_out, bad_out,
                  y_raw, x_raw, y3, x3, bias, top, total, scores, col_top, col_sum, tabs, tab_s, mine, src_list, tgt_list, count_ref, mass_b_ref, row_out, row_logs, row_got,
                  col_out, col_got,
                  load_sem, send_sem, recv_sem, mate_send, mate_recv, z_send, z_recv, l_send, l_recv,
                  row_send, row_recv, col_send, col_recv):
    y, k, x, z = place()
    row = y * 2 + k
    sigma = 1 - 2 * k

    def wrap4(v):
        return lax.rem(v + 8, 4)

    def step_a(n):
        return wrap4(y + n * sigma * k), wrap4(x + n * sigma * (1 - k))

    def step_b(n):
        return wrap4(y + n * (1 - k)), wrap4(x + n * k)

    def dev_of(name):
        n = 1 if name[1] == "+" else -1
        ny, nx = step_a(n) if name[0] == "A" else step_b(n)
        return device(ny, k, nx, z)

    mate = device(y, 1 - k, x, z)
    z_long = device(y, k, x, lax.rem(z + sigma + NZ, NZ))
    z_short = device(y, k, x, lax.rem(z - sigma + NZ, NZ))

    def slot(da, db, core):
        oy = wrap4(y - db * (1 - core) + da * core)
        ox = wrap4(x - da * (1 - core) - db * core)
        return ox, oy * 2 + core

    loads = [
        pltpu.make_async_copy(tgt_ref, y_raw.at[x, row, pl.ds(0, BLK)], load_sem.at[0]),
        pltpu.make_async_copy(pot_ref, y_raw.at[x, row, pl.ds(BLK, 1)], load_sem.at[1]),
        pltpu.make_async_copy(src_ref, x_raw.at[z, pl.ds(0, BLK)], load_sem.at[2]),
        pltpu.make_async_copy(mass_ref, x_raw.at[z, pl.ds(BLK, 1)], load_sem.at[3]),
    ]
    small = [
        pltpu.make_async_copy(src_in, src_list, load_sem.at[4]),
        pltpu.make_async_copy(tgt_in, tgt_list, load_sem.at[5]),
        pltpu.make_async_copy(count_in, count_ref, load_sem.at[6]),
        pltpu.make_async_copy(mass_b_in, mass_b_ref, load_sem.at[7]),
    ]
    for copy in loads + small:
        copy.start()
    barrier = pltpu.get_barrier_semaphore()
    peers = [device(y, k, wrap4(x + 1), z), device(y, k, wrap4(x + 3), z), device(y, k, wrap4(x + 2), z),
             device(wrap4(y + 1), k, x, z), device(wrap4(y + 3), k, x, z), mate, z_long, z_short]
    for peer in peers:
        signal(barrier, peer)

    pl.semaphore_wait(barrier, len(peers))
    for copy in loads:
        copy.wait()

    pending = []

    def at(pos):
        return pos[0] * 4 + pos[1]

    def part(ref, ch):
        return ref.at[pl.ds(*PARTS[ch])]

    def remote(src, dst, send, recv, where):
        return pltpu.make_async_remote_copy(src_ref=src, dst_ref=dst, send_sem=send, recv_sem=recv,
                                            device_id=where, device_id_type=MESH)

    def start(copy):
        copy.start()
        pending.append(copy)

    def arrived(ref, sem):
        remote(ref, ref, send_sem.at[0, 0, 0], sem, mate).wait_recv()

    def send_y(pos, ch):
        ref = part(y_raw.at[slot(*pos, k)], ch)
        for n, (name, target) in enumerate(chunk_sends(pos, ch)):
            start(remote(ref, ref, send_sem.at[at(pos), ch, n], recv_sem.at[at(target), ch], dev_of(name)))

    def send_mate(pos, ch):
        ref = part(y_raw.at[slot(*pos, k)], ch)
        start(remote(ref, ref, mate_send.at[at(pos), ch], mate_recv.at[at(pos), ch], mate))

    def recv_y(pos, ch):
        arrived(part(y_raw.at[slot(*pos, k)], ch), recv_sem.at[at(pos), ch])

    def z_slot(n):
        return lax.rem(z - n * sigma + NZ * 4, NZ)

    def send_z(n, ch, long):
        target = n + 1 if long else n - 1
        ref = part(x_raw.at[z_slot(n)], ch)
        start(remote(ref, ref, z_send.at[n + 4, ch, 0 if long else 1], z_recv.at[target + 4, ch],
                     z_long if long else z_short))

    def recv_z(n, ch):
        arrived(part(x_raw.at[z_slot(n)], ch), z_recv.at[n + 4, ch])

    def prep_x(zb):
        hi, lo = split3(x_raw[zb, pl.ds(0, BLK), :])
        x3[zb, :, pl.ds(0, D)] = hi
        x3[zb, :, pl.ds(D, D)] = lo
        x3[zb, :, pl.ds(2 * D, D)] = hi

    def prep_y(da, db, core):
        xq, t = slot(da, db, core)
        block = y_raw[xq, t, pl.ds(0, BLK), :]
        square = jnp.sum(block * block, axis=1, keepdims=True)
        square = jnp.broadcast_to(square, (BLK, 128)).T[0:8]
        bias[xq, t] = KAPPA * (y_raw[xq, t, pl.ds(BLK, 1), :] - square * (1.0 / D))
        hi, lo = split3(block * (2.0 * KAPPA / D))
        y3[xq, t, :, pl.ds(0, D)] = hi
        y3[xq, t, :, pl.ds(D, D)] = hi
        y3[xq, t, :, pl.ds(2 * D, D)] = lo

    def prep_mate(da, db):
        for ch in (0, 1):
            arrived(part(y_raw.at[slot(da, db, 1 - k)], ch), mate_recv.at[da * 4 + db, ch])
        prep_y(da, db, 1 - k)

    def pair(xq, zb):
        parts = []
        for n in (0, 1):
            t = tab_s[xq, zb, 64 * n]
            alive = t > 0
            t = lax.max(t - 1, 0)
            g = nt_dot(x3[zb], y3[xq, t])
            scores[xq, n, zb] = g
            shift = jnp.where(alive, bias[xq, t], LOWEST)[0:1]
            parts += [g[:, :128] + shift[:, :128], g[:, 128:] + shift[:, 128:]]
        old = top[zb]
        new = jnp.maximum(old, jnp.maximum(jnp.maximum(parts[0], parts[1]), jnp.maximum(parts[2], parts[3])))
        e = [jnp.exp2(v - new) for v in parts]
        total[zb] = total[zb] * jnp.exp2(old - new) + ((e[0] + e[1]) + (e[2] + e[3]))
        top[zb] = new

    for ch in (0, 1):
        send_y((0, 0), ch)
        send_z(0, ch, True)
        send_z(0, ch, False)
        send_mate((0, 0), ch)
    for copy in small:
        copy.wait()
    ids = lax.broadcasted_iota(jnp.int32, (N_COL, 128), 0)
    left = lax.broadcasted_iota(jnp.int32, (N_COL, 128), 1) < 64
    live = count_ref[0]

    def enter(i, carry):
        table, named = carry
        one = jnp.where(i < live, tgt_list[i] + 1, 0)
        two = jnp.where(i + 32 < live, tgt_list[i + 32] + 1, 0)
        here = ids == src_list[i]
        table = table + jnp.where(here, jnp.where(left, one, two), 0)
        named = named + jnp.where(here, jnp.where(i < live, 1, 0), 0)
        return table, named

    nothing = jnp.zeros((N_COL, 128), jnp.int32)
    table, named = lax.fori_loop(0, 32, enter, (nothing, nothing))
    mine[...] = jnp.minimum(table, N_ROW)
    bad = jnp.max(jnp.where(named > 1, 1.0, 0.0), axis=0, keepdims=True)
    top[...] = jnp.full(top.shape, LOWEST, jnp.float32)
    total[...] = jnp.zeros(total.shape, jnp.float32)

    keep = pltpu.make_async_copy(mine.at[pl.ds(x * NZ, NZ)], tabs.at[x], load_sem.at[0])
    keep.start()
    for n in (1, 2, 3):
        to = wrap4(x + n)
        start(remote(mine.at[pl.ds(to * NZ, NZ)], tabs.at[x], l_send.at[n - 1], l_recv.at[n - 1], device(y, k, to, z)))
    keep.wait()
    tab_copy = pltpu.make_async_copy(tabs, tab_s, load_sem.at[1])
    paired = 0
    for step in STEPS:
        kind = step[0]
        if kind == "y":
            pos, ch = step[1:3], step[3]
            recv_y(pos, ch)
            send_y(pos, ch)
            send_mate(pos, ch)
        elif kind == "z":
            n, ch = step[1:]
            recv_z(n, ch)
            if 0 < n < 4:
                send_z(n, ch, True)
            if -3 < n < 0:
                send_z(n, ch, False)
        elif kind == "X":
            prep_x(z_slot(step[1]))
            if step[1] == -1:
                for n in (1, 2, 3):
                    arrived(tabs.at[wrap4(x - n)], l_recv.at[n - 1])
                tab_copy.start()
        elif kind == "Y":
            prep_y(step[1], step[2], k)
        elif kind == "M":
            prep_mate(step[1], step[2])
        else:
            if not paired:
                tab_copy.wait()
            paired += 1
            pair(x, z_slot(step[1]))
            pair(x, z_slot(step[2]))

    def row_copy(b, n):
        return remote(row_out.at[b], row_got.at[b, n - 1], row_send.at[b, n - 1], row_recv.at[b, n - 1],
                      device(y, k, x, lax.rem(z + n, NZ)))

    def close(b):
        high = jnp.max(top[b], axis=1, keepdims=True)
        whole = jnp.sum(total[b] * jnp.exp2(top[b] - high), axis=1, keepdims=True)
        logs = jnp.where(whole > 0.0, high + jnp.log2(whole), LOWEST)
        row_out[b, :, pl.ds(0, BLK)] = jnp.broadcast_to(logs, (BLK, 128)).T[0:1]
        row_out[b, :, pl.ds(BLK, 128)] = bad

    def far(i, carry):
        for away in (1, 3, 2):
            for b in (2 * i, 2 * i + 1):
                pair(wrap4(x + away), b)
        for b in (2 * i, 2 * i + 1):
            close(b)
        for b in (2 * i, 2 * i + 1):
            for n in range(1, NZ):
                row_copy(b, n).start()
        return carry

    lax.fori_loop(0, NZ // 2, far, 0)

    def rows_of(b, bad):
        for n in range(1, NZ):
            arrived(row_got.at[b, n - 1], row_recv.at[b, n - 1])
        own = row_out[b, :, pl.ds(0, BLK)]
        others = [row_got[b, n, :, pl.ds(0, BLK)] for n in range(NZ - 1)]
        for n in range(NZ - 1):
            bad = jnp.maximum(bad, row_got[b, n, :, pl.ds(BLK, 128)])
        high = own
        for v in others:
            high = jnp.maximum(high, v)
        whole = jnp.exp2(own - high)
        for v in others:
            whole = whole + jnp.exp2(v - high)
        logs = high + jnp.log2(whole)
        row_logs[pl.ds(b, 1), :] = logs
        shift = LOG2E * x_raw[b, pl.ds(BLK, 1), :] - logs
        top[b] = jnp.broadcast_to(shift, (128, BLK)).T
        return bad

    def second(xq, zb):
        for n in (0, 1):
            for h in (0, 128):
                u = (scores[xq, n, zb, :, pl.ds(h, 128)] + top[zb]).reshape(BLK // 8, 8, 128)
                m = jnp.max(u, axis=0)
                col_top[xq, n, zb, :, pl.ds(h, 128)] = m
                col_sum[xq, n, zb, :, pl.ds(h, 128)] = jnp.sum(jnp.exp2(u - m[None]), axis=0)

    def early(b, bad):
        bad = rows_of(b, bad)

        def one(i, carry):
            second(2 * i, b)
            second(2 * i + 1, b)
            return carry

        lax.fori_loop(0, NX // 2, one, 0)
        return bad

    bad = lax.fori_loop(0, NZ - 2, early, bad)
    bad = rows_of(NZ - 1, rows_of(NZ - 2, bad))

    def columns(xq):
        m = col_top[xq].reshape(2 * NZ, 8, BLK)
        high = jnp.max(m, axis=1)
        whole = jnp.sum(col_sum[xq].reshape(2 * NZ, 8, BLK) * jnp.exp2(m - high[:, None, :]), axis=1)
        slots = high + jnp.log2(whole)
        named = tabs[xq]
        named = jnp.concatenate([jnp.broadcast_to(named[:, 0:1], (NZ, BLK)),
                                 jnp.broadcast_to(named[:, 64:65], (NZ, BLK))], axis=0)
        for t in range(N_ROW):
            v = jnp.where(named == t + 1, slots, LOWEST)
            high = jnp.max(v, axis=0, keepdims=True)
            whole = jnp.sum(jnp.exp2(v - high), axis=0, keepdims=True)
            col_out[xq, t, :, pl.ds(0, BLK)] = high + jnp.log2(whole)
            col_out[xq, t, :, pl.ds(BLK, 128)] = bad

    def col_copy(xq, t):
        return remote(col_out.at[xq, t], col_got.at[x, row], col_send.at[xq, t], col_recv.at[x, row],
                      {"row": t, "col": xq * NZ + z})

    for away in (2, 1, 3, 0):
        xq = wrap4(x + away)
        second(xq, NZ - 2)
        second(xq, NZ - 1)
        columns(xq)
        for n in range(N_ROW):
            if away or n:
                start(col_copy(xq, lax.rem(row + n, N_ROW)))
    f_square = x_raw[z, pl.ds(0, BLK), :]
    f_square = jnp.broadcast_to(jnp.sum(f_square * f_square, axis=1, keepdims=True), (BLK, 128)).T[0:1]
    g_square = y_raw[x, row, pl.ds(0, BLK), :]
    g_square = jnp.broadcast_to(jnp.sum(g_square * g_square, axis=1, keepdims=True), (BLK, 128)).T[0:1]
    both_out[pl.ds(0, 1), :] = (ENTROPY * x_raw[z, pl.ds(BLK, 1), :] - (ENTROPY * LN2) * row_logs[pl.ds(z, 1), :]
                  + f_square * (1.0 / D))
    col_got[x, row] = col_out[x, row]
    for away in (2, 1, 3, 0):
        for n in range(N_ROW):
            if away or n:
                ox, orow = wrap4(x + away), lax.rem(row + n, N_ROW)
                arrived(col_got.at[ox, orow], col_recv.at[ox, orow])
    every = col_got[...].reshape(NX * N_ROW, 1, BLK + 128)
    high = jnp.max(every[:, :, :BLK], axis=0)
    whole = jnp.sum(jnp.exp2(every[:, :, :BLK] - high[None]), axis=0)
    both_out[pl.ds(1, 1), :] = (ENTROPY * mass_b_ref[...] - (ENTROPY * LN2) * (high + jnp.log2(whole)) + g_square * (1.0 / D))
    bad_out[...] = jnp.max(every[:, :, BLK:], axis=0)

    def sent(b, carry):
        for n in range(1, NZ):
            row_copy(b, n).wait_send()
        return carry

    lax.fori_loop(0, NZ, sent, 0)
    for copy in pending:
        copy.wait_send()


def shape(*dims, kind=jnp.float32):
    return jax.ShapeDtypeStruct(dims, kind)


def general(sources, targets, g_pot, log_a, log_b, src_block, tgt_block, pair_count):
    whole = pl.BlockSpec(memory_space=pltpu.VMEM)
    anywhere = pl.BlockSpec(memory_space=pl.ANY)
    scalars = pl.BlockSpec(memory_space=pltpu.SMEM)
    dma = pltpu.SemaphoreType.DMA
    packed = jnp.zeros((8, 128), jnp.int32)
    packed = packed.at[0, :64].set(src_block).at[0, 64:].set(tgt_block).at[1, 0].set(pair_count[0])
    x_raw, y_raw, lists = pl.pallas_call(
        gather_kernel,
        out_shape=(shape(NZ, ROWS, D), shape(NX, N_ROW, ROWS, D), shape(NX, 8, 128, kind=jnp.int32)),
        in_specs=[anywhere] * 5,
        out_specs=(whole, whole, whole),
        scratch_shapes=[dma((5,)), dma((16, 2, 4)), dma((16, 2)), dma((16, 2)), dma((16, 2)),
                        dma((9, 2, 2)), dma((9, 2)), dma((3,)), dma((3,))],
        compiler_params=pltpu.CompilerParams(collective_id=3, has_side_effects=True, vmem_limit_bytes=VMEM_LIMIT),
    )(sources, targets, g_pot[None], log_a[None], packed)
    y_raw = y_raw.reshape(NX * N_ROW, ROWS, D)
    quarter = (lax.axis_index("col") // NZ).astype(jnp.int32).reshape(1)
    x3, y3, part = pl.pallas_call(
        first_kernel,
        out_shape=(shape(NZ, BLK, 3 * D, kind=jnp.bfloat16), shape(NX * N_ROW, 3 * D, BLK, kind=jnp.bfloat16),
                   shape(NZ, 8, BLK)),
        in_specs=[scalars, scalars, whole, whole],
        out_specs=(whole, whole, whole),
        scratch_shapes=[pltpu.VMEM((NX * N_ROW, 8, BLK), jnp.float32), pltpu.VMEM((NZ, BLK, 128), jnp.float32),
                        pltpu.VMEM((NZ, BLK, 128), jnp.float32)],
        compiler_params=pltpu.CompilerParams(vmem_limit_bytes=VMEM_LIMIT),
    )(lists, quarter, x_raw, y_raw)
    f_own, c_all = pl.pallas_call(
        row_exchange_kernel,
        out_shape=(shape(1, BLK), shape(NZ, 8, BLK)),
        in_specs=[whole, whole],
        out_specs=(whole, whole),
        scratch_shapes=[pltpu.VMEM((NZ - 1, NZ, 8, BLK), jnp.float32), dma((NZ - 1,)), dma((NZ - 1,))],
        compiler_params=pltpu.CompilerParams(collective_id=1, has_side_effects=True, vmem_limit_bytes=VMEM_LIMIT),
    )(part, x_raw)
    sums = pl.pallas_call(
        second_kernel,
        out_shape=shape(NX * N_ROW, 1, BLK),
        in_specs=[scalars, scalars, whole, whole, whole],
        out_specs=whole,
        scratch_shapes=[pltpu.VMEM((NZ, BLK, 128), jnp.float32), pltpu.VMEM((NX * N_ROW, 8, BLK), jnp.float32),
                        pltpu.VMEM((NX * N_ROW, 8, BLK), jnp.float32)],
        compiler_params=pltpu.CompilerParams(vmem_limit_bytes=VMEM_LIMIT),
    )(lists, quarter, x3, y3, c_all)
    g_own = pl.pallas_call(
        col_exchange_kernel,
        out_shape=shape(1, BLK),
        in_specs=[whole, whole, whole],
        out_specs=whole,
        scratch_shapes=[pltpu.VMEM((NX * N_ROW, 1, BLK), jnp.float32), dma((NX * N_ROW,)), dma((NX * N_ROW,))],
        compiler_params=pltpu.CompilerParams(collective_id=2, has_side_effects=True),
    )(sums, targets, log_b[None])
    return f_own.reshape(BLK), g_own.reshape(BLK)


def local(sources, targets, g_pot, log_a, log_b, src_block, tgt_block, pair_count):
    whole = pl.BlockSpec(memory_space=pltpu.VMEM)
    anywhere = pl.BlockSpec(memory_space=pl.ANY)
    dma = pltpu.SemaphoreType.DMA
    vmem = pltpu.VMEM
    f32 = jnp.float32
    both, bad = pl.pallas_call(
        merged_kernel,
        out_shape=(shape(2, BLK), shape(1, 128)),
        in_specs=[anywhere] * 8,
        out_specs=(whole, whole),
        scratch_shapes=[
            vmem((NX, N_ROW, ROWS, D), f32), vmem((NZ, ROWS, D), f32),
            vmem((NX, N_ROW, BLK, 3 * D), jnp.bfloat16), vmem((NZ, BLK, 3 * D), jnp.bfloat16),
            vmem((NX, N_ROW, 8, BLK), f32), vmem((NZ, BLK, 128), f32), vmem((NZ, BLK, 128), f32),
            vmem((NX, 2, NZ, BLK, BLK), f32), vmem((NX, 2, NZ, 8, BLK), f32), vmem((NX, 2, NZ, 8, BLK), f32),
            vmem((NX, NZ, 128), jnp.int32), pltpu.SMEM((NX, NZ, 128), jnp.int32), vmem((N_COL, 128), jnp.int32),
            pltpu.SMEM((64,), jnp.int32), pltpu.SMEM((64,), jnp.int32), pltpu.SMEM((1,), jnp.int32), vmem((1, BLK), f32),
            vmem((NZ, 1, BLK + 128), f32), vmem((NZ, BLK), f32), vmem((NZ, NZ - 1, 1, BLK + 128), f32),
            vmem((NX, N_ROW, 1, BLK + 128), f32), vmem((NX, N_ROW, 1, BLK + 128), f32),
            dma((8,)), dma((16, 2, 4)), dma((16, 2)), dma((16, 2)), dma((16, 2)),
            dma((9, 2, 2)), dma((9, 2)), dma((3,)), dma((3,)),
            dma((NZ, NZ - 1)), dma((NZ, NZ - 1)), dma((NX, N_ROW)), dma((NX, N_ROW))],
        compiler_params=pltpu.CompilerParams(collective_id=0, has_side_effects=True, vmem_limit_bytes=VMEM_LIMIT),
    )(src_block, tgt_block, pair_count, sources, targets, g_pot[None], log_a[None], log_b[None])
    args = (sources, targets, g_pot, log_a, log_b, src_block, tgt_block, pair_count)
    both = lax.cond(bad[0, 0] > 0.5, lambda: jnp.stack(general(*args)), lambda: both)
    return both[0], both[1]


def solution(mesh):
    placed = (
        P(("row", "col"), None),
        P(("col", "row"), None),
        P(("col", "row")),
        P(("row", "col")),
        P(("col", "row")),
        P(("row", "col")),
        P(("row", "col")),
        P(("row", "col")),
    )
    return jax.shard_map(
        local,
        mesh=mesh,
        in_specs=placed,
        out_specs=(P(("row", "col")), P(("col", "row"))),
        check_vma=False,
    )
```

```python
import functools
import math

import jax
import jax.numpy as jnp
from jax import lax
from jax.experimental import pallas as pl
from jax.experimental.pallas import tpu as pltpu
from jax.sharding import PartitionSpec as P

MESH = pl.DeviceIdType.MESH
BLK = 256
D = 256
ROWS = 264
NX, NY, NZ = 4, 4, 8
N_ROW, N_COL = 8, 32
ENTROPY = 0.05
LOG2E = 1.0 / math.log(2.0)
LN2 = math.log(2.0)
KAPPA = LOG2E / ENTROPY
LOWEST = -1.0e30
CHUNKS = ((0, 128), (128, 136))
VMEM_LIMIT = 60 * 1024 * 1024


def place():
    r, c = lax.axis_index("row"), lax.axis_index("col")
    return r // 2, lax.rem(r, 2), c // NZ, lax.rem(c, NZ)


def device(y, core, x, z):
    return {"row": y * 2 + core, "col": x * NZ + z}


def signal(sem, where):
    pl.semaphore_signal(sem, inc=1, device_id=where, device_id_type=MESH)


FIRST = ((1, 0), (3, 0), (0, 1), (0, 3))
SECOND = ((2, 0), (1, 1), (1, 3), (3, 1), (3, 3), (0, 2))
THIRD = ((2, 1), (2, 3), (1, 2), (3, 2))
FOURTH = ((2, 2),)


def sends_of(da, db):
    out = []
    if db == 0:
        if da == 0:
            out += [("A+", (1, 0)), ("A-", (3, 0))]
        if da == 1:
            out += [("A+", (2, 0))]
        out += [("B+", (da, 1)), ("B-", (da, 3))]
    elif db == 1 and da in (0, 1):
        out += [("B+", (da, 2))]
    elif db == 3 and da in (2, 3):
        out += [("B-", (da, 2))]
    return out


REACHED = FIRST + SECOND + THIRD + FOURTH
OTHER_WAY = {"A+": "A-", "A-": "A+", "B+": "B+", "B-": "B-"}


def mirror(pos):
    return (4 - pos[0]) % 4, pos[1]


def chunk_sends(pos, ch):
    if ch == 0:
        return sends_of(*pos)
    return [(OTHER_WAY[name], mirror(target)) for name, target in sends_of(*mirror(pos))]


PARTS = ((0, 160), (160, 104))
STEPS = (
    ("X", 0), ("Y", 0, 0), ("M", 0, 0), ("y", 1, 0, 0), ("y", 0, 1, 0), ("z", 1, 0), ("y", 0, 3, 0), ("y", 3, 0, 0),
    ("z", -1, 0), ("y", 1, 0, 1), ("y", 0, 1, 1), ("z", 1, 1), ("y", 0, 3, 1), ("y", 3, 0, 1), ("z", -1, 1), ("X", 1),
    ("X", -1), ("Y", 1, 0), ("Y", 3, 0), ("Y", 0, 1), ("Y", 0, 3), ("M", 1, 0), ("M", 0, 1), ("M", 0, 3), ("z", 2, 0),
    ("y", 2, 0, 0), ("y", 1, 3, 0), ("y", 1, 1, 0), ("z", -2, 0), ("M", 3, 0), ("y", 2, 0, 1), ("Y", 2, 0),
    ("y", 3, 3, 0), ("y", 0, 2, 0), ("M", 2, 0), ("y", 3, 1, 0), ("z", -2, 1), ("z", 2, 1), ("X", 2), ("y", 1, 3, 1),
    ("X", -2), ("Y", 1, 3), ("y", 1, 1, 1), ("Y", 1, 1), ("y", 3, 3, 1), ("Y", 3, 3), ("M", 1, 3), ("z", -3, 0),
    ("z", 3, 0), ("M", 1, 1), ("y", 0, 2, 1), ("y", 2, 3, 0), ("Y", 0, 2), ("M", 3, 3), ("M", 0, 2), ("y", 2, 3, 1),
    ("y", 3, 1, 1), ("Y", 3, 1), ("Y", 2, 3), ("D", 0, 1), ("z", -3, 1), ("z", 3, 1), ("y", 3, 2, 0), ("y", 2, 1, 0),
    ("X", 3), ("X", -3), ("M", 2, 3), ("M", 3, 1), ("D", -1, 2), ("z", 4, 0), ("y", 1, 2, 0), ("y", 1, 2, 1),
    ("Y", 1, 2), ("D", -2, 3), ("y", 2, 2, 0), ("y", 2, 1, 1), ("Y", 2, 1), ("z", 4, 1), ("X", 4), ("D", -3, 4),
    ("M", 1, 2), ("y", 3, 2, 1), ("y", 2, 2, 1), ("Y", 3, 2), ("Y", 2, 2), ("M", 2, 1), ("M", 3, 2),
)


def gather_kernel(src_ref, tgt_ref, pot_ref, mass_ref, list_ref, x_out, y_out, lists_out,
                  load_sem, send_sem, recv_sem, mate_send, mate_recv, z_send, z_recv, l_send, l_recv):
    y, k, x, z = place()
    row = y * 2 + k

    def wrap4(v):
        return lax.rem(v + 8, 4)

    sigma = 1 - 2 * k

    def step_a(n):
        return wrap4(y + n * sigma * k), wrap4(x + n * sigma * (1 - k))

    def step_b(n):
        return wrap4(y + n * (1 - k)), wrap4(x + n * k)

    def dev_of(name):
        n = 1 if name[1] == "+" else -1
        ny, nx = step_a(n) if name[0] == "A" else step_b(n)
        return device(ny, k, nx, z)

    mate = device(y, 1 - k, x, z)
    z_long = device(y, k, x, lax.rem(z + sigma + NZ, NZ))
    z_short = device(y, k, x, lax.rem(z - sigma + NZ, NZ))

    def slot(da, db, core=None):
        if core is None:
            core = k
        oy = wrap4(y - db * (1 - core) + da * core)
        ox = wrap4(x - da * (1 - core) - db * core)
        return ox, oy * 2 + core

    loads = [
        pltpu.make_async_copy(tgt_ref, y_out.at[x, row, pl.ds(0, BLK)], load_sem.at[0]),
        pltpu.make_async_copy(pot_ref, y_out.at[x, row, pl.ds(BLK, 1)], load_sem.at[1]),
        pltpu.make_async_copy(src_ref, x_out.at[z, pl.ds(0, BLK)], load_sem.at[2]),
        pltpu.make_async_copy(mass_ref, x_out.at[z, pl.ds(BLK, 1)], load_sem.at[3]),
        pltpu.make_async_copy(list_ref, lists_out.at[x], load_sem.at[4]),
    ]
    for copy in loads:
        copy.start()
    barrier = pltpu.get_barrier_semaphore()
    peers = [device(y, k, wrap4(x + 1), z), device(y, k, wrap4(x + 3), z), device(y, k, wrap4(x + 2), z),
             device(wrap4(y + 1), k, x, z), device(wrap4(y + 3), k, x, z), mate, z_long, z_short]
    for peer in peers:
        signal(barrier, peer)
    pl.semaphore_wait(barrier, len(peers))
    for copy in loads:
        copy.wait()

    pending = []

    def at(pos):
        return pos[0] * 4 + pos[1]

    def part(ref, ch):
        return ref.at[pl.ds(*CHUNKS[ch])]

    def y_copy(pos, ch, where, target, n):
        ox, orow = slot(*pos)
        return pltpu.make_async_remote_copy(
            src_ref=part(y_out.at[ox, orow], ch), dst_ref=part(y_out.at[ox, orow], ch),
            send_sem=send_sem.at[at(pos), ch, n], recv_sem=recv_sem.at[at(target), ch],
            device_id=where, device_id_type=MESH)

    def mate_copy(pos, ch):
        ox, orow = slot(*pos)
        return pltpu.make_async_remote_copy(
            src_ref=part(y_out.at[ox, orow], ch), dst_ref=part(y_out.at[ox, orow], ch),
            send_sem=mate_send.at[at(pos), ch], recv_sem=mate_recv.at[at(pos), ch],
            device_id=mate, device_id_type=MESH)

    def send_y(pos, ch):
        for n, (name, target) in enumerate(sends_of(*pos)):
            copy = y_copy(pos, ch, dev_of(name), target, n)
            copy.start()
            pending.append(copy)
        copy = mate_copy(pos, ch)
        copy.start()
        pending.append(copy)

    def recv_y(pos, ch):
        ox, orow = slot(*pos)
        ref = part(y_out.at[ox, orow], ch)
        pltpu.make_async_remote_copy(src_ref=ref, dst_ref=ref, send_sem=send_sem.at[0, 0, 0],
                                     recv_sem=recv_sem.at[at(pos), ch], device_id=mate,
                                     device_id_type=MESH).wait_recv()

    def recv_mate(pos, ch):
        ox, orow = slot(*pos, core=1 - k)
        ref = part(y_out.at[ox, orow], ch)
        pltpu.make_async_remote_copy(src_ref=ref, dst_ref=ref, send_sem=send_sem.at[0, 0, 0],
                                     recv_sem=mate_recv.at[at(pos), ch], device_id=mate,
                                     device_id_type=MESH).wait_recv()

    def z_slot(n):
        return lax.rem(z - n * sigma + NZ * 4, NZ)

    def send_z(n, ch, long):
        target = n + 1 if long else n - 1
        ref = part(x_out.at[z_slot(n)], ch)
        copy = pltpu.make_async_remote_copy(
            src_ref=ref, dst_ref=ref, send_sem=z_send.at[n + 4, ch, 0 if long else 1],
            recv_sem=z_recv.at[target + 4, ch],
            device_id=z_long if long else z_short, device_id_type=MESH)
        copy.start()
        pending.append(copy)

    def recv_z(n, ch):
        ref = part(x_out.at[z_slot(n)], ch)
        pltpu.make_async_remote_copy(src_ref=ref, dst_ref=ref, send_sem=send_sem.at[0, 0, 0],
                                     recv_sem=z_recv.at[n + 4, ch], device_id=mate,
                                     device_id_type=MESH).wait_recv()

    for n in (1, 2, 3):
        copy = pltpu.make_async_remote_copy(
            src_ref=lists_out.at[x], dst_ref=lists_out.at[x], send_sem=l_send.at[n - 1], recv_sem=l_recv.at[n - 1],
            device_id=device(y, k, wrap4(x + n), z), device_id_type=MESH)
        copy.start()
        pending.append(copy)
    for ch in (0, 1):
        send_y((0, 0), ch)
        send_z(0, ch, True)
        send_z(0, ch, False)
    levels = (FIRST, SECOND, THIRD, FOURTH)
    for level in range(4):
        for ch in (0, 1):
            for pos in levels[level]:
                recv_y(pos, ch)
                send_y(pos, ch)
            n = level + 1
            recv_z(n, ch)
            if n < 4:
                send_z(n, ch, True)
                recv_z(-n, ch)
                if n < 3:
                    send_z(-n, ch, False)
    for n in (1, 2, 3):
        ref = lists_out.at[wrap4(x - n)]
        pltpu.make_async_remote_copy(src_ref=ref, dst_ref=ref, send_sem=l_send.at[0], recv_sem=l_recv.at[n - 1],
                                     device_id=mate, device_id_type=MESH).wait_recv()
    for ch in (0, 1):
        for da in range(4):
            for db in range(4):
                recv_mate((da, db), ch)
    for copy in pending:
        copy.wait_send()


def split3(v):
    hi = v.astype(jnp.bfloat16)
    lo = (v - hi.astype(jnp.float32)).astype(jnp.bfloat16)
    return hi, lo


def prep_kernel_body(x_raw, y_raw, x3, y3, bias):
    def one_x(i, carry):
        hi, lo = split3(x_raw[i, pl.ds(0, BLK), :])
        x3[i, :, pl.ds(0, D)] = hi
        x3[i, :, pl.ds(D, D)] = lo
        x3[i, :, pl.ds(2 * D, D)] = hi
        return carry

    lax.fori_loop(0, NZ, one_x, 0)

    def one_y(i, carry):
        block = y_raw[i, pl.ds(0, BLK), :].T
        pot = y_raw[i, pl.ds(BLK, 1), :]
        square = jnp.sum(block * block, axis=0, keepdims=True)
        row = KAPPA * (pot - square * (1.0 / D))
        bias[i] = jnp.broadcast_to(row, (8, BLK))
        hi, lo = split3(block * (2.0 * KAPPA / D))
        y3[i, pl.ds(0, D), :] = hi
        y3[i, pl.ds(D, D), :] = hi
        y3[i, pl.ds(2 * D, D), :] = lo
        return carry

    lax.fori_loop(0, NX * N_ROW, one_y, 0)


def pairs_of(lists, quarter, body):
    for other in range(NX):
        def one(i, carry, other=other):
            src = lists[other, 0, i]

            @pl.when(src // NZ == quarter)
            def _():
                body(lax.rem(src, NZ), other * N_ROW + lists[other, 0, 64 + i])
            return carry

        lax.fori_loop(0, lists[other, 1, 0], one, 0)


def first_kernel(lists, quarter, x_raw, y_raw, x3, y3, part_out, bias, top, total):
    prep_kernel_body(x_raw, y_raw, x3, y3, bias)
    top[...] = jnp.full(top.shape, LOWEST, jnp.float32)
    total[...] = jnp.zeros(total.shape, jnp.float32)

    def pair(b, t):
        g = jnp.dot(x3[b], y3[t], preferred_element_type=jnp.float32)
        row = bias[t]
        s1 = g[:, :128] + row[0:1, :128]
        s2 = g[:, 128:] + row[0:1, 128:]
        old = top[b]
        new = jnp.maximum(old, jnp.maximum(s1, s2))
        total[b] = total[b] * jnp.exp2(old - new) + jnp.exp2(s1 - new) + jnp.exp2(s2 - new)
        top[b] = new

    pairs_of(lists, quarter[0], pair)

    def close(b, carry):
        high = jnp.max(top[b], axis=1, keepdims=True)
        whole = jnp.sum(total[b] * jnp.exp2(top[b] - high), axis=1, keepdims=True)
        logs = jnp.where(whole > 0.0, high + jnp.log2(whole), LOWEST)
        part_out[b] = jnp.broadcast_to(logs, (BLK, 128)).T[0:8, :]
        return carry

    lax.fori_loop(0, NZ, close, 0)


def row_exchange_kernel(part_ref, x_raw, f_out, c_out, got, send_sem, recv_sem):
    y, k, x, z = place()
    barrier = pltpu.get_barrier_semaphore()
    for n in range(1, NZ):
        signal(barrier, device(y, k, x, lax.rem(z + n, NZ)))
    pl.semaphore_wait(barrier, NZ - 1)
    copies = []
    for n in range(1, NZ):
        copy = pltpu.make_async_remote_copy(
            src_ref=part_ref, dst_ref=got.at[n - 1], send_sem=send_sem.at[n - 1], recv_sem=recv_sem.at[n - 1],
            device_id=device(y, k, x, lax.rem(z + n, NZ)), device_id_type=MESH)
        copy.start()
        copies.append(copy)
    for copy in copies:
        copy.wait()
    own = part_ref[...]
    others = [got[n] for n in range(NZ - 1)]
    top = own
    for v in others:
        top = jnp.maximum(top, v)
    total = jnp.exp2(own - top)
    for v in others:
        total = total + jnp.exp2(v - top)
    logs = top + jnp.log2(total)
    c_out[...] = LOG2E * x_raw[:, pl.ds(BLK, 1), :] - logs
    square = x_raw[z, pl.ds(0, BLK), :].T
    square = jnp.sum(square * square, axis=0, keepdims=True)
    mass = x_raw[z, pl.ds(BLK, 1), :]
    c_here = c_out[z]
    f_out[...] = ENTROPY * mass - (ENTROPY * LN2) * (LOG2E * mass - c_here[0:1, :]) + square * (1.0 / D)


def second_kernel(lists, quarter, x3, y3, c_ref, part_out, cols, top, total):
    top[...] = jnp.full(top.shape, LOWEST, jnp.float32)
    total[...] = jnp.zeros(total.shape, jnp.float32)

    def widen(b, carry):
        cols[b] = jnp.broadcast_to(c_ref[b, pl.ds(0, 1), :], (128, BLK)).T
        return carry

    lax.fori_loop(0, NZ, widen, 0)

    def pair(b, t):
        g = jnp.dot(x3[b], y3[t], preferred_element_type=jnp.float32)
        col = cols[b]
        u = g + jnp.concatenate([col, col], axis=1)
        u = u.reshape(BLK // 8, 8, BLK)
        old = top[t]
        new = jnp.maximum(old, jnp.max(u, axis=0))
        total[t] = total[t] * jnp.exp2(old - new) + jnp.sum(jnp.exp2(u - new[None]), axis=0)
        top[t] = new

    pairs_of(lists, quarter[0], pair)

    def close(t, carry):
        high = jnp.max(top[t], axis=0, keepdims=True)
        whole = jnp.sum(total[t] * jnp.exp2(top[t] - high), axis=0, keepdims=True)
        part_out[t] = jnp.where(whole > 0.0, high + jnp.log2(whole), LOWEST)
        return carry

    lax.fori_loop(0, NX * N_ROW, close, 0)


def col_exchange_kernel(part_ref, tgt_ref, mass_ref, g_out, got, send_sem, recv_sem):
    y, k, x, z = place()
    me = x * N_ROW + y * 2 + k
    many = NX * N_ROW
    barrier = pltpu.get_barrier_semaphore()

    def peer(n):
        other = lax.rem(me + n, many)
        return other, {"row": lax.rem(other, N_ROW), "col": (other // N_ROW) * NZ + z}

    for n in range(1, many):
        signal(barrier, peer(n)[1])
    pl.semaphore_wait(barrier, many - 1)
    copies = []
    for n in range(1, many):
        other, where = peer(n)
        copy = pltpu.make_async_remote_copy(
            src_ref=part_ref.at[other], dst_ref=got.at[n], send_sem=send_sem.at[n], recv_sem=recv_sem.at[n],
            device_id=where, device_id_type=MESH)
        copy.start()
        copies.append(copy)
    block = tgt_ref[...].T
    square = jnp.sum(block * block, axis=0, keepdims=True)
    for copy in copies:
        copy.wait()
    got[0] = part_ref[me]
    every = got[...]
    top = jnp.max(every, axis=0)
    total = jnp.sum(jnp.exp2(every - top[None]), axis=0)
    logs = top + jnp.log2(total)
    g_out[...] = ENTROPY * mass_ref[...] - (ENTROPY * LN2) * logs + square * (1.0 / D)

def nt_dot(a, b):
    return lax.dot_general(a, b, (((1,), (1,)), ((), ())), preferred_element_type=jnp.float32)


def merged_kernel(src_in, tgt_in, count_in, src_ref, tgt_ref, pot_ref, mass_ref, mass_b_in,
                  both_out, bad_out,
                  y_raw, x_raw, y3, x3, bias, top, total, scores, col_top, col_sum, tabs, tab_s, mine, src_list, tgt_list, count_ref, mass_b_ref, row_out, row_logs, row_got,
                  col_out, col_got,
                  load_sem, send_sem, recv_sem, mate_send, mate_recv, z_send, z_recv, l_send, l_recv,
                  row_send, row_recv, col_send, col_recv):
    y, k, x, z = place()
    row = y * 2 + k
    sigma = 1 - 2 * k

    def wrap4(v):
        return lax.rem(v + 8, 4)

    def step_a(n):
        return wrap4(y + n * sigma * k), wrap4(x + n * sigma * (1 - k))

    def step_b(n):
        return wrap4(y + n * (1 - k)), wrap4(x + n * k)

    def dev_of(name):
        n = 1 if name[1] == "+" else -1
        ny, nx = step_a(n) if name[0] == "A" else step_b(n)
        return device(ny, k, nx, z)

    mate = device(y, 1 - k, x, z)
    z_long = device(y, k, x, lax.rem(z + sigma + NZ, NZ))
    z_short = device(y, k, x, lax.rem(z - sigma + NZ, NZ))

    def slot(da, db, core):
        oy = wrap4(y - db * (1 - core) + da * core)
        ox = wrap4(x - da * (1 - core) - db * core)
        return ox, oy * 2 + core

    loads = [
        pltpu.make_async_copy(tgt_ref, y_raw.at[x, row, pl.ds(0, BLK)], load_sem.at[0]),
        pltpu.make_async_copy(pot_ref, y_raw.at[x, row, pl.ds(BLK, 1)], load_sem.at[1]),
        pltpu.make_async_copy(src_ref, x_raw.at[z, pl.ds(0, BLK)], load_sem.at[2]),
        pltpu.make_async_copy(mass_ref, x_raw.at[z, pl.ds(BLK, 1)], load_sem.at[3]),
    ]
    small = [
        pltpu.make_async_copy(src_in, src_list, load_sem.at[4]),
        pltpu.make_async_copy(tgt_in, tgt_list, load_sem.at[5]),
        pltpu.make_async_copy(count_in, count_ref, load_sem.at[6]),
        pltpu.make_async_copy(mass_b_in, mass_b_ref, load_sem.at[7]),
    ]
    for copy in loads + small:
        copy.start()
    barrier = pltpu.get_barrier_semaphore()
    peers = [device(y, k, wrap4(x + 1), z), device(y, k, wrap4(x + 3), z), device(y, k, wrap4(x + 2), z),
             device(wrap4(y + 1), k, x, z), device(wrap4(y + 3), k, x, z), mate, z_long, z_short]
    for peer in peers:
        signal(barrier, peer)

    pl.semaphore_wait(barrier, len(peers))
    for copy in loads:
        copy.wait()

    pending = []

    def at(pos):
        return pos[0] * 4 + pos[1]

    def part(ref, ch):
        return ref.at[pl.ds(*PARTS[ch])]

    def remote(src, dst, send, recv, where):
        return pltpu.make_async_remote_copy(src_ref=src, dst_ref=dst, send_sem=send, recv_sem=recv,
                                            device_id=where, device_id_type=MESH)

    def start(copy):
        copy.start()
        pending.append(copy)

    def arrived(ref, sem):
        remote(ref, ref, send_sem.at[0, 0, 0], sem, mate).wait_recv()

    def send_y(pos, ch):
        ref = part(y_raw.at[slot(*pos, k)], ch)
        for n, (name, target) in enumerate(chunk_sends(pos, ch)):
            start(remote(ref, ref, send_sem.at[at(pos), ch, n], recv_sem.at[at(target), ch], dev_of(name)))

    def send_mate(pos, ch):
        ref = part(y_raw.at[slot(*pos, k)], ch)
        start(remote(ref, ref, mate_send.at[at(pos), ch], mate_recv.at[at(pos), ch], mate))

    def recv_y(pos, ch):
        arrived(part(y_raw.at[slot(*pos, k)], ch), recv_sem.at[at(pos), ch])

    def z_slot(n):
        return lax.rem(z - n * sigma + NZ * 4, NZ)

    def send_z(n, ch, long):
        target = n + 1 if long else n - 1
        ref = part(x_raw.at[z_slot(n)], ch)
        start(remote(ref, ref, z_send.at[n + 4, ch, 0 if long else 1], z_recv.at[target + 4, ch],
                     z_long if long else z_short))

    def recv_z(n, ch):
        arrived(part(x_raw.at[z_slot(n)], ch), z_recv.at[n + 4, ch])

    def prep_x(zb):
        hi, lo = split3(x_raw[zb, pl.ds(0, BLK), :])
        x3[zb, :, pl.ds(0, D)] = hi
        x3[zb, :, pl.ds(D, D)] = lo
        x3[zb, :, pl.ds(2 * D, D)] = hi

    def prep_y(da, db, core):
        xq, t = slot(da, db, core)
        block = y_raw[xq, t, pl.ds(0, BLK), :]
        square = jnp.sum(block * block, axis=1, keepdims=True)
        square = jnp.broadcast_to(square, (BLK, 128)).T[0:8]
        bias[xq, t] = KAPPA * (y_raw[xq, t, pl.ds(BLK, 1), :] - square * (1.0 / D))
        hi, lo = split3(block * (2.0 * KAPPA / D))
        y3[xq, t, :, pl.ds(0, D)] = hi
        y3[xq, t, :, pl.ds(D, D)] = hi
        y3[xq, t, :, pl.ds(2 * D, D)] = lo

    def prep_mate(da, db):
        for ch in (0, 1):
            arrived(part(y_raw.at[slot(da, db, 1 - k)], ch), mate_recv.at[da * 4 + db, ch])
        prep_y(da, db, 1 - k)

    def pair(xq, zb):
        parts = []
        for n in (0, 1):
            t = tab_s[xq, zb, 64 * n]
            alive = t > 0
            t = lax.max(t - 1, 0)
            g = nt_dot(x3[zb], y3[xq, t])
            scores[xq, n, zb] = g
            shift = jnp.where(alive, bias[xq, t], LOWEST)[0:1]
            parts += [g[:, :128] + shift[:, :128], g[:, 128:] + shift[:, 128:]]
        old = top[zb]
        new = jnp.maximum(old, jnp.maximum(jnp.maximum(parts[0], parts[1]), jnp.maximum(parts[2], parts[3])))
        e = [jnp.exp2(v - new) for v in parts]
        total[zb] = total[zb] * jnp.exp2(old - new) + ((e[0] + e[1]) + (e[2] + e[3]))
        top[zb] = new

    for ch in (0, 1):
        send_y((0, 0), ch)
        send_z(0, ch, True)
        send_z(0, ch, False)
        send_mate((0, 0), ch)
    for copy in small:
        copy.wait()
    ids = lax.broadcasted_iota(jnp.int32, (N_COL, 128), 0)
    left = lax.broadcasted_iota(jnp.int32, (N_COL, 128), 1) < 64
    live = count_ref[0]

    def enter(i, carry):
        table, named = carry
        one = jnp.where(i < live, tgt_list[i] + 1, 0)
        two = jnp.where(i + 32 < live, tgt_list[i + 32] + 1, 0)
        here = ids == src_list[i]
        table = table + jnp.where(here, jnp.where(left, one, two), 0)
        named = named + jnp.where(here, jnp.where(i < live, 1, 0), 0)
        return table, named

    nothing = jnp.zeros((N_COL, 128), jnp.int32)
    table, named = lax.fori_loop(0, 32, enter, (nothing, nothing))
    mine[...] = jnp.minimum(table, N_ROW)
    bad = jnp.max(jnp.where(named > 1, 1.0, 0.0), axis=0, keepdims=True)
    top[...] = jnp.full(top.shape, LOWEST, jnp.float32)
    total[...] = jnp.zeros(total.shape, jnp.float32)

    keep = pltpu.make_async_copy(mine.at[pl.ds(x * NZ, NZ)], tabs.at[x], load_sem.at[0])
    keep.start()
    for n in (1, 2, 3):
        to = wrap4(x + n)
        start(remote(mine.at[pl.ds(to * NZ, NZ)], tabs.at[x], l_send.at[n - 1], l_recv.at[n - 1], device(y, k, to, z)))
    keep.wait()
    tab_copy = pltpu.make_async_copy(tabs, tab_s, load_sem.at[1])
    paired = 0
    for step in STEPS:
        kind = step[0]
        if kind == "y":
            pos, ch = step[1:3], step[3]
            recv_y(pos, ch)
            send_y(pos, ch)
            send_mate(pos, ch)
        elif kind == "z":
            n, ch = step[1:]
            recv_z(n, ch)
            if 0 < n < 4:
                send_z(n, ch, True)
            if -3 < n < 0:
                send_z(n, ch, False)
        elif kind == "X":
            prep_x(z_slot(step[1]))
            if step[1] == -1:
                for n in (1, 2, 3):
                    arrived(tabs.at[wrap4(x - n)], l_recv.at[n - 1])
                tab_copy.start()
        elif kind == "Y":
            prep_y(step[1], step[2], k)
        elif kind == "M":
            prep_mate(step[1], step[2])
        else:
            if not paired:
                tab_copy.wait()
            paired += 1
            pair(x, z_slot(step[1]))
            pair(x, z_slot(step[2]))

    def row_copy(b, n):
        return remote(row_out.at[b], row_got.at[b, n - 1], row_send.at[b, n - 1], row_recv.at[b, n - 1],
                      device(y, k, x, lax.rem(z + n, NZ)))

    def sums_of(b):
        high = jnp.max(top[b], axis=1, keepdims=True)
        whole = jnp.sum(total[b] * jnp.exp2(top[b] - high), axis=1, keepdims=True)
        return jnp.where(whole > 0.0, high + jnp.log2(whole), LOWEST)

    first_half = lax.broadcasted_iota(jnp.int32, (BLK, 128), 1) < 64

    def pairs_with(i, groups):
        for away in groups:
            for b in (2 * i, 2 * i + 1):
                pair(wrap4(x + away), b)

    def leave(i):
        both_sums = jnp.where(first_half, sums_of(2 * i), sums_of(2 * i + 1)).T
        for n in (0, 1):
            row_out[2 * i + n, :, pl.ds(0, BLK)] = both_sums[64 * n:64 * n + 1]
            row_out[2 * i + n, :, pl.ds(BLK, 128)] = bad
        for b in (2 * i, 2 * i + 1):
            for n in range(1, NZ):
                row_copy(b, n).start()

    def far(i, carry):
        pairs_with(i, (1, 3, 2))
        leave(i)
        return carry

    pairs_with(0, (1, 3))
    prep_mate(2, 2)
    pairs_with(0, (2,))
    leave(0)
    lax.fori_loop(1, NZ // 2, far, 0)

    def rows_of(b, bad):
        for n in range(1, NZ):
            arrived(row_got.at[b, n - 1], row_recv.at[b, n - 1])
        own = row_out[b, :, pl.ds(0, BLK)]
        others = [row_got[b, n, :, pl.ds(0, BLK)] for n in range(NZ - 1)]
        for n in range(NZ - 1):
            bad = jnp.maximum(bad, row_got[b, n, :, pl.ds(BLK, 128)])
        high = own
        for v in others:
            high = jnp.maximum(high, v)
        whole = jnp.exp2(own - high)
        for v in others:
            whole = whole + jnp.exp2(v - high)
        logs = high + jnp.log2(whole)
        row_logs[pl.ds(b, 1), :] = logs
        shift = LOG2E * x_raw[b, pl.ds(BLK, 1), :] - logs
        top[b] = jnp.broadcast_to(shift, (128, BLK)).T
        return bad

    def second(xq, zb):
        for n in (0, 1):
            for h in (0, 128):
                u = (scores[xq, n, zb, :, pl.ds(h, 128)] + top[zb]).reshape(BLK // 8, 8, 128)
                m = jnp.max(u, axis=0)
                col_top[xq, n, zb, :, pl.ds(h, 128)] = m
                col_sum[xq, n, zb, :, pl.ds(h, 128)] = jnp.sum(jnp.exp2(u - m[None]), axis=0)

    def early(b, bad):
        bad = rows_of(b, bad)

        def one(i, carry):
            second(2 * i, b)
            second(2 * i + 1, b)
            return carry

        lax.fori_loop(0, NX // 2, one, 0)
        return bad

    bad = lax.fori_loop(0, NZ - 2, early, bad)
    bad = rows_of(NZ - 1, rows_of(NZ - 2, bad))

    def columns(xq):
        m = col_top[xq].reshape(2 * NZ, 8, BLK)
        high = jnp.max(m, axis=1)
        whole = jnp.sum(col_sum[xq].reshape(2 * NZ, 8, BLK) * jnp.exp2(m - high[:, None, :]), axis=1)
        slots = high + jnp.log2(whole)
        named = tabs[xq]
        named = jnp.concatenate([jnp.broadcast_to(named[:, 0:1], (NZ, BLK)),
                                 jnp.broadcast_to(named[:, 64:65], (NZ, BLK))], axis=0)
        for t in range(N_ROW):
            v = jnp.where(named == t + 1, slots, LOWEST)
            high = jnp.max(v, axis=0, keepdims=True)
            whole = jnp.sum(jnp.exp2(v - high), axis=0, keepdims=True)
            col_out[xq, t, :, pl.ds(0, BLK)] = high + jnp.log2(whole)
            col_out[xq, t, :, pl.ds(BLK, 128)] = bad

    def col_copy(xq, t):
        return remote(col_out.at[xq, t], col_got.at[x, row], col_send.at[xq, t], col_recv.at[x, row],
                      {"row": t, "col": xq * NZ + z})

    for away in (2, 1, 3, 0):
        xq = wrap4(x + away)
        second(xq, NZ - 2)
        second(xq, NZ - 1)
        columns(xq)
        for n in range(N_ROW):
            if away or n:
                start(col_copy(xq, lax.rem(row + n, N_ROW)))
    f_square = x_raw[z, pl.ds(0, BLK), :]
    f_square = jnp.broadcast_to(jnp.sum(f_square * f_square, axis=1, keepdims=True), (BLK, 128)).T[0:1]
    g_square = y_raw[x, row, pl.ds(0, BLK), :]
    g_square = jnp.broadcast_to(jnp.sum(g_square * g_square, axis=1, keepdims=True), (BLK, 128)).T[0:1]
    both_out[pl.ds(0, 1), :] = (ENTROPY * x_raw[z, pl.ds(BLK, 1), :] - (ENTROPY * LN2) * row_logs[pl.ds(z, 1), :]
                  + f_square * (1.0 / D))
    col_got[x, row] = col_out[x, row]
    for away in (2, 1, 3, 0):
        for n in range(N_ROW):
            if away or n:
                ox, orow = wrap4(x + away), lax.rem(row + n, N_ROW)
                arrived(col_got.at[ox, orow], col_recv.at[ox, orow])
    every = col_got[...].reshape(NX * N_ROW, 1, BLK + 128)
    high = jnp.max(every[:, :, :BLK], axis=0)
    whole = jnp.sum(jnp.exp2(every[:, :, :BLK] - high[None]), axis=0)
    both_out[pl.ds(1, 1), :] = (ENTROPY * mass_b_ref[...] - (ENTROPY * LN2) * (high + jnp.log2(whole)) + g_square * (1.0 / D))
    bad_out[0, 0] = jnp.max(every[:, :, BLK:])

    def sent(b, carry):
        for n in range(1, NZ):
            row_copy(b, n).wait_send()
        return carry

    lax.fori_loop(0, NZ, sent, 0)
    for copy in pending:
        copy.wait_send()


def shape(*dims, kind=jnp.float32):
    return jax.ShapeDtypeStruct(dims, kind)


def general(sources, targets, g_pot, log_a, log_b, src_block, tgt_block, pair_count):
    whole = pl.BlockSpec(memory_space=pltpu.VMEM)
    anywhere = pl.BlockSpec(memory_space=pl.ANY)
    scalars = pl.BlockSpec(memory_space=pltpu.SMEM)
    dma = pltpu.SemaphoreType.DMA
    packed = jnp.zeros((8, 128), jnp.int32)
    packed = packed.at[0, :64].set(src_block).at[0, 64:].set(tgt_block).at[1, 0].set(pair_count[0])
    x_raw, y_raw, lists = pl.pallas_call(
        gather_kernel,
        out_shape=(shape(NZ, ROWS, D), shape(NX, N_ROW, ROWS, D), shape(NX, 8, 128, kind=jnp.int32)),
        in_specs=[anywhere] * 5,
        out_specs=(whole, whole, whole),
        scratch_shapes=[dma((5,)), dma((16, 2, 4)), dma((16, 2)), dma((16, 2)), dma((16, 2)),
                        dma((9, 2, 2)), dma((9, 2)), dma((3,)), dma((3,))],
        compiler_params=pltpu.CompilerParams(collective_id=3, has_side_effects=True, vmem_limit_bytes=VMEM_LIMIT),
    )(sources, targets, g_pot[None], log_a[None], packed)
    y_raw = y_raw.reshape(NX * N_ROW, ROWS, D)
    quarter = (lax.axis_index("col") // NZ).astype(jnp.int32).reshape(1)
    x3, y3, part = pl.pallas_call(
        first_kernel,
        out_shape=(shape(NZ, BLK, 3 * D, kind=jnp.bfloat16), shape(NX * N_ROW, 3 * D, BLK, kind=jnp.bfloat16),
                   shape(NZ, 8, BLK)),
        in_specs=[scalars, scalars, whole, whole],
        out_specs=(whole, whole, whole),
        scratch_shapes=[pltpu.VMEM((NX * N_ROW, 8, BLK), jnp.float32), pltpu.VMEM((NZ, BLK, 128), jnp.float32),
                        pltpu.VMEM((NZ, BLK, 128), jnp.float32)],
        compiler_params=pltpu.CompilerParams(vmem_limit_bytes=VMEM_LIMIT),
    )(lists, quarter, x_raw, y_raw)
    f_own, c_all = pl.pallas_call(
        row_exchange_kernel,
        out_shape=(shape(1, BLK), shape(NZ, 8, BLK)),
        in_specs=[whole, whole],
        out_specs=(whole, whole),
        scratch_shapes=[pltpu.VMEM((NZ - 1, NZ, 8, BLK), jnp.float32), dma((NZ - 1,)), dma((NZ - 1,))],
        compiler_params=pltpu.CompilerParams(collective_id=1, has_side_effects=True, vmem_limit_bytes=VMEM_LIMIT),
    )(part, x_raw)
    sums = pl.pallas_call(
        second_kernel,
        out_shape=shape(NX * N_ROW, 1, BLK),
        in_specs=[scalars, scalars, whole, whole, whole],
        out_specs=whole,
        scratch_shapes=[pltpu.VMEM((NZ, BLK, 128), jnp.float32), pltpu.VMEM((NX * N_ROW, 8, BLK), jnp.float32),
                        pltpu.VMEM((NX * N_ROW, 8, BLK), jnp.float32)],
        compiler_params=pltpu.CompilerParams(vmem_limit_bytes=VMEM_LIMIT),
    )(lists, quarter, x3, y3, c_all)
    g_own = pl.pallas_call(
        col_exchange_kernel,
        out_shape=shape(1, BLK),
        in_specs=[whole, whole, whole],
        out_specs=whole,
        scratch_shapes=[pltpu.VMEM((NX * N_ROW, 1, BLK), jnp.float32), dma((NX * N_ROW,)), dma((NX * N_ROW,))],
        compiler_params=pltpu.CompilerParams(collective_id=2, has_side_effects=True),
    )(sums, targets, log_b[None])
    return f_own.reshape(BLK), g_own.reshape(BLK)


def local(sources, targets, g_pot, log_a, log_b, src_block, tgt_block, pair_count):
    whole = pl.BlockSpec(memory_space=pltpu.VMEM)
    anywhere = pl.BlockSpec(memory_space=pl.ANY)
    dma = pltpu.SemaphoreType.DMA
    vmem = pltpu.VMEM
    f32 = jnp.float32
    both, bad = pl.pallas_call(
        merged_kernel,
        out_shape=(shape(2, BLK), shape(1, 1)),
        in_specs=[anywhere] * 8,
        out_specs=(whole, pl.BlockSpec(memory_space=pltpu.SMEM)),
        scratch_shapes=[
            vmem((NX, N_ROW, ROWS, D), f32), vmem((NZ, ROWS, D), f32),
            vmem((NX, N_ROW, BLK, 3 * D), jnp.bfloat16), vmem((NZ, BLK, 3 * D), jnp.bfloat16),
            vmem((NX, N_ROW, 8, BLK), f32), vmem((NZ, BLK, 128), f32), vmem((NZ, BLK, 128), f32),
            vmem((NX, 2, NZ, BLK, BLK), f32), vmem((NX, 2, NZ, 8, BLK), f32), vmem((NX, 2, NZ, 8, BLK), f32),
            vmem((NX, NZ, 128), jnp.int32), pltpu.SMEM((NX, NZ, 128), jnp.int32), vmem((N_COL, 128), jnp.int32),
            pltpu.SMEM((64,), jnp.int32), pltpu.SMEM((64,), jnp.int32), pltpu.SMEM((1,), jnp.int32), vmem((1, BLK), f32),
            vmem((NZ, 1, BLK + 128), f32), vmem((NZ, BLK), f32), vmem((NZ, NZ - 1, 1, BLK + 128), f32),
            vmem((NX, N_ROW, 1, BLK + 128), f32), vmem((NX, N_ROW, 1, BLK + 128), f32),
            dma((8,)), dma((16, 2, 4)), dma((16, 2)), dma((16, 2)), dma((16, 2)),
            dma((9, 2, 2)), dma((9, 2)), dma((3,)), dma((3,)),
            dma((NZ, NZ - 1)), dma((NZ, NZ - 1)), dma((NX, N_ROW)), dma((NX, N_ROW))],
        compiler_params=pltpu.CompilerParams(collective_id=0, has_side_effects=True, vmem_limit_bytes=VMEM_LIMIT),
    )(src_block, tgt_block, pair_count, sources, targets, g_pot[None], log_a[None], log_b[None])
    args = (sources, targets, g_pot, log_a, log_b, src_block, tgt_block, pair_count)
    both = lax.cond(bad[0, 0] > 0.5, lambda: jnp.stack(general(*args)), lambda: both)
    return both[0], both[1]


def solution(mesh):
    placed = (
        P(("row", "col"), None),
        P(("col", "row"), None),
        P(("col", "row")),
        P(("row", "col")),
        P(("col", "row")),
        P(("row", "col")),
        P(("row", "col")),
        P(("row", "col")),
    )
    return jax.shard_map(
        local,
        mesh=mesh,
        in_specs=placed,
        out_specs=(P(("row", "col")), P(("col", "row"))),
        check_vma=False,
    )
```
